32 devices in a mesh: fsdp: 32 (over z, y, x, core).
Axes of the slice: x: 2, y: 2, z: 4, core: 2. Of those that a mesh axis runs over, the one named last changes fastest.
Arguments:
- hidden_in: bfloat16 [16384, 768], P('fsdp'), may hold values from -6 to 6
- segment_ids: int32 [32, 512], P('fsdp'), may hold values from 0 to 7, never falling along the last dimension, each value on 1 to 128 neighbouring positions
- cotangent: bfloat16 [16384, 768], P('fsdp'), may hold values from -6 to 6
- w_in: bfloat16 [768, 3352], P('fsdp'), may hold values from -0.21875 to 0.21875
- w_out: bfloat16 [1536, 768], P('fsdp'), may hold values from -0.15625 to 0.15625
- conv_taps: bfloat16 [5, 1792], P(None, 'fsdp'), may hold values from -3 to 3
- gains: bfloat16 [2304], P('fsdp'), may hold values from 0.5 to 1.5
- a_log: float32 [24], replicated, may hold values from 0 to 2.77
- d_skip: float32 [24], replicated, may hold values from 0.5 to 1.5
- dt_bias: float32 [24], replicated, may hold values from -6.9 to -2.3
Outputs:
- output: bfloat16 [16384, 768], P('fsdp')
- input_grad: float32 [16384, 768], P('fsdp')
- grad_w_in: float32 [768, 3352], P('fsdp')
- grad_w_out: float32 [1536, 768], P('fsdp')
- grad_conv_taps: float32 [5, 1792], P(None, 'fsdp')
- grad_gains: float32 [2304], P('fsdp')
- grad_a_log: float32 [24], replicated
- grad_d_skip: float32 [24], replicated
- grad_dt_bias: float32 [24], replicated
The draws below stay inside these ranges and needn't reach their ends.
Inputs may be any that keep to these rules, and one draw needn't show every extreme that they name: `segment_ids`: within each sequence the numbers never fall; each segment has 1 to 128 positions, and one has exactly 128.
All inputs are finite; a program needn't handle non-finite values.
Results may differ from the reference program's by a relative error of at most 0.0068.
Values may be sent and summed in bfloat16 or wider, within the bound.
No kernel may reach another device: no remote copies, remote signals or barrier semaphores. Data moves between devices by JAX's collectives and lax.ppermute only.
A program may use at most 192 MiB of HBM per device.

```python
import math
import jax
import jax.numpy as jnp
import numpy as np
from jax import lax

D = 768
HEADS = 24
CONV_K = 4
SPAN = 256
SEQLEN = 512
INNER = 1536
CONVCH = 1792
PROJ = 3352
SEQS = 32
TOKENS = 16384


def raised(array, key, source, target, shards_of, factor):
    owner, partner = [(jnp.arange(array.shape[axis_at]) // (array.shape[axis_at] // shards_of)).reshape([-1 if axis == axis_at else 1 for axis in range(array.ndim)]) for axis_at in (source, target)]
    chosen = jax.random.permutation(key, shards_of)[partner]
    strong = (owner == chosen) | (owner == (partner + shards_of // 2) % shards_of)
    return jnp.where(strong, factor * array, array)


def steps_of(own_key, extent, split, low, high):
    level = 1.0
    for dim, parts in split:
        steps = jax.random.uniform(jax.random.fold_in(jax.random.fold_in(own_key, 6), dim), (parts,), jnp.float32, low / len(split), high / len(split))
        level = level * jnp.repeat(jnp.exp(steps), extent[dim] // parts).reshape((-1,) + (1,) * (len(extent) - 1 - dim))
    return level


def profile(count, total, reach, slope):
    loads = [(1 << 20) // math.isqrt(rank ** slope) + 1 for rank in range(2, count + 1)]
    rest, given = total - reach - (count - 1), [1] * (count - 1)
    while rest > 0:
        movable = [i for i in range(count - 1) if given[i] < reach]
        whole, left = sum([loads[i] for i in movable]), rest
        for i in movable:
            addition = min(reach - given[i], max(1, left * loads[i] // whole), rest)
            given[i] = given[i] + addition
            rest = rest - addition
    return np.array([reach] + given)


def uneven(key, amount, total, reach, slope):
    if amount == 2:
        one = jax.random.randint(key, (), max(1, total - reach), min(reach, total - 1) + 1)
        return jnp.stack([one, total - one])
    tallies = jnp.asarray(profile(amount, total, reach, slope), jnp.int32)
    pairs = (amount - 1) // 2
    donor, receiver = tallies[1:1 + 2 * pairs:2], tallies[2:2 + 2 * pairs:2]
    margin = jnp.minimum(donor - 1, reach - receiver)
    passed = jax.random.randint(jax.random.fold_in(key, 1), (pairs,), 0, 1 << 20) % (margin + 1)
    tallies = tallies.at[1:1 + 2 * pairs:2].set(donor - passed).at[2:2 + 2 * pairs:2].set(receiver + passed)
    return tallies[jax.random.permutation(jax.random.fold_in(key, 2), amount)]


def gaussian(rng, extent, spread, limit, cuts=(), held_as=jnp.bfloat16):
    result = jax.random.normal(rng, extent, jnp.float32) * spread
    if len(cuts) > 0:
        result = steps_of(rng, extent, cuts, -0.22, 0.18) * result
    return jnp.clip(result, min=-limit, max=limit).astype(held_as)


def gaussian_with(stream_key, extent, spread, bound, split, heavy, held_as=jnp.bfloat16):
    array = spread * jax.random.normal(stream_key, extent, jnp.float32)
    if split:
        array = array * steps_of(stream_key, extent, split, -0.22, 0.18)
    return jnp.clip(raised(array, jax.random.fold_in(stream_key, 3), *heavy), -bound, bound).astype(held_as)


def setup_inputs(seed: int = 0) -> dict:
    keys = jax.random.split(jax.random.key(seed), 11)
    return {
        "hidden_in": gaussian_with(keys[0], (TOKENS, D), 1.0, 6.0, ((0, 32),), (0, 1, 32, 2.75)),
        "segment_ids": jax.vmap(lambda own: jnp.searchsorted(jnp.cumsum(uneven(own, 8, SEQLEN, SEQLEN // 4, 1)), jnp.arange(SEQLEN), side="right"))(jax.random.split(keys[1], SEQS)).reshape((SEQS, SEQLEN)).astype(jnp.int32),
        "cotangent": gaussian(keys[2], (TOKENS, D), 1.0, 6.0, ((0, 32),)),
        "w_in": gaussian(keys[3], (D, PROJ), D ** -0.5, 0.21875, ((0, 32),)),
        "w_out": gaussian(keys[4], (INNER, D), INNER ** -0.5, 0.15625, ((0, 32),)),
        "conv_taps": gaussian(keys[5], (CONV_K + 1, CONVCH), CONV_K ** -0.5, 3.0, ((1, 32),)),
        "gains": jnp.clip(1.0 + 0.1 * jax.random.normal(keys[6], (D + INNER,), jnp.float32), 0.5, 1.5).astype(jnp.bfloat16),
        "a_log": jnp.clip(jax.random.uniform(keys[7], (HEADS,), jnp.float32, 0.0, 2.77), 0.0, 2.77),
        "d_skip": jnp.clip(jax.random.uniform(keys[8], (HEADS,), jnp.float32, 0.5, 1.5), 0.5, 1.5),
        "dt_bias": jnp.clip(jax.random.uniform(keys[9], (HEADS,), jnp.float32, -6.9, -2.3), -6.9, -2.3),
    }


def pre_norm(tokens, gain):
    return tokens * lax.rsqrt(lax.optimization_barrier(jnp.mean(tokens * tokens, axis=-1, keepdims=True)) + 1e-05) * gain

def conv_mix(conv_in, conv_taps, segments):
    kernel = conv_taps.shape[0] - 1
    length = conv_in.shape[1]
    summed = conv_taps[kernel] + conv_taps[kernel - 1] * conv_in
    for offset in range(1, kernel):
        shifted = jnp.pad(conv_in, ((0, 0), (offset, 0), (0, 0)))[:, :length]
        seg_shift = jnp.pad(segments, ((0, 0), (offset, 0)), constant_values=-1)[:, :length]
        same_seg = (seg_shift == segments).astype(conv_in.dtype)[..., None]
        summed = summed + conv_taps[kernel - 1 - offset] * shifted * same_seg
    return jax.nn.silu(summed)

def state_scan(values, b_rows, c_rows, step_size, rates, segments):
    highest = lax.Precision.HIGHEST
    seqs, length, heads, width = values.shape
    states = b_rows.shape[-1]
    blocks = length // SPAN
    val_blk = values.reshape(seqs, blocks, SPAN, heads, width)
    b_blk = b_rows.reshape(seqs, blocks, SPAN, states)
    c_blk = c_rows.reshape(seqs, blocks, SPAN, states)
    step_blk = step_size.reshape(seqs, blocks, SPAN, heads)
    seg_blk = segments.reshape(seqs, blocks, SPAN)
    cumul = jnp.cumsum(rates.reshape(seqs, blocks, SPAN, heads), axis=2)
    cum_heads = jnp.moveaxis(cumul, 3, 2)
    step_heads = jnp.moveaxis(step_blk, 3, 2)
    positions = jnp.arange(SPAN)
    causal = positions[:, None] >= positions[None, :]
    same_doc = ((seg_blk[:, :, :, None] == seg_blk[:, :, None, :]) & causal)[:, :, None]
    differ = cum_heads[..., :, None] - cum_heads[..., None, :]
    decay = jnp.exp(jnp.where(same_doc, differ, 0.0)) * same_doc.astype(cumul.dtype)
    scores = jnp.einsum('skti,skui->sktu', c_blk, b_blk, precision=highest)
    weights = decay * scores[:, :, None] * step_heads[:, :, :, None, :]
    inside = jnp.einsum('skhtu,skuhp->skthp', weights, val_blk, precision=highest)
    last_seg = seg_blk[:, :, -1]
    to_end = jnp.exp(cumul[:, :, -1:, :] - cumul) * (seg_blk == last_seg[:, :, None]).astype(cumul.dtype)[..., None] * step_blk
    local_state = jnp.einsum('skuh,skun,skuhp->skhpn', to_end, b_blk, val_blk, precision=highest)
    whole_decay = jnp.exp(cumul[:, :, -1, :])
    carried = jnp.zeros((seqs, heads, width, states), values.dtype)
    previous = jnp.full((seqs,), -1, jnp.int32)
    results = []
    for block in range(blocks):
        linked = (seg_blk[:, block] == previous[:, None]).astype(cumul.dtype)
        factor = jnp.exp(cumul[:, block]) * linked[..., None]
        reached = jnp.einsum('sti,shpi->sthp', c_blk[:, block], carried, precision=highest)
        results.append(inside[:, block] + factor[..., None] * reached)
        keep_all = (last_seg[:, block] == previous).astype(cumul.dtype)
        carried = carried * (whole_decay[:, block] * keep_all[:, None])[:, :, None, None] + local_state[:, block]
        previous = last_seg[:, block]
    return jnp.stack(results, axis=1).reshape(seqs, length, heads, width)

def mixer(projected, conv_taps, inner_gain, a_log, d_skip, dt_bias, segments):
    inner = inner_gain.shape[0]
    channels = conv_taps.shape[1]
    states = (channels - inner) // 2
    heads = a_log.shape[0]
    seqs, length = segments.shape
    gate_in = projected[..., :inner]
    conv_out = conv_mix(projected[..., inner:inner + channels], conv_taps, segments)
    values = conv_out[..., :inner].reshape(seqs, length, heads, inner // heads)
    b_rows = conv_out[..., inner:inner + states]
    c_rows = conv_out[..., inner + states:]
    step_size = jax.nn.softplus(projected[..., inner + channels:] + dt_bias)
    rates = -step_size * jnp.exp(a_log)
    scanned = state_scan(values, b_rows, c_rows, step_size, rates, segments) + d_skip[:, None] * values
    gated = scanned.reshape(seqs, length, inner) * jax.nn.silu(gate_in)
    scale = lax.rsqrt(lax.optimization_barrier(jnp.mean(gated * gated, axis=-1, keepdims=True)) + 1e-05)
    return gated * scale * inner_gain

def block_pass(hidden, segments, upstream, w_in, w_out, conv_taps, gains, a_log, d_skip, dt_bias):
    seqs, length, width = hidden.shape
    rows_all = seqs * length
    tokens = hidden.astype(jnp.float32)
    pre_gain = gains[:width].astype(jnp.float32)
    inner_gain = gains[width:].astype(jnp.float32)
    normed, pre_pull = jax.vjp(pre_norm, tokens, pre_gain)
    normed_low = normed.astype(jnp.bfloat16).reshape(rows_all, width)
    projected = jnp.dot(normed_low, w_in, preferred_element_type=jnp.float32).reshape(seqs, length, -1)

    def mixer_of(proj_in, taps_in, gain_in, alog_in, skip_in, bias_in):
        return mixer(proj_in, taps_in, gain_in, alog_in, skip_in, bias_in, segments)
    gated, mix_pull = jax.vjp(mixer_of, projected, conv_taps.astype(jnp.float32), inner_gain, a_log, d_skip, dt_bias)
    mixed_low = gated.astype(jnp.bfloat16).reshape(rows_all, -1)
    branch = jnp.dot(mixed_low, w_out, preferred_element_type=jnp.float32)
    output = (tokens.reshape(rows_all, width) + branch).astype(jnp.bfloat16)
    upstream_flat = upstream.reshape(rows_all, width)
    grad_out = jnp.dot(mixed_low.T, upstream_flat, preferred_element_type=jnp.float32)
    d_mixed = jnp.dot(upstream_flat, w_out.T, preferred_element_type=jnp.float32)
    d_proj, d_taps, d_inner_gain, d_alog, d_dskip, d_dtbias = mix_pull(d_mixed.reshape(seqs, length, -1))
    d_proj_low = d_proj.astype(jnp.bfloat16).reshape(rows_all, -1)
    grad_in = jnp.dot(normed_low.T, d_proj_low, preferred_element_type=jnp.float32)
    d_normed = jnp.dot(d_proj_low, w_in.T, preferred_element_type=jnp.float32)
    d_tokens, d_pre_gain = pre_pull(d_normed.reshape(seqs, length, width))
    input_grad = upstream.astype(jnp.float32) + d_tokens
    grad_gains = jnp.concatenate([d_pre_gain, d_inner_gain])
    grads = (grad_in, grad_out, d_taps, grad_gains, d_alog, d_dskip, d_dtbias)
    return (output.reshape(seqs, length, width), input_grad, grads)

def reference(hidden_in, segment_ids, cotangent, w_in, w_out, conv_taps, gains, a_log, d_skip, dt_bias):
    seqs_all, length = segment_ids.shape
    width = hidden_in.shape[1]
    group = math.gcd(8, seqs_all)
    count = seqs_all // group
    hidden_blocks = hidden_in.reshape(count, group, length, width)
    seg_blocks = segment_ids.reshape(count, group, length)
    up_blocks = cotangent.reshape(count, group, length, width)
    zeros = (jnp.zeros(w_in.shape, jnp.float32), jnp.zeros(w_out.shape, jnp.float32), jnp.zeros(conv_taps.shape, jnp.float32), jnp.zeros(gains.shape, jnp.float32), jnp.zeros(a_log.shape, jnp.float32), jnp.zeros(d_skip.shape, jnp.float32), jnp.zeros(dt_bias.shape, jnp.float32))

    def visit(carry, pieces):
        hidden, segments, upstream = pieces
        output, input_grad, grads = block_pass(hidden, segments, upstream, w_in, w_out, conv_taps, gains, a_log, d_skip, dt_bias)
        return (jax.tree.map(jnp.add, carry, grads), (output, input_grad))
    totals, (outputs, in_grads) = lax.scan(visit, zeros, (hidden_blocks, seg_blocks, up_blocks))
    output = outputs.reshape(seqs_all * length, width)
    input_grad = in_grads.reshape(seqs_all * length, width)
    return (output, input_grad, totals[0], totals[1], totals[2], totals[3], totals[4], totals[5], totals[6])
```

```python
import jax
import jax.numpy as jnp
import numpy as np
from jax import lax
from jax.experimental import pallas as pl
from jax.experimental.pallas import tpu as pltpu
from jax.sharding import PartitionSpec as P


BLK = 128
LOG2E = 1.4426950408889634
F32 = jnp.float32
BF16 = jnp.bfloat16
HIGH = lax.Precision.HIGHEST


def mm(a, b):
    return lax.dot_general(a, b, (((1,), (0,)), ((), ())), preferred_element_type=F32)


def mm_nt(a, b):
    return lax.dot_general(a, b, (((1,), (1,)), ((), ())), preferred_element_type=F32)


def mm_tn(a, b):
    return lax.dot_general(a, b, (((0,), (0,)), ((), ())), preferred_element_type=F32)


def split2(x):
    hi = x.astype(BF16)
    return hi, (x - hi.astype(F32)).astype(BF16)


def iota(shape, dim):
    return lax.broadcasted_iota(jnp.int32, shape, dim)


def perm_matrix(dvec, width):
    return (iota((width, width), 0) == dvec).astype(F32).astype(BF16)


def norm_kernel(hid_ref, gain_ref, dvec_ref, xn_ref):
    tokens = hid_ref[...].astype(F32)
    scale = lax.rsqrt(jnp.mean(tokens * tokens, axis=-1, keepdims=True) + 1e-05)
    normed = (tokens * scale * gain_ref[...]).astype(BF16)
    perm = perm_matrix(dvec_ref[...], tokens.shape[1])
    xn_ref[...] = mm(normed, perm).astype(BF16)


def head_setup(dt_raw, heads_ref, step_ref, cc_ref, al_ref, ew_ref, wq_ref, cct_ref):
    length = dt_raw.shape[0]
    biased = dt_raw + heads_ref[2:3, :]
    step = jnp.maximum(biased, 0.0) + jnp.log1p(jnp.exp(-jnp.abs(biased)))
    step_ref[...] = step
    rate = step * (jnp.exp(heads_ref[0:1, :]) * (-LOG2E))
    lower = (iota((BLK, BLK), 0) >= iota((BLK, BLK), 1)).astype(F32)
    for i in range(length // BLK):
        rows = slice(i * BLK, (i + 1) * BLK)
        cc = jnp.dot(lower, rate[rows], precision=HIGH, preferred_element_type=F32)
        cc_ref[rows, :] = cc
        al_ref[rows, :] = jnp.exp2(cc)
        ew = jnp.exp2(jnp.minimum(cc[BLK - 1 : BLK, :] - cc, 0.0))
        ew_ref[rows, :] = ew
        wq_ref[rows, :] = ew * step[rows]
        cct_ref[:, rows] = cc.T[: cct_ref.shape[0]]


def mask_setup(segc_ref, mask_ref):
    seg = segc_ref[...]
    length = seg.shape[0]
    pos = iota((length, BLK), 0)
    segb = jnp.broadcast_to(seg, (length, BLK))
    for j in range(1, mask_ref.shape[0] + 1):
        prev = pltpu.roll(segb, j, axis=0)
        mask_ref[j - 1] = ((prev == segb) & (pos >= j)).astype(F32)


def conv_parts(x, taps_ref, lanes, mask_ref):
    kernel = mask_ref.shape[0] + 1
    shifts = [x] + [pltpu.roll(x, j, axis=0) * mask_ref[j - 1] for j in range(1, kernel)]
    pre = taps_ref[kernel : kernel + 1, lanes] + taps_ref[kernel - 1 : kernel, lanes] * x
    for j in range(1, kernel):
        pre = pre + taps_ref[kernel - 1 - j : kernel - j, lanes] * shifts[j]
    return shifts, pre


def sigmoid(x):
    return 1.0 / (1.0 + jnp.exp(-x))


def score_setup(bmat, cmat, segc_ref, segr_ref, sd_ref, so_ref, sdt_ref, sot_ref):
    length = bmat.shape[0]
    bb, cb = bmat.astype(BF16), cmat.astype(BF16)
    causal = iota((BLK, BLK), 0) >= iota((BLK, BLK), 1)
    for i in range(length // BLK):
        rows = slice(i * BLK, (i + 1) * BLK)
        before = slice((i - 1) * BLK, i * BLK)
        same = (segc_ref[rows, :] == segr_ref[:, rows]) & causal
        diag = jnp.where(same, mm_nt(cb[rows], bb[rows]), 0.0)
        if sd_ref is not None:
            sd_ref[i] = diag
        if sdt_ref is not None:
            sdt_ref[i] = diag.T
        if i > 0:
            linked = segc_ref[rows, :] == segr_ref[:, before]
            off = jnp.where(linked, mm_nt(cb[rows], bb[before]), 0.0)
            so_ref[i] = off.astype(BF16)
            if sot_ref is not None:
                sot_ref[i] = off.T.astype(BF16)


def pair_lanes(ref, shift, low):
    both = pltpu.roll(ref[...], shift, axis=1)
    return jnp.where(low, both[:, 0:1], both[:, 1:2])


def block_diag(x, low):
    zero = jnp.zeros_like(x)
    return jnp.concatenate([jnp.where(low, x, zero), jnp.where(low, zero, x)], axis=0)


def scan_fwd_kernel(
    xn_ref, wa_ref, wb_ref, taps_ref, segc_ref, segr_ref, heads_ref, skip_ref,
    ci_ref, dt_ref, sc_ref, yd_ref,
    step_ref, cc_ref, al_ref, ew_ref, wq_ref, cct_ref, mask_ref, sd_ref, so_ref,
):
    t = pl.program_id(0)
    length = xn_ref.shape[0]
    channels = ci_ref.shape[1]
    states = BLK
    inner = channels - 2 * states
    nheads = wa_ref.shape[1] - channels

    @pl.when(t == 0)
    def _():
        half = wa_ref.shape[0]
        xa, xb = xn_ref[:, :half], xn_ref[:, half:]
        ci_ref[...] = mm(xa, wa_ref[:, :channels]) + mm(xb, wb_ref[:, :channels])
        dt_ref[...] = jnp.zeros_like(dt_ref)
        dt_ref[:, :nheads] = mm(xa, wa_ref[:, channels:]) + mm(xb, wb_ref[:, channels:])
        head_setup(dt_ref[...], heads_ref, step_ref, cc_ref, al_ref, ew_ref, wq_ref, cct_ref)
        mask_setup(segc_ref, mask_ref)
        lanes_b = slice(inner, inner + states)
        lanes_c = slice(inner + states, channels)
        _, pre_b = conv_parts(ci_ref[:, lanes_b], taps_ref, lanes_b, mask_ref)
        _, pre_c = conv_parts(ci_ref[:, lanes_c], taps_ref, lanes_c, mask_ref)
        score_setup(
            pre_b * sigmoid(pre_b), pre_c * sigmoid(pre_c),
            segc_ref, segr_ref, sd_ref, so_ref, None, None,
        )

    lanes = pl.ds(pl.multiple_of(t * BLK, BLK), BLK)
    _, pre = conv_parts(ci_ref[:, lanes], taps_ref, lanes, mask_ref)
    v = pre * sigmoid(pre)
    low = iota((1, BLK), 1) < BLK // 2
    shift = lax.rem(BLK - 2 * t, BLK)
    vt = (v * pair_lanes(step_ref, shift, low)).astype(BF16)
    vp = (v * pair_lanes(wq_ref, shift, low)).astype(BF16)
    al2 = pair_lanes(al_ref, shift, low)
    c2 = pltpu.roll(cc_ref[...], shift, axis=1)
    r2 = pltpu.roll(cct_ref[...], lax.rem(cct_ref.shape[0] - 2 * t, cct_ref.shape[0]), axis=0)
    for i in range(length // BLK):
        rows = slice(i * BLK, (i + 1) * BLK)
        before = slice((i - 1) * BLK, i * BLK)
        ms = []
        for k in range(2):
            row = r2[k : k + 1, rows]
            d = jnp.exp2(jnp.minimum(c2[rows, k : k + 1] - row, 0.0))
            ms.append((sd_ref[i] * d).astype(BF16))
        yd = mm(jnp.concatenate(ms, axis=1), block_diag(vt[rows], low))
        yd_ref[rows, :] = yd
        y = yd + skip_ref[...] * v[rows]
        if i > 0:
            y = y + al2[rows] * mm(so_ref[i], vp[before])
        sc_ref[rows, :] = y


def gate_kernel(xn_ref, wa_ref, wb_ref, sc_ref, gain_ref, cot_ref, gate_ref, mixed_ref, gwo_ref):
    half = wa_ref.shape[0]
    gate_ref[...] = mm(xn_ref[:, :half], wa_ref[...]) + mm(xn_ref[:, half:], wb_ref[...])
    length = xn_ref.shape[0]
    sub = 32

    def body(k, carry):
        rows = pl.ds(pl.multiple_of(k * sub, sub), sub)
        gate = gate_ref[rows, :]
        gated = sc_ref[rows, :] * (gate * sigmoid(gate))
        scale = lax.rsqrt(jnp.mean(gated * gated, axis=-1, keepdims=True) + 1e-05)
        mixed_ref[rows, :] = (gated * scale * gain_ref[...]).astype(BF16)
        return carry

    lax.fori_loop(0, length // sub, body, 0)
    gwo_ref[...] = mm_tn(mixed_ref[...], cot_ref[...]).astype(BF16)


def out_kernel(
    xn_ref, wa_ref, wb_ref, wo_ref, sc_ref, gate_ref, mixed_ref, gain_ref, cot_ref, hid_ref,
    out_ref, g_ref, gg_ref, dn_ref, ginner_ref,
    dm_ref, dgate_ref,
):
    wo = wo_ref[...]
    branch = mm(mixed_ref[...], wo)
    out_ref[...] = (hid_ref[...].astype(F32) + branch).astype(BF16)
    dm_ref[...] = mm_nt(cot_ref[...], wo)
    length = xn_ref.shape[0]
    sub = 32
    ginner_ref[...] = jnp.zeros_like(ginner_ref)

    def body(k, carry):
        rows = pl.ds(pl.multiple_of(k * sub, sub), sub)
        gate = gate_ref[rows, :]
        sig = sigmoid(gate)
        silu = gate * sig
        scanned = sc_ref[rows, :]
        gated = scanned * silu
        scale = lax.rsqrt(jnp.mean(gated * gated, axis=-1, keepdims=True) + 1e-05)
        dm = dm_ref[rows, :]
        unit = gated * scale
        ginner_ref[...] += jnp.sum((dm * unit).reshape(sub // 8, 8, -1), axis=0)
        dunit = dm * gain_ref[...]
        inner = jnp.mean(unit * dunit, axis=-1, keepdims=True)
        du = scale * (dunit - unit * inner)
        g_ref[rows, :] = du * silu
        dgate_ref[rows, :] = (du * scanned * (sig * (1.0 + gate * (1.0 - sig)))).astype(BF16)
        return carry

    lax.fori_loop(0, length // sub, body, 0)
    dgate = dgate_ref[...]
    half = wa_ref.shape[0]
    gg_ref[...] = mm_tn(xn_ref[...], dgate).astype(BF16)
    dn_ref[:, :half] = mm_nt(dgate, wa_ref[...])
    dn_ref[:, half:] = mm_nt(dgate, wb_ref[...])


def conv_back(dpre, x, taps_ref, lanes, mask_ref, dtaps_ref, dp_ref):
    kernel = mask_ref.shape[0] + 1
    length = dpre.shape[0]

    def total(z):
        return jnp.sum(z, axis=0, keepdims=True)

    dtaps_ref[kernel : kernel + 1, lanes] = total(dpre)
    dtaps_ref[kernel - 1 : kernel, lanes] = total(dpre * x)
    dx = taps_ref[kernel - 1 : kernel, lanes] * dpre
    for j in range(1, kernel):
        masked = dpre * mask_ref[j - 1]
        tap = slice(kernel - 1 - j, kernel - j)
        dtaps_ref[tap, lanes] = total(masked * pltpu.roll(x, j, axis=0))
        dx = dx + taps_ref[tap, lanes] * pltpu.roll(masked, length - j, axis=0)
    dp_ref[:, lanes] = dx.astype(BF16)


def silu_and_slope(pre):
    sig = sigmoid(pre)
    return pre * sig, sig * (1.0 + pre * (1.0 - sig))


def scan_bwd_kernel(
    g_ref, yd_ref, ci_ref, dt_ref, taps_ref, segc_ref, segr_ref, heads_ref, skip_ref,
    dp_ref, dtaps_ref, dskip_ref, dheads_ref,
    step_ref, cc_ref, al_ref, ew_ref, wq_ref, cct_ref, mask_ref,
    sdt_ref, so_ref, sot_ref, dsdt_ref, dso_ref, acc_ref, dpre_ref,
):
    t = pl.program_id(0)
    length = ci_ref.shape[0]
    blocks = length // BLK
    channels = ci_ref.shape[1]
    states = BLK
    inner = channels - 2 * states
    nheads = dp_ref.shape[1] - channels
    lanes_b = slice(inner, inner + states)
    lanes_c = slice(inner + states, channels)

    @pl.when(t == 0)
    def _():
        head_setup(dt_ref[...], heads_ref, step_ref, cc_ref, al_ref, ew_ref, wq_ref, cct_ref)
        mask_setup(segc_ref, mask_ref)
        _, pre_b = conv_parts(ci_ref[:, lanes_b], taps_ref, lanes_b, mask_ref)
        _, pre_c = conv_parts(ci_ref[:, lanes_c], taps_ref, lanes_c, mask_ref)
        score_setup(
            pre_b * sigmoid(pre_b), pre_c * sigmoid(pre_c),
            segc_ref, segr_ref, None, so_ref, sdt_ref, sot_ref,
        )
        dsdt_ref[...] = jnp.zeros_like(dsdt_ref)
        dso_ref[...] = jnp.zeros_like(dso_ref)
        acc_ref[...] = jnp.zeros_like(acc_ref)

    lanes = pl.ds(pl.multiple_of(t * BLK, BLK), BLK)
    x = ci_ref[:, lanes]
    _, pre = conv_parts(x, taps_ref, lanes, mask_ref)
    v, slope = silu_and_slope(pre)
    low = iota((1, BLK), 1) < BLK // 2
    shift = lax.rem(BLK - 2 * t, BLK)
    st2 = pair_lanes(step_ref, shift, low)
    wq2 = pair_lanes(wq_ref, shift, low)
    ew2 = pair_lanes(ew_ref, shift, low)
    al2 = pair_lanes(al_ref, shift, low)
    c2 = pltpu.roll(cc_ref[...], shift, axis=1)
    r2 = pltpu.roll(cct_ref[...], lax.rem(cct_ref.shape[0] - 2 * t, cct_ref.shape[0]), axis=0)
    vtb = (v * st2).astype(BF16)
    vpb = (v * wq2).astype(BF16)
    g = g_ref[...]
    gb = g.astype(BF16)
    gpb = (al2 * g).astype(BF16)
    dskip_ref[...] = jnp.sum(g * v, axis=0, keepdims=True)
    k_row = iota((4 * BLK, BLK), 0)
    target = jnp.where(k_row >= 2 * BLK, BLK // 2, 0) + 2 * t
    target = target + jnp.where((k_row & (BLK - 1)) >= BLK // 2, 1, 0)
    collect = (iota((4 * BLK, BLK), 1) == target).astype(F32).astype(BF16)
    for i in range(blocks):
        rows = slice(i * BLK, (i + 1) * BLK)
        before = slice((i - 1) * BLK, i * BLK)
        after = slice((i + 1) * BLK, (i + 2) * BLK)
        gdiag = block_diag(gb[rows], low)
        both = mm_nt(vtb[rows], gdiag)
        ms = []
        part = jnp.zeros((BLK, BLK), F32)
        for k in range(2):
            row = r2[k : k + 1, rows]
            d = jnp.exp2(jnp.minimum(row - c2[rows, k : k + 1], 0.0))
            ms.append((sdt_ref[i] * d).astype(BF16))
            part = part + both[:, k * BLK : (k + 1) * BLK] * d
        dsdt_ref[i] += part
        dvt = mm(jnp.concatenate(ms, axis=1), gdiag)
        x1 = gb[rows].astype(F32) * yd_ref[rows, :] - dvt * vtb[rows].astype(F32)
        dv = st2[rows] * dvt + skip_ref[...] * g[rows]
        dstep = dvt
        if i > 0:
            z = mm(so_ref[i], vpb[before])
            x1 = x1 + gpb[rows].astype(F32) * z
            dso_ref[i] += mm_nt(gpb[rows], vpb[before])
        if i + 1 < blocks:
            dvp = mm(sot_ref[i + 1], gpb[after])
            x1 = x1 - dvp * vpb[rows].astype(F32)
            dv = dv + wq2[rows] * dvp
            dstep = dstep + ew2[rows] * dvp
        h1, l1 = split2(x1)
        h2, l2 = split2(dstep * v[rows])
        acc_ref[rows, :] += mm(jnp.concatenate([h1, l1, h2, l2], axis=1), collect)
        dpre_ref[rows, :] = dv * slope[rows]
    conv_back(dpre_ref[...], x, taps_ref, lanes, mask_ref, dtaps_ref, dp_ref)

    @pl.when(t == pl.num_programs(0) - 1)
    def _():
        xb, xc = ci_ref[:, lanes_b], ci_ref[:, lanes_c]
        _, pre_b = conv_parts(xb, taps_ref, lanes_b, mask_ref)
        _, pre_c = conv_parts(xc, taps_ref, lanes_c, mask_ref)
        bmat, slope_b = silu_and_slope(pre_b)
        cmat, slope_c = silu_and_slope(pre_c)
        bb, cb = bmat.astype(BF16), cmat.astype(BF16)
        causal_t = iota((BLK, BLK), 1) >= iota((BLK, BLK), 0)
        upper = causal_t.astype(F32)
        dst, dso = [], [None]
        for i in range(blocks):
            rows = slice(i * BLK, (i + 1) * BLK)
            before = slice((i - 1) * BLK, i * BLK)
            same = (segc_ref[rows, :] == segr_ref[:, rows]) & causal_t
            dst.append(jnp.where(same, dsdt_ref[i], 0.0))
            if i > 0:
                linked = segc_ref[rows, :] == segr_ref[:, before]
                dso.append(jnp.where(linked, dso_ref[i], 0.0))
        for i in range(blocks):
            rows = slice(i * BLK, (i + 1) * BLK)
            before = slice((i - 1) * BLK, i * BLK)
            after = slice((i + 1) * BLK, (i + 2) * BLK)
            dc = mm(dst[i].T.astype(BF16), bb[rows])
            if i > 0:
                dc = dc + mm(dso[i].astype(BF16), bb[before])
            dpre_ref[rows, :] = dc * slope_c[rows]
        conv_back(dpre_ref[...], xc, taps_ref, lanes_c, mask_ref, dtaps_ref, dp_ref)
        for i in range(blocks):
            rows = slice(i * BLK, (i + 1) * BLK)
            after = slice((i + 1) * BLK, (i + 2) * BLK)
            db = mm(dst[i].astype(BF16), cb[rows])
            if i + 1 < blocks:
                db = db + mm(dso[i + 1].T.astype(BF16), cb[after])
            dpre_ref[rows, :] = db * slope_b[rows]
        conv_back(dpre_ref[...], xb, taps_ref, lanes_b, mask_ref, dtaps_ref, dp_ref)

        decay = jnp.exp(heads_ref[0:1, :])
        later = jnp.zeros((1, BLK), F32)
        dalog = jnp.zeros((1, BLK), F32)
        dbias = jnp.zeros((1, BLK), F32)
        for i in reversed(range(blocks)):
            rows = slice(i * BLK, (i + 1) * BLK)
            dcum = acc_ref[rows, :]
            drate = later + jnp.dot(upper, dcum, precision=HIGH, preferred_element_type=F32)
            later = drate[0:1, :]
            step = step_ref[rows, :]
            dalog = dalog - jnp.sum(drate * step, axis=0, keepdims=True) * decay
            dstep = pltpu.roll(dcum, BLK // 2, axis=1) - drate * decay
            ddt = dstep * sigmoid(dt_ref[rows, :] + heads_ref[2:3, :])
            dbias = dbias + jnp.sum(ddt, axis=0, keepdims=True)
            dp_ref[rows, channels:] = ddt[:, :nheads].astype(BF16)
        dheads_ref[...] = jnp.zeros_like(dheads_ref)
        dheads_ref[0:1, :] = dalog
        dheads_ref[1:2, :] = dbias


def grad_in_kernel(xn_ref, dp_ref, gc_ref):
    gc_ref[...] = mm_tn(xn_ref[...], dp_ref[...]).astype(BF16)


def input_kernel(dp_ref, wa_ref, wb_ref, dn_ref, dvec_ref, hid_ref, cot_ref, gain_ref, ig_ref, gp_ref):
    dp = dp_ref[...]
    dn = dn_ref[...] + jnp.concatenate([mm_nt(dp, wa_ref[...]), mm_nt(dp, wb_ref[...])], axis=1)
    perm = perm_matrix(dvec_ref[...], dn.shape[1])
    hi, lo = split2(dn)
    dn = mm_nt(hi, perm) + mm_nt(lo, perm)
    tokens = hid_ref[...].astype(F32)
    scale = lax.rsqrt(jnp.mean(tokens * tokens, axis=-1, keepdims=True) + 1e-05)
    unit = tokens * scale
    gp_ref[...] = jnp.sum(dn * unit, axis=0, keepdims=True)
    dunit = dn * gain_ref[...]
    inner = jnp.mean(unit * dunit, axis=-1, keepdims=True)
    ig_ref[...] = cot_ref[...].astype(F32) + scale * (dunit - unit * inner)


def sds(shape, dtype):
    return jax.ShapeDtypeStruct(shape, dtype)


PARAMS = dict(compiler_params=pltpu.CompilerParams(vmem_limit_bytes=60 * 1024 * 1024))


def head_scratch(length, inner):
    nheads = -(-2 * inner // (8 * BLK)) * 8
    return [pltpu.VMEM((length, BLK), F32)] * 5 + [pltpu.VMEM((nheads, length), F32)]


def full(shape):
    return pl.BlockSpec(shape, lambda t: (0,) * len(shape))


def tile(rows):
    return pl.BlockSpec((rows, BLK), lambda t: (0, t))


def scan_fwd(xn, wa, wb, taps, segc, segr, heads, skip_row):
    length = xn.shape[0]
    channels, inner = taps.shape[1], skip_row.shape[1]
    kernel = 4
    blocks = length // BLK
    ins = (xn, wa, wb, taps, segc, segr, heads, skip_row)
    return pl.pallas_call(
        scan_fwd_kernel,
        grid=(inner // BLK,),
        in_specs=[full(a.shape) for a in ins[:-1]] + [tile(1)],
        out_specs=[full((length, channels)), full((length, BLK)), tile(length), tile(length)],
        out_shape=[
            sds((length, channels), F32), sds((length, BLK), F32),
            sds((length, inner), F32), sds((length, inner), F32),
        ],
        scratch_shapes=head_scratch(length, inner) + [
            pltpu.VMEM((kernel - 1, length, BLK), F32),
            pltpu.VMEM((blocks, BLK, BLK), F32),
            pltpu.VMEM((blocks, BLK, BLK), BF16),
        ],
        name="scan_fwd",
        **PARAMS,
    )(*ins)


def scan_bwd(g, yd, ci, dt, taps, segc, segr, heads, skip_row, proj):
    length, channels = ci.shape
    inner = skip_row.shape[1]
    kernel = 4
    blocks = length // BLK
    ins = (g, yd, ci, dt, taps, segc, segr, heads, skip_row)
    return pl.pallas_call(
        scan_bwd_kernel,
        grid=(inner // BLK,),
        in_specs=[tile(length), tile(length)] + [full(a.shape) for a in ins[2:-1]] + [tile(1)],
        out_specs=[full((length, proj)), full(taps.shape), tile(1), full((8, BLK))],
        out_shape=[
            sds((length, proj), BF16), sds(taps.shape, F32), sds((1, inner), F32), sds((8, BLK), F32),
        ],
        scratch_shapes=head_scratch(length, inner) + [
            pltpu.VMEM((kernel - 1, length, BLK), F32),
            pltpu.VMEM((blocks, BLK, BLK), F32),
            pltpu.VMEM((blocks, BLK, BLK), BF16),
            pltpu.VMEM((blocks, BLK, BLK), BF16),
            pltpu.VMEM((blocks, BLK, BLK), F32),
            pltpu.VMEM((blocks, BLK, BLK), F32),
            pltpu.VMEM((length, BLK), F32),
            pltpu.VMEM((length, BLK), F32),
        ],
        name="scan_bwd",
        **PARAMS,
    )(*ins)


def call(kernel, name, outs, *ins, scratch=()):
    return pl.pallas_call(kernel, out_shape=outs, scratch_shapes=list(scratch), name=name, **PARAMS)(*ins)


def schedule(devices):
    bits = devices.bit_length() - 1
    masks = [1 << b for b in range(bits)]
    high = masks[3:]
    groups = []
    for start in range(0, len(high), 2):
        part = high[start : start + 2]
        groups.append([part[0]] if len(part) == 1 else [part[0], part[1], part[0] | part[1]])
    plane = masks[1:3]
    return groups, plane, masks


def orders(devices):
    groups, plane, _ = schedule(devices)
    tables = [np.zeros((1,), np.int32), np.zeros((1,), np.int32)]
    for group in groups:
        tables = [np.concatenate([o] + [o ^ m for m in group]) for o in tables]
    for a, b in zip(plane, reversed(plane)):
        tables = [np.concatenate([o, o ^ m]) for o, m in zip(tables, (a, b))]
    return np.stack([np.concatenate([tables[c], tables[1 - c] ^ 1]) for c in range(2)])


def send(x, devices, mask_even, mask_odd=None):
    mask_odd = mask_even if mask_odd is None else mask_odd
    pairs = [(i, i ^ (mask_odd if i & 1 else mask_even)) for i in range(devices)]
    return lax.ppermute(x, "fsdp", pairs)


def gather(x, devices):
    groups, plane, _ = schedule(devices)
    for group in groups:
        x = jnp.concatenate([x] + [send(x, devices, m) for m in group], axis=0)
    for a, b in zip(plane, reversed(plane)):
        x = jnp.concatenate([x, send(x, devices, a, b)], axis=0)
    return x, send(x, devices, 1)


def reduce_shares(x, devices):
    groups, plane, _ = schedule(devices)

    def fold(x, masks, last):
        count = len(masks) + 1
        size = x.shape[0] // count
        parts = [x[k * size : (k + 1) * size] for k in range(count)]
        total = parts[0].astype(F32)
        for part, m in zip(parts[1:], masks):
            total = total + send(part, devices, *m).astype(F32)
        return total if last else total.astype(BF16)

    x = fold(x, [(1, 1)], False)
    for a, b in zip(reversed(plane), plane):
        x = fold(x, [(a, b)], False)
    for k, group in enumerate(reversed(groups)):
        x = fold(x, [(m, m) for m in group], k == len(groups) - 1)
    return x


def total_of(x, devices):
    for m in schedule(devices)[2]:
        x = x + send(x, devices, m)
    return x


def shards(
    hidden, segment_ids, cot, w_in, w_out, conv_taps, gains, a_log, d_skip, dt_bias
):
    length = segment_ids.shape[1]
    width = hidden.shape[1]
    devices = lax.axis_size("fsdp")
    me = lax.axis_index("fsdp")
    nheads = a_log.shape[0]
    taps_n, tap_share = conv_taps.shape
    channels = tap_share * devices
    gain_share = gains.shape[0]
    inner = w_out.shape[0] * devices
    proj = w_in.shape[1]
    rows_in, rows_out = w_in.shape[0], w_out.shape[0]

    table = orders(devices)
    inverse = np.argsort(table, axis=1).astype(np.int32)
    odd = (me & 1) == 1
    order = jnp.where(odd, table[1], table[0]) ^ me
    place = jnp.where(odd, inverse[1], inverse[0])[me ^ jnp.arange(devices)]
    dvec = (order[:, None] * rows_in + jnp.arange(rows_in)[None, :]).reshape(1, width)

    small = jnp.zeros((8, BLK), F32)
    small = small.at[:taps_n, :tap_share].set(conv_taps.astype(F32))
    small = small.at[taps_n, :gain_share].set(gains.astype(F32))
    sa, sb = gather(small[None], devices)
    small_all = jnp.concatenate([sa, sb], axis=0)[place]
    taps = jnp.moveaxis(small_all[:, :, :tap_share], 0, 1).reshape(8, channels)
    gains_all = small_all[:, taps_n, :gain_share].reshape(1, width + inner)
    pre_gain, inner_gain = gains_all[:, :width], gains_all[:, width:]

    ca, cb = gather(w_in[:, inner:], devices)
    ga, gb = gather(w_in[:, :inner], devices)
    oa, ob = gather(w_out, devices)

    heads = jnp.zeros((8, BLK), F32)
    heads = heads.at[0, :nheads].set(a_log).at[1, :nheads].set(d_skip).at[2, :nheads].set(dt_bias)
    skip_row = jnp.repeat(d_skip, inner // nheads)[None]
    segc = segment_ids.reshape(length, 1)

    xn = call(norm_kernel, "norm", sds((length, width), BF16), hidden, pre_gain, dvec)
    ci, dt, sc, yd = scan_fwd(xn, ca, cb, taps, segc, segment_ids, heads, skip_row)
    gate, mixed, gwo = call(
        gate_kernel, "gate",
        (sds((length, inner), F32), sds((length, inner), BF16), sds((inner, width), BF16)),
        xn, ga, gb, sc, inner_gain, cot,
    )
    gwo_parts = gwo.reshape(devices, rows_out, width)[order].reshape(inner, width)
    out_share = reduce_shares(gwo_parts, devices)
    wo = jnp.concatenate([oa, ob], axis=0).reshape(devices, rows_out, width)[place].reshape(inner, width)
    output, g, gg, dn, ginner = call(
        out_kernel, "out",
        (
            sds((length, width), BF16), sds((length, inner), F32), sds((width, inner), BF16),
            sds((length, width), F32), sds((8, inner), F32),
        ),
        xn, ga, gb, wo, sc, gate, mixed, inner_gain, cot, hidden,
        scratch=(pltpu.VMEM((length, inner), F32), pltpu.VMEM((length, inner), BF16)),
    )
    gate_share = reduce_shares(gg, devices)
    dp, dtaps, dskip, dheads = scan_bwd(
        g, yd, ci, dt, taps, segc, segment_ids, heads, skip_row, proj - inner
    )
    gc = call(grad_in_kernel, "grad_in", sds((width, proj - inner), BF16), xn, dp)
    conv_share = reduce_shares(gc, devices)
    input_grad, gpre = call(
        input_kernel, "input",
        (sds((length, width), F32), sds((1, width), F32)),
        dp, ca, cb, dn, dvec, hidden, cot, pre_gain,
    )
    in_share = jnp.concatenate([gate_share, conv_share], axis=1)

    pieces = [dtaps[:taps_n].reshape(-1), gpre.reshape(-1), ginner.sum(axis=0), dheads[0, :nheads],
              dheads[1, :nheads], dskip.reshape(nheads, -1).sum(axis=1)]
    flat = jnp.concatenate(pieces)
    pad = -flat.shape[0] % 1024
    sums = total_of(jnp.pad(flat, (0, pad)).reshape(-1, BLK), devices).reshape(-1)
    dtaps_all = sums[: taps_n * channels].reshape(taps_n, channels)
    at = taps_n * channels
    taps_share = lax.dynamic_slice_in_dim(dtaps_all, me * tap_share, tap_share, axis=1)
    gains_share = lax.dynamic_slice_in_dim(sums[at : at + width + inner], me * gain_share, gain_share)
    at = at + width + inner
    return (
        output, input_grad, in_share, out_share, taps_share, gains_share,
        sums[at : at + nheads], sums[at + 2 * nheads : at + 3 * nheads], sums[at + nheads : at + 2 * nheads],
    )


def solution(mesh):
    axis = P("fsdp")
    rows = P("fsdp", None)
    cols = P(None, "fsdp")
    return jax.shard_map(
        shards,
        mesh=mesh,
        in_specs=(rows, rows, rows, rows, rows, cols, axis, P(), P(), P()),
        out_specs=(rows, rows, rows, rows, cols, axis, P(), P(), P()),
        check_vma=False,
    )
```

```python
import jax
import jax.numpy as jnp
import numpy as np
from jax import lax
from jax.experimental import pallas as pl
from jax.experimental.pallas import tpu as pltpu
from jax.sharding import PartitionSpec as P


BLK = 128
LOG2E = 1.4426950408889634
F32 = jnp.float32
BF16 = jnp.bfloat16
HIGH = lax.Precision.HIGHEST


def mm(a, b):
    return lax.dot_general(a, b, (((1,), (0,)), ((), ())), preferred_element_type=F32)


def mm_nt(a, b):
    return lax.dot_general(a, b, (((1,), (1,)), ((), ())), preferred_element_type=F32)


def mm_tn(a, b):
    return lax.dot_general(a, b, (((0,), (0,)), ((), ())), preferred_element_type=F32)


def split2(x):
    hi = x.astype(BF16)
    return hi, (x - hi.astype(F32)).astype(BF16)


def iota(shape, dim):
    return lax.broadcasted_iota(jnp.int32, shape, dim)


def perm_matrix(dvec, width):
    return (iota((width, width), 0) == dvec).astype(F32).astype(BF16)


def rows_of(refs, lanes=slice(None)):
    return jnp.concatenate([ref[:, lanes] for ref in refs], axis=0)


def normed_of(hid_ref, gain, dvec_ref, xn_ref):
    tokens = hid_ref[...].astype(F32)
    scale = lax.rsqrt(jnp.mean(tokens * tokens, axis=-1, keepdims=True) + 1e-05)
    normed = (tokens * scale * gain).astype(BF16)
    perm = perm_matrix(dvec_ref[...], tokens.shape[1])
    xn_ref[...] = mm(normed, perm).astype(BF16)


def norm_kernel(hid_ref, gains_ref, dvec_ref, xn_ref):
    normed_of(hid_ref, gains_ref[:, : hid_ref.shape[1]], dvec_ref, xn_ref)


def prep_kernel(at, taps_n, hid_ref, dvec_ref, owner_ref, where_ref, *refs):
    pieces, (xn_ref, taps_ref, gains_ref) = refs[:-3], refs[-3:]
    held = rows_of(pieces)
    devices = owner_ref.shape[0]
    rows_in = held.shape[0] // devices
    row = iota((8 * devices, held.shape[0]), 0)
    bits = devices.bit_length() - 1
    source = (row & (devices - 1)) * rows_in + lax.shift_right_logical(row, bits)
    pick = (iota(row.shape, 1) == source).astype(F32).astype(BF16)
    small = mm(pick, held).astype(BF16)

    def spread(part, line, width):
        lane, owner = where_ref[line : line + 1, :width], where_ref[line + 1 : line + 2, :width]
        chosen = (iota((BLK, width), 0) == lane + at).astype(F32).astype(BF16)
        wide = mm(part, chosen)
        return jnp.sum(jnp.where(owner_ref[...] == owner, wide, 0.0), axis=0, keepdims=True)

    channels, width = taps_ref.shape[1], gains_ref.shape[1]
    taps_ref[...] = jnp.zeros_like(taps_ref)
    for j in range(taps_n):
        taps_ref[j : j + 1, :] = spread(small[j * devices : (j + 1) * devices], 0, channels)
    gains_ref[...] = spread(small[taps_n * devices : (taps_n + 1) * devices], 2, width)
    normed_of(hid_ref, gains_ref[:, : hid_ref.shape[1]], dvec_ref, xn_ref)


def head_setup(dt_raw, heads_ref, step_ref, cc_ref, al_ref, ew_ref, wq_ref, cct_ref):
    length = dt_raw.shape[0]
    biased = dt_raw + heads_ref[2:3, :]
    step = jnp.maximum(biased, 0.0) + jnp.log1p(jnp.exp(-jnp.abs(biased)))
    step_ref[...] = step
    rate = step * (jnp.exp(heads_ref[0:1, :]) * (-LOG2E))
    lower = (iota((BLK, BLK), 0) >= iota((BLK, BLK), 1)).astype(F32)
    for i in range(length // BLK):
        rows = slice(i * BLK, (i + 1) * BLK)
        cc = jnp.dot(lower, rate[rows], precision=HIGH, preferred_element_type=F32)
        cc_ref[rows, :] = cc
        al_ref[rows, :] = jnp.exp2(cc)
        ew = jnp.exp2(jnp.minimum(cc[BLK - 1 : BLK, :] - cc, 0.0))
        ew_ref[rows, :] = ew
        wq_ref[rows, :] = ew * step[rows]
        cct_ref[:, rows] = cc.T[: cct_ref.shape[0]]


def mask_setup(segc_ref, mask_ref):
    seg = segc_ref[...]
    length = seg.shape[0]
    pos = iota((length, BLK), 0)
    segb = jnp.broadcast_to(seg, (length, BLK))
    for j in range(1, mask_ref.shape[0] + 1):
        prev = pltpu.roll(segb, j, axis=0)
        mask_ref[j - 1] = ((prev == segb) & (pos >= j)).astype(F32)


def conv_parts(x, taps_ref, lanes, mask_ref):
    kernel = mask_ref.shape[0] + 1
    shifts = [x] + [pltpu.roll(x, j, axis=0) * mask_ref[j - 1] for j in range(1, kernel)]
    pre = taps_ref[kernel : kernel + 1, lanes] + taps_ref[kernel - 1 : kernel, lanes] * x
    for j in range(1, kernel):
        pre = pre + taps_ref[kernel - 1 - j : kernel - j, lanes] * shifts[j]
    return shifts, pre


def sigmoid(x):
    return 0.5 * jnp.tanh(0.5 * x) + 0.5


def score_setup(bmat, cmat, segc_ref, segr_ref, sd_ref, so_ref, sdt_ref, sot_ref):
    length = bmat.shape[0]
    bb, cb = bmat.astype(BF16), cmat.astype(BF16)
    causal = iota((BLK, BLK), 0) >= iota((BLK, BLK), 1)
    for i in range(length // BLK):
        rows = slice(i * BLK, (i + 1) * BLK)
        before = slice((i - 1) * BLK, i * BLK)
        same = (segc_ref[rows, :] == segr_ref[:, rows]) & causal
        diag = jnp.where(same, mm_nt(cb[rows], bb[rows]), 0.0)
        if sd_ref is not None:
            sd_ref[i] = diag
        if sdt_ref is not None:
            sdt_ref[i] = diag.T
        if i > 0:
            linked = segc_ref[rows, :] == segr_ref[:, before]
            off = jnp.where(linked, mm_nt(cb[rows], bb[before]), 0.0)
            so_ref[i] = off.astype(BF16)
            if sot_ref is not None:
                sot_ref[i] = off.T.astype(BF16)


def pair_lanes(ref, shift, low):
    both = pltpu.roll(ref[...], shift, axis=1)
    return jnp.where(low, both[:, 0:1], both[:, 1:2])


def block_diag(x, low):
    zero = jnp.zeros_like(x)
    return jnp.concatenate([jnp.where(low, x, zero), jnp.where(low, zero, x)], axis=0)


def scan_fwd_kernel(pieces, *refs):
    w_refs = refs[:pieces]
    (
        xn_ref, taps_ref, segc_ref, segr_ref, heads_ref, skip_ref,
        ci_ref, dt_ref, sc_ref, yd_ref,
        step_ref, cc_ref, al_ref, ew_ref, wq_ref, cct_ref, mask_ref, sd_ref, so_ref,
    ) = refs[pieces:]
    t = pl.program_id(0)
    length = xn_ref.shape[0]
    channels = ci_ref.shape[1]
    states = BLK
    inner = channels - 2 * states

    @pl.when(t == 0)
    def _():
        xn = xn_ref[...]
        ci_ref[...] = mm(xn, rows_of(w_refs, slice(0, channels)))
        dt_ref[...] = mm(xn, rows_of(w_refs, slice(channels, channels + BLK)))
        head_setup(dt_ref[...], heads_ref, step_ref, cc_ref, al_ref, ew_ref, wq_ref, cct_ref)
        mask_setup(segc_ref, mask_ref)
        lanes_b = slice(inner, inner + states)
        lanes_c = slice(inner + states, channels)
        _, pre_b = conv_parts(ci_ref[:, lanes_b], taps_ref, lanes_b, mask_ref)
        _, pre_c = conv_parts(ci_ref[:, lanes_c], taps_ref, lanes_c, mask_ref)
        score_setup(
            pre_b * sigmoid(pre_b), pre_c * sigmoid(pre_c),
            segc_ref, segr_ref, sd_ref, so_ref, None, None,
        )

    lanes = pl.ds(pl.multiple_of(t * BLK, BLK), BLK)
    _, pre = conv_parts(ci_ref[:, lanes], taps_ref, lanes, mask_ref)
    v = pre * sigmoid(pre)
    low = iota((1, BLK), 1) < BLK // 2
    shift = lax.rem(BLK - 2 * t, BLK)
    vt = (v * pair_lanes(step_ref, shift, low)).astype(BF16)
    vp = (v * pair_lanes(wq_ref, shift, low)).astype(BF16)
    al2 = pair_lanes(al_ref, shift, low)
    c2 = pltpu.roll(cc_ref[...], shift, axis=1)
    r2 = pltpu.roll(cct_ref[...], lax.rem(cct_ref.shape[0] - 2 * t, cct_ref.shape[0]), axis=0)
    for i in range(length // BLK):
        rows = slice(i * BLK, (i + 1) * BLK)
        before = slice((i - 1) * BLK, i * BLK)
        ms = []
        for k in range(2):
            row = r2[k : k + 1, rows]
            d = jnp.exp2(jnp.minimum(c2[rows, k : k + 1] - row, 0.0))
            ms.append((sd_ref[i] * d).astype(BF16))
        yd = mm(jnp.concatenate(ms, axis=1), block_diag(vt[rows], low))
        yd_ref[rows, :] = yd
        y = yd + skip_ref[...] * v[rows]
        if i > 0:
            y = y + al2[rows] * mm(so_ref[i], vp[before])
        sc_ref[rows, :] = y


def mid_kernel(pieces, *refs):
    gw_refs, ow_refs = refs[:pieces], refs[pieces : 2 * pieces]
    (
        order_ref, xn_ref, sc_ref, gains_ref, cot_ref,
        lo_ref, hi_ref, g_ref, dgate_ref, mixed_ref, ginner_ref, wo_ref,
        gate_ref, dm_ref, nat_ref,
    ) = refs[2 * pieces :]
    devices = order_ref.shape[0]
    share = wo_ref.shape[0] // devices
    per = ow_refs[0].shape[0] // share
    gain = slice(xn_ref.shape[1], gains_ref.shape[1])
    inner = sc_ref.shape[1]
    width = cot_ref.shape[1]
    rows_in = xn_ref.shape[1] // devices
    xn = xn_ref[...]
    gate_ref[...] = mm(xn, rows_of(gw_refs))
    if share % 16:
        wo_ref[...] = rows_of(ow_refs)
    else:
        for p in range(devices):
            at = pl.multiple_of(order_ref[p] * share, 16)
            row = (p % per) * share
            wo_ref[pl.ds(at, share), :] = ow_refs[p // per][row : row + share, :]
    dm_ref[...] = mm_nt(cot_ref[...], wo_ref[...])
    length = xn_ref.shape[0]
    sub = 32
    ginner_ref[...] = jnp.zeros_like(ginner_ref)

    def body(k, carry):
        rows = pl.ds(pl.multiple_of(k * sub, sub), sub)
        gate = gate_ref[rows, :]
        sig = sigmoid(gate)
        silu = gate * sig
        scanned = sc_ref[rows, :]
        gated = scanned * silu
        scale = lax.rsqrt(jnp.mean(gated * gated, axis=-1, keepdims=True) + 1e-05)
        dm = dm_ref[rows, :]
        unit = gated * scale
        mixed_ref[rows, :] = (unit * gains_ref[:, gain]).astype(BF16)
        ginner_ref[...] += jnp.sum((dm * unit).reshape(sub // 8, 8, -1), axis=0)
        dunit = dm * gains_ref[:, gain]
        dot = jnp.mean(unit * dunit, axis=-1, keepdims=True)
        du = scale * (dunit - unit * dot)
        g_ref[rows, :] = du * silu
        dgate_ref[rows, :] = (du * scanned * (sig * (1.0 + gate * (1.0 - sig)))).astype(BF16)
        return carry

    lax.fori_loop(0, length // sub, body, 0)
    if rows_in % 8:
        lo_ref[...] = mm_tn(xn, dgate_ref[...]).astype(BF16)
        hi_ref[...] = mm_tn(mixed_ref[...], cot_ref[...]).astype(BF16)
        return
    gg = mm_tn(xn, dgate_ref[...]).astype(BF16)
    half = gg.shape[0] // 2
    lo_ref[:, :inner] = gg[:half]
    hi_ref[:, :inner] = gg[half:]
    nat_ref[...] = mm_tn(mixed_ref[...], cot_ref[...])
    for p in range(0, devices, 2):
        target = lo_ref if p < devices // 2 else hi_ref
        row = (p % (devices // 2)) * rows_in
        for k in range(2):
            both = [
                nat_ref[pl.ds(pl.multiple_of(order_ref[q] * share + k * rows_in, 8), rows_in), :]
                for q in (p, p + 1)
            ]
            lanes = slice(inner + k * width, inner + (k + 1) * width)
            target[row : row + 2 * rows_in, lanes] = jnp.concatenate(both, axis=0).astype(BF16)


def branch_kernel(mixed_ref, wo_ref, hid_ref, out_ref):
    out_ref[...] = (hid_ref[...].astype(F32) + mm(mixed_ref[...], wo_ref[...])).astype(BF16)


def conv_back(dpre, x, taps_ref, lanes, mask_ref, dtaps_ref, dp_ref, to):
    kernel = mask_ref.shape[0] + 1
    length = dpre.shape[0]

    def total(z):
        return jnp.sum(z, axis=0, keepdims=True)

    dtaps_ref[kernel : kernel + 1, to] = total(dpre)
    dtaps_ref[kernel - 1 : kernel, to] = total(dpre * x)
    dx = taps_ref[kernel - 1 : kernel, lanes] * dpre
    for j in range(1, kernel):
        masked = dpre * mask_ref[j - 1]
        tap = slice(kernel - 1 - j, kernel - j)
        dtaps_ref[tap, to] = total(masked * pltpu.roll(x, j, axis=0))
        dx = dx + taps_ref[tap, lanes] * pltpu.roll(masked, length - j, axis=0)
    dp_ref[:, to] = dx.astype(BF16)


def silu_and_slope(pre):
    sig = sigmoid(pre)
    return pre * sig, sig * (1.0 + pre * (1.0 - sig))


def scan_bwd_kernel(
    g_ref, yd_ref, ci_ref, dt_ref, taps_ref, segc_ref, segr_ref, heads_ref, skip_ref,
    dp_ref, dtaps_ref, dskip_ref, dheads_ref,
    step_ref, cc_ref, al_ref, ew_ref, wq_ref, cct_ref, mask_ref,
    sdt_ref, so_ref, sot_ref, dsdt_ref, dso_ref, acc_ref, dpre_ref,
):
    t = pl.program_id(0)
    length = ci_ref.shape[0]
    blocks = length // BLK
    channels = ci_ref.shape[1]
    states = BLK
    inner = channels - 2 * states
    nheads = inner // (BLK // 2)
    lanes_b = slice(inner, inner + states)
    lanes_c = slice(inner + states, channels)

    @pl.when(t == 0)
    def _():
        head_setup(dt_ref[...], heads_ref, step_ref, cc_ref, al_ref, ew_ref, wq_ref, cct_ref)
        mask_setup(segc_ref, mask_ref)
        dheads_ref[...] = jnp.zeros_like(dheads_ref)
        dtaps_ref[...] = jnp.zeros_like(dtaps_ref)
        _, pre_b = conv_parts(ci_ref[:, lanes_b], taps_ref, lanes_b, mask_ref)
        _, pre_c = conv_parts(ci_ref[:, lanes_c], taps_ref, lanes_c, mask_ref)
        score_setup(
            pre_b * sigmoid(pre_b), pre_c * sigmoid(pre_c),
            segc_ref, segr_ref, None, so_ref, sdt_ref, sot_ref,
        )
        dsdt_ref[...] = jnp.zeros_like(dsdt_ref)
        dso_ref[...] = jnp.zeros_like(dso_ref)
        acc_ref[...] = jnp.zeros_like(acc_ref)

    lanes = pl.ds(pl.multiple_of(t * BLK, BLK), BLK)
    x = ci_ref[:, lanes]
    _, pre = conv_parts(x, taps_ref, lanes, mask_ref)
    v, slope = silu_and_slope(pre)
    low = iota((1, BLK), 1) < BLK // 2
    shift = lax.rem(BLK - 2 * t, BLK)
    st2 = pair_lanes(step_ref, shift, low)
    wq2 = pair_lanes(wq_ref, shift, low)
    ew2 = pair_lanes(ew_ref, shift, low)
    al2 = pair_lanes(al_ref, shift, low)
    c2 = pltpu.roll(cc_ref[...], shift, axis=1)
    r2 = pltpu.roll(cct_ref[...], lax.rem(cct_ref.shape[0] - 2 * t, cct_ref.shape[0]), axis=0)
    vtb = (v * st2).astype(BF16)
    vpb = (v * wq2).astype(BF16)
    g = g_ref[...]
    gb = g.astype(BF16)
    gpb = (al2 * g).astype(BF16)
    dskip_ref[...] = jnp.sum(g * v, axis=0, keepdims=True)
    k_row = iota((4 * BLK, BLK), 0)
    target = jnp.where(k_row >= 2 * BLK, BLK // 2, 0) + 2 * t
    target = target + jnp.where((k_row & (BLK - 1)) >= BLK // 2, 1, 0)
    collect = (iota((4 * BLK, BLK), 1) == target).astype(F32).astype(BF16)
    for i in range(blocks):
        rows = slice(i * BLK, (i + 1) * BLK)
        before = slice((i - 1) * BLK, i * BLK)
        after = slice((i + 1) * BLK, (i + 2) * BLK)
        gdiag = block_diag(gb[rows], low)
        both = mm_nt(vtb[rows], gdiag)
        ms = []
        part = jnp.zeros((BLK, BLK), F32)
        for k in range(2):
            row = r2[k : k + 1, rows]
            d = jnp.exp2(jnp.minimum(row - c2[rows, k : k + 1], 0.0))
            ms.append((sdt_ref[i] * d).astype(BF16))
            part = part + both[:, k * BLK : (k + 1) * BLK] * d
        dsdt_ref[i] += part
        dvt = mm(jnp.concatenate(ms, axis=1), gdiag)
        x1 = gb[rows].astype(F32) * yd_ref[rows, :] - dvt * vtb[rows].astype(F32)
        dv = st2[rows] * dvt + skip_ref[...] * g[rows]
        dstep = dvt
        if i > 0:
            z = mm(so_ref[i], vpb[before])
            x1 = x1 + gpb[rows].astype(F32) * z
            dso_ref[i] += mm_nt(gpb[rows], vpb[before])
        if i + 1 < blocks:
            dvp = mm(sot_ref[i + 1], gpb[after])
            x1 = x1 - dvp * vpb[rows].astype(F32)
            dv = dv + wq2[rows] * dvp
            dstep = dstep + ew2[rows] * dvp
        h1, l1 = split2(x1)
        h2, l2 = split2(dstep * v[rows])
        acc_ref[rows, :] += mm(jnp.concatenate([h1, l1, h2, l2], axis=1), collect)
        dpre_ref[rows, :] = dv * slope[rows]
    conv_back(dpre_ref[...], x, taps_ref, lanes, mask_ref, dtaps_ref, dp_ref, lanes)

    @pl.when(t == pl.num_programs(0) - 1)
    def _():
        xb, xc = ci_ref[:, lanes_b], ci_ref[:, lanes_c]
        _, pre_b = conv_parts(xb, taps_ref, lanes_b, mask_ref)
        _, pre_c = conv_parts(xc, taps_ref, lanes_c, mask_ref)
        bmat, slope_b = silu_and_slope(pre_b)
        cmat, slope_c = silu_and_slope(pre_c)
        bb, cb = bmat.astype(BF16), cmat.astype(BF16)
        causal_t = iota((BLK, BLK), 1) >= iota((BLK, BLK), 0)
        upper = causal_t.astype(F32)
        dst, dso = [], [None]
        for i in range(blocks):
            rows = slice(i * BLK, (i + 1) * BLK)
            before = slice((i - 1) * BLK, i * BLK)
            same = (segc_ref[rows, :] == segr_ref[:, rows]) & causal_t
            dst.append(jnp.where(same, dsdt_ref[i], 0.0))
            if i > 0:
                linked = segc_ref[rows, :] == segr_ref[:, before]
                dso.append(jnp.where(linked, dso_ref[i], 0.0))
        for i in range(blocks):
            rows = slice(i * BLK, (i + 1) * BLK)
            before = slice((i - 1) * BLK, i * BLK)
            after = slice((i + 1) * BLK, (i + 2) * BLK)
            dc = mm(dst[i].T.astype(BF16), bb[rows])
            if i > 0:
                dc = dc + mm(dso[i].astype(BF16), bb[before])
            dpre_ref[rows, :] = dc * slope_c[rows]
        conv_back(dpre_ref[...], xc, taps_ref, lanes_c, mask_ref, dtaps_ref, dp_ref, lanes_c)
        for i in range(blocks):
            rows = slice(i * BLK, (i + 1) * BLK)
            after = slice((i + 1) * BLK, (i + 2) * BLK)
            db = mm(dst[i].astype(BF16), cb[rows])
            if i + 1 < blocks:
                db = db + mm(dso[i + 1].T.astype(BF16), cb[after])
            dpre_ref[rows, :] = db * slope_b[rows]
        conv_back(dpre_ref[...], xb, taps_ref, lanes_b, mask_ref, dtaps_ref, dp_ref, lanes_b)

        decay = jnp.exp(heads_ref[0:1, :])
        later = jnp.zeros((1, BLK), F32)
        dalog = jnp.zeros((1, BLK), F32)
        dbias = jnp.zeros((1, BLK), F32)
        for i in reversed(range(blocks)):
            rows = slice(i * BLK, (i + 1) * BLK)
            dcum = acc_ref[rows, :]
            drate = later + jnp.dot(upper, dcum, precision=HIGH, preferred_element_type=F32)
            later = drate[0:1, :]
            step = step_ref[rows, :]
            dalog = dalog - jnp.sum(drate * step, axis=0, keepdims=True) * decay
            dstep = pltpu.roll(dcum, BLK // 2, axis=1) - drate * decay
            ddt = dstep * sigmoid(dt_ref[rows, :] + heads_ref[2:3, :])
            dbias = dbias + jnp.sum(ddt, axis=0, keepdims=True)
            dp_ref[rows, channels:] = jnp.where(iota((1, BLK), 1) < nheads, ddt, 0.0).astype(BF16)
        dheads_ref[0:1, :] = dalog
        dheads_ref[1:2, :] = dbias


def grad_in_kernel(xn_ref, dp_ref, lo_ref, hi_ref):
    grad = mm_tn(xn_ref[...], dp_ref[...]).astype(BF16)
    half = grad.shape[0] // 2
    lo_ref[...] = grad[:half]
    hi_ref[...] = grad[half:]


def input_kernel(pieces, *refs):
    cw_refs, gw_refs = refs[:pieces], refs[pieces : 2 * pieces]
    (
        dp_ref, dgate_ref, dvec_ref, hid_ref, cot_ref, gains_ref,
        dtaps_ref, ginner_ref, dskip_ref, dheads_ref,
        ig_ref, sums_ref,
    ) = refs[2 * pieces :]
    dn = mm_nt(dp_ref[...], rows_of(cw_refs)) + mm_nt(dgate_ref[...], rows_of(gw_refs))
    perm = perm_matrix(dvec_ref[...], dn.shape[1])
    hi, lo = split2(dn)
    dn = mm_nt(hi, perm) + mm_nt(lo, perm)
    tokens = hid_ref[...].astype(F32)
    scale = lax.rsqrt(jnp.mean(tokens * tokens, axis=-1, keepdims=True) + 1e-05)
    unit = tokens * scale
    width = tokens.shape[1]
    sums_ref[...] = jnp.zeros_like(sums_ref)
    sums_ref[0:5, : dtaps_ref.shape[1]] = dtaps_ref[0:5, :]
    sums_ref[5:6, :width] = jnp.sum(dn * unit, axis=0, keepdims=True)
    sums_ref[5:6, width:] = jnp.sum(ginner_ref[...], axis=0, keepdims=True)
    sums_ref[6:7, : dskip_ref.shape[1]] = dskip_ref[...]
    sums_ref[7:8, :BLK] = dheads_ref[0:1, :]
    sums_ref[7:8, BLK : 2 * BLK] = dheads_ref[1:2, :]
    dunit = dn * gains_ref[:, :width]
    inner = jnp.mean(unit * dunit, axis=-1, keepdims=True)
    ig_ref[...] = cot_ref[...].astype(F32) + scale * (dunit - unit * inner)


def fold_kernel(count, *refs):
    total = refs[0][...].astype(F32)
    for ref in refs[1:count]:
        total = total + ref[...].astype(F32)
    size = total.shape[0] // len(refs[count:])
    for k, ref in enumerate(refs[count:]):
        ref[...] = total[k * size : (k + 1) * size].astype(ref.dtype)


def last_out_kernel(a_ref, b_ref, c_ref, d_ref, gate_ref, out_ref):
    total = a_ref[...].astype(F32) + b_ref[...].astype(F32) + c_ref[...].astype(F32) + d_ref[...].astype(F32)
    inner = gate_ref.shape[1]
    rows, width = a_ref.shape[0], out_ref.shape[1]
    gate_ref[...] = total[:, :inner]
    out_ref[:rows, :] = total[:, inner : inner + width]
    out_ref[rows:, :] = total[:, inner + width :]


def last_in_kernel(a_ref, b_ref, c_ref, d_ref, gate_ref, in_ref):
    total = a_ref[...].astype(F32) + b_ref[...].astype(F32) + c_ref[...].astype(F32) + d_ref[...].astype(F32)
    inner = gate_ref.shape[1]
    in_ref[:, :inner] = gate_ref[...]
    in_ref[:, inner:] = total[:, : in_ref.shape[1] - inner]


def sds(shape, dtype):
    return jax.ShapeDtypeStruct(shape, dtype)


PARAMS = dict(compiler_params=pltpu.CompilerParams(vmem_limit_bytes=60 * 1024 * 1024))


def head_scratch(length, inner):
    nheads = -(-2 * inner // (8 * BLK)) * 8
    return [pltpu.VMEM((length, BLK), F32)] * 5 + [pltpu.VMEM((nheads, length), F32)]


def full(shape):
    return pl.BlockSpec(shape, lambda t: (0,) * len(shape))


def tile(rows):
    return pl.BlockSpec((rows, BLK), lambda t: (0, t))


def scan_fwd(weights, xn, taps, segc, segr, heads, skip_row):
    length = xn.shape[0]
    channels, inner = taps.shape[1], skip_row.shape[1]
    kernel = 4
    blocks = length // BLK
    ins = tuple(weights) + (xn, taps, segc, segr, heads, skip_row)
    count = len(weights)
    return pl.pallas_call(
        lambda *refs: scan_fwd_kernel(count, *refs),
        grid=(inner // BLK,),
        in_specs=[full(a.shape) for a in ins[:-1]] + [tile(1)],
        out_specs=[full((length, channels)), full((length, BLK)), tile(length), tile(length)],
        out_shape=[
            sds((length, channels), F32), sds((length, BLK), F32),
            sds((length, inner), F32), sds((length, inner), F32),
        ],
        scratch_shapes=head_scratch(length, inner) + [
            pltpu.VMEM((kernel - 1, length, BLK), F32),
            pltpu.VMEM((blocks, BLK, BLK), F32),
            pltpu.VMEM((blocks, BLK, BLK), BF16),
        ],
        name="scan_fwd",
        **PARAMS,
    )(*ins)


def scan_bwd(g, yd, ci, dt, taps, segc, segr, heads, skip_row):
    length, channels = ci.shape
    inner = skip_row.shape[1]
    kernel = 4
    blocks = length // BLK
    ins = (g, yd, ci, dt, taps, segc, segr, heads, skip_row)
    score = (blocks, BLK, BLK)
    return pl.pallas_call(
        scan_bwd_kernel,
        grid=(inner // BLK,),
        in_specs=[tile(length), tile(length)] + [full(a.shape) for a in ins[2:8]] + [tile(1)],
        out_specs=[full((length, channels + BLK)), full(taps.shape), tile(1), full((8, BLK))],
        out_shape=[
            sds((length, channels + BLK), BF16), sds(taps.shape, F32), sds((1, inner), F32), sds((8, BLK), F32),
        ],
        scratch_shapes=head_scratch(length, inner) + [
            pltpu.VMEM((kernel - 1, length, BLK), F32),
            pltpu.VMEM(score, F32),
            pltpu.VMEM(score, BF16),
            pltpu.VMEM(score, BF16),
            pltpu.VMEM(score, F32),
            pltpu.VMEM(score, F32),
            pltpu.VMEM((length, BLK), F32),
            pltpu.VMEM((length, BLK), F32),
        ],
        name="scan_bwd",
        **PARAMS,
    )(*ins)


def prep(at, taps_n, hidden, dvec, owner, where, pieces, channels, width):
    ins = (hidden, dvec, owner, where) + tuple(pieces)
    last = pieces[0].shape[1] // BLK - 1
    outs = (sds(hidden.shape, BF16), sds((8, channels), F32), sds((1, width), F32))
    return pl.pallas_call(
        lambda *refs: prep_kernel(at, taps_n, *refs),
        grid=(1,),
        in_specs=[full(a.shape) for a in ins[:4]]
        + [pl.BlockSpec((a.shape[0], BLK), lambda t: (0, last)) for a in pieces],
        out_specs=[full(a.shape) for a in outs],
        out_shape=outs,
        name="prep",
        **PARAMS,
    )(*ins)


def call(kernel, outs, *ins, scratch=(), scalar=None):
    specs = [
        pl.BlockSpec(memory_space=pltpu.SMEM if k == scalar else pltpu.VMEM) for k in range(len(ins))
    ]
    return pl.pallas_call(
        kernel, out_shape=outs, in_specs=specs, scratch_shapes=list(scratch), **PARAMS
    )(*ins)


def stages(devices):
    masks = [1 << b for b in range(devices.bit_length() - 1)]
    groups = []
    for end in range(len(masks), 1, -2):
        part = masks[max(end - 2, 1) : end]
        groups.append(part if len(part) == 1 else [part[0], part[1], part[0] | part[1]])
    return groups + [masks[:1]]


def order_table(devices):
    table = np.zeros((1,), np.int32)
    for group in stages(devices):
        table = np.concatenate([table] + [table ^ m for m in group])
    return table


def send(x, devices, mask):
    return lax.ppermute(x, "fsdp", [(i, i ^ mask) for i in range(devices)])


def send_all(parts, devices, stage):
    return [send(part, devices, m) for part, m in zip(parts, stages(devices)[stage])]


def gather(x, devices):
    groups = stages(devices)
    core = len(groups) - 1
    pieces = [x]
    for stage in range(core):
        x = pieces[0] if len(pieces) == 1 else jnp.concatenate(pieces, axis=0)
        pieces = [x] + send_all([x] * len(groups[stage]), devices, stage)
    return pieces + [send(a, devices, 1) for a in pieces]


def fold(parts, fan, dtype):
    rows, cols = parts[0].shape
    size = rows // fan
    if size % 8:
        total = sum(part.astype(F32) for part in parts).astype(dtype)
        return [total[k * size : (k + 1) * size] for k in range(fan)]
    count = len(parts)
    return call(
        lambda *refs: fold_kernel(count, *refs), tuple(sds((size, cols), dtype) for _ in range(fan)), *parts
    )


def reduce_shares(lo, hi, devices):
    groups = stages(devices)
    parts = [lo, hi]
    for stage in reversed(range(len(groups))):
        parts = [parts[0]] + send_all(parts[1:], devices, stage)
        if stage:
            parts = fold(parts, len(groups[stage - 1]) + 1, BF16)
    return parts


def total_of(x, devices):
    for stage in reversed(range(len(stages(devices)))):
        group = stages(devices)[stage]
        got = send_all([x] * len(group), devices, stage)
        x = x + got[0] if len(got) == 1 else (x + got[0]) + (got[1] + got[2])
    return x


def layer(
    hidden, segment_ids, cot, w_in, w_out, conv_taps, gains, a_log, d_skip, dt_bias
):
    length = segment_ids.shape[1]
    width = hidden.shape[1]
    devices = lax.axis_size("fsdp")
    me = lax.axis_index("fsdp")
    nheads = a_log.shape[0]
    taps_n, tap_share = conv_taps.shape
    channels = tap_share * devices
    gain_share = gains.shape[0]
    inner = w_out.shape[0] * devices
    proj = w_in.shape[1]
    rows_in, rows_out = w_in.shape[0], w_out.shape[0]

    table = order_table(devices)
    inverse = np.argsort(table).astype(np.int32)
    order = jnp.asarray(table) ^ me
    place = jnp.asarray(inverse)[me ^ jnp.arange(devices)]
    dvec = (order[:, None] * rows_in + jnp.arange(rows_in)[None, :]).reshape(1, width)

    spare = BLK - (proj - inner - channels)
    packed = rows_in > taps_n and max(tap_share, gain_share) <= spare
    small = jnp.zeros((rows_in if packed else 8, BLK if not packed else spare), BF16)
    small = small.at[:taps_n, :tap_share].set(conv_taps)
    small = small.at[taps_n, :gain_share].set(gains)
    if packed:
        w_conv = jnp.concatenate([w_in[:, inner:], small], axis=1)
    else:
        w_conv = jnp.pad(w_in[:, inner:], ((0, 0), (0, spare)))
    cw = gather(w_conv, devices)
    gw = gather(w_in[:, :inner], devices)
    ow = gather(w_out, devices)
    count = len(cw)

    heads = jnp.zeros((8, BLK), F32)
    heads = heads.at[0, :nheads].set(a_log).at[1, :nheads].set(d_skip).at[2, :nheads].set(dt_bias)
    skip_row = jnp.repeat(d_skip, inner // nheads)[None]
    segc = segment_ids.reshape(length, 1)

    if packed:
        at = np.arange(width + inner)
        where = np.stack([at % tap_share, at // tap_share, at % gain_share, at // gain_share])
        where = jnp.asarray(np.pad(where, ((0, 4), (0, 0))).astype(np.int32))
        xn, taps, gains_all = prep(
            proj - inner - channels, taps_n, hidden, dvec, order.reshape(devices, 1), where, cw,
            channels, width + inner,
        )
    else:
        rows = jnp.concatenate(gather(small.astype(F32)[None], devices), axis=0)[place]
        taps = jnp.moveaxis(rows[:, :, :tap_share], 0, 1).reshape(8, channels)
        gains_all = rows[:, taps_n, :gain_share].reshape(1, width + inner)
        xn = call(norm_kernel, sds((length, width), BF16), hidden, gains_all, dvec)
    ci, dt, sc, yd = scan_fwd(cw, xn, taps, segc, segment_ids, heads, skip_row)
    if rows_out % 16:
        wo_all = jnp.concatenate(ow, axis=0).reshape(devices, rows_out, width)[place].reshape(inner, width)
        ow = [wo_all[k * (inner // count) : (k + 1) * (inner // count)] for k in range(count)]
    aligned = rows_in % 8 == 0
    if aligned:
        halves = (sds((width // 2, inner + 2 * width), BF16), sds((width // 2, inner + 2 * width), BF16))
    else:
        halves = (sds((width, inner), BF16), sds((inner, width), BF16))
    lo, hi, g, dgate, mixed, ginner, wo = call(
        lambda *refs: mid_kernel(count, *refs),
        halves + (
            sds((length, inner), F32), sds((length, inner), BF16), sds((length, inner), BF16),
            sds((8, inner), F32), sds((inner, width), BF16),
        ),
        *gw, *ow, order, xn, sc, gains_all, cot,
        scratch=(
            pltpu.VMEM((length, inner), F32), pltpu.VMEM((length, inner), F32),
            pltpu.VMEM((inner, width), F32),
        ),
        scalar=2 * count,
    )
    if not aligned:
        gwo = hi.reshape(devices, 2, rows_in, width)[order]
        both = jnp.concatenate([lo, gwo[:, 0].reshape(width, width), gwo[:, 1].reshape(width, width)], axis=1)
        lo, hi = both[: width // 2], both[width // 2 :]
    mid_parts = reduce_shares(lo, hi, devices)
    output = call(branch_kernel, sds((length, width), BF16), mixed, wo, hidden)
    dp, dtaps, dskip, dheads = scan_bwd(g, yd, ci, dt, taps, segc, segment_ids, heads, skip_row)
    half = sds((width // 2, dp.shape[1]), BF16)
    clo, chi = call(grad_in_kernel, (half, half), xn, dp)
    conv_parts_in = reduce_shares(clo, chi, devices)
    input_grad, sums = call(
        lambda *refs: input_kernel(count, *refs),
        (sds((length, width), F32), sds((8, width + inner), F32)),
        *cw, *gw, dp, dgate, dvec, hidden, cot, gains_all, dtaps, ginner, dskip, dheads,
    )
    if aligned and len(mid_parts) == 4:
        gate_share, out_share = call(
            last_out_kernel,
            (sds((rows_in, inner), F32), sds((rows_out, width), F32)), *mid_parts,
        )
        in_share = call(last_in_kernel, sds((rows_in, proj), F32), *conv_parts_in, gate_share)
    else:
        total = sum(part.astype(F32) for part in mid_parts)
        out_share = jnp.concatenate([total[:, inner : inner + width], total[:, inner + width :]], axis=0)
        conv_total = sum(part.astype(F32) for part in conv_parts_in)
        in_share = jnp.concatenate([total[:, :inner], conv_total], axis=1)[:, :proj]

    sums = total_of(sums, devices)
    taps_share = lax.dynamic_slice_in_dim(sums[:taps_n, :channels], me * tap_share, tap_share, axis=1)
    gains_share = lax.dynamic_slice_in_dim(sums[5], me * gain_share, gain_share)
    return (
        output, input_grad, in_share, out_share, taps_share, gains_share,
        sums[7, :nheads], sums[6, :inner].reshape(nheads, -1).sum(axis=1), sums[7, BLK : BLK + nheads],
    )


def solution(mesh):
    axis = P("fsdp")
    rows = P("fsdp", None)
    cols = P(None, "fsdp")
    return jax.shard_map(
        layer,
        mesh=mesh,
        in_specs=(rows, rows, rows, rows, rows, cols, axis, P(), P(), P()),
        out_specs=(rows, rows, rows, rows, cols, axis, P(), P(), P()),
        check_vma=False,
    )
```

```python
import jax
import jax.numpy as jnp
import numpy as np
from jax import lax
from jax.experimental import pallas as pl
from jax.experimental.pallas import tpu as pltpu
from jax.sharding import PartitionSpec as P


BLK = 128
LOG2E = 1.4426950408889634
F32 = jnp.float32
BF16 = jnp.bfloat16
HIGH = lax.Precision.HIGHEST


def mm(a, b):
    return lax.dot_general(a, b, (((1,), (0,)), ((), ())), preferred_element_type=F32)


def mm_nt(a, b):
    return lax.dot_general(a, b, (((1,), (1,)), ((), ())), preferred_element_type=F32)


def mm_tn(a, b):
    return lax.dot_general(a, b, (((0,), (0,)), ((), ())), preferred_element_type=F32)


def split2(x):
    hi = x.astype(BF16)
    return hi, (x - hi.astype(F32)).astype(BF16)


def iota(shape, dim):
    return lax.broadcasted_iota(jnp.int32, shape, dim)


def perm_matrix(dvec, width):
    return (iota((width, width), 0) == dvec).astype(F32).astype(BF16)


def rows_of(refs, lanes=slice(None)):
    return jnp.concatenate([ref[:, lanes] for ref in refs], axis=0)


def normed_of(hid_ref, gain, dvec_ref, xn_ref):
    tokens = hid_ref[...].astype(F32)
    scale = lax.rsqrt(jnp.mean(tokens * tokens, axis=-1, keepdims=True) + 1e-05)
    normed = (tokens * scale * gain).astype(BF16)
    perm = perm_matrix(dvec_ref[...], tokens.shape[1])
    xn_ref[...] = mm(normed, perm).astype(BF16)


def norm_kernel(hid_ref, gains_ref, dvec_ref, xn_ref):
    normed_of(hid_ref, gains_ref[:, : hid_ref.shape[1]], dvec_ref, xn_ref)


def prep_kernel(at, taps_n, hid_ref, dvec_ref, owner_ref, where_ref, *refs):
    pieces, (xn_ref, taps_ref, gains_ref) = refs[:-3], refs[-3:]
    last = pieces[0].shape[1] - BLK
    tail = rows_of(pieces, slice(last, last + BLK))
    devices = owner_ref.shape[0]
    rows_in = tail.shape[0] // devices
    row = iota((8 * devices, tail.shape[0]), 0)
    bits = devices.bit_length() - 1
    source = (row & (devices - 1)) * rows_in + lax.shift_right_logical(row, bits)
    pick = (iota(row.shape, 1) == source).astype(F32).astype(BF16)
    small = mm(pick, tail).astype(BF16)

    def spread(part, line, width):
        lane, owner = where_ref[line : line + 1, :width], where_ref[line + 1 : line + 2, :width]
        chosen = (iota((BLK, width), 0) == lane + at).astype(F32).astype(BF16)
        wide = mm(part, chosen)
        return jnp.sum(jnp.where(owner_ref[...] == owner, wide, 0.0), axis=0, keepdims=True)

    channels, width = taps_ref.shape[1], gains_ref.shape[1]
    taps_ref[...] = jnp.zeros_like(taps_ref)
    for j in range(taps_n):
        taps_ref[j : j + 1, :] = spread(small[j * devices : (j + 1) * devices], 0, channels)
    gains_ref[...] = spread(small[taps_n * devices : (taps_n + 1) * devices], 2, width)
    normed_of(hid_ref, gains_ref[:, : hid_ref.shape[1]], dvec_ref, xn_ref)


def head_setup(dt_raw, heads_ref, step_ref, cc_ref, al_ref, ew_ref, wq_ref, cct_ref):
    length = dt_raw.shape[0]
    biased = dt_raw + heads_ref[2:3, :]
    step = jnp.maximum(biased, 0.0) + jnp.log1p(jnp.exp(-jnp.abs(biased)))
    step_ref[...] = step
    rate = step * (jnp.exp(heads_ref[0:1, :]) * (-LOG2E))
    lower = (iota((BLK, BLK), 0) >= iota((BLK, BLK), 1)).astype(F32)
    for i in range(length // BLK):
        rows = slice(i * BLK, (i + 1) * BLK)
        cc = jnp.dot(lower, rate[rows], precision=HIGH, preferred_element_type=F32)
        cc_ref[rows, :] = cc
        al_ref[rows, :] = jnp.exp2(cc)
        ew = jnp.exp2(jnp.minimum(cc[BLK - 1 : BLK, :] - cc, 0.0))
        ew_ref[rows, :] = ew
        wq_ref[rows, :] = ew * step[rows]
        cct_ref[:, rows] = cc.T[: cct_ref.shape[0]]


def mask_setup(segc_ref, mask_ref):
    seg = segc_ref[...]
    length = seg.shape[0]
    pos = iota((length, BLK), 0)
    segb = jnp.broadcast_to(seg, (length, BLK))
    for j in range(1, mask_ref.shape[0] + 1):
        prev = pltpu.roll(segb, j, axis=0)
        mask_ref[j - 1] = ((prev == segb) & (pos >= j)).astype(F32)


def conv_parts(x, taps_ref, lanes, mask_ref):
    kernel = mask_ref.shape[0] + 1
    shifts = [x] + [pltpu.roll(x, j, axis=0) * mask_ref[j - 1] for j in range(1, kernel)]
    pre = taps_ref[kernel : kernel + 1, lanes] + taps_ref[kernel - 1 : kernel, lanes] * x
    for j in range(1, kernel):
        pre = pre + taps_ref[kernel - 1 - j : kernel - j, lanes] * shifts[j]
    return shifts, pre


def sigmoid(x):
    return 0.5 * jnp.tanh(0.5 * x) + 0.5


def score_setup(bmat, cmat, segc_ref, segr_ref, sd_ref, so_ref, sdt_ref, sot_ref):
    length = bmat.shape[0]
    bb, cb = bmat.astype(BF16), cmat.astype(BF16)
    causal = iota((BLK, BLK), 0) >= iota((BLK, BLK), 1)
    for i in range(length // BLK):
        rows = slice(i * BLK, (i + 1) * BLK)
        before = slice((i - 1) * BLK, i * BLK)
        same = (segc_ref[rows, :] == segr_ref[:, rows]) & causal
        diag = jnp.where(same, mm_nt(cb[rows], bb[rows]), 0.0)
        if sd_ref is not None:
            sd_ref[i] = diag
        if sdt_ref is not None:
            sdt_ref[i] = diag.T
        if i > 0:
            linked = segc_ref[rows, :] == segr_ref[:, before]
            off = jnp.where(linked, mm_nt(cb[rows], bb[before]), 0.0)
            so_ref[i] = off.astype(BF16)
            if sot_ref is not None:
                sot_ref[i] = off.T.astype(BF16)


def pair_lanes(ref, shift, low):
    both = pltpu.roll(ref[...], shift, axis=1)
    return jnp.where(low, both[:, 0:1], both[:, 1:2])


def block_diag(x, low):
    zero = jnp.zeros_like(x)
    return jnp.concatenate([jnp.where(low, x, zero), jnp.where(low, zero, x)], axis=0)


def scan_fwd_kernel(pieces, *refs):
    w_refs = refs[:pieces]
    (
        xn_ref, taps_ref, segc_ref, segr_ref, heads_ref, skip_ref,
        ci_ref, dt_ref, sc_ref, yd_ref,
        step_ref, cc_ref, al_ref, ew_ref, wq_ref, cct_ref, mask_ref, sd_ref, so_ref,
    ) = refs[pieces:]
    length = xn_ref.shape[0]
    channels = ci_ref.shape[1]
    states = BLK
    inner = channels - 2 * states

    xn = xn_ref[...]
    ci_ref[...] = mm(xn, rows_of(w_refs, slice(0, channels)))
    dt_ref[...] = mm(xn, rows_of(w_refs, slice(channels, channels + BLK)))
    head_setup(dt_ref[...], heads_ref, step_ref, cc_ref, al_ref, ew_ref, wq_ref, cct_ref)
    mask_setup(segc_ref, mask_ref)
    lanes_b = slice(inner, inner + states)
    lanes_c = slice(inner + states, channels)
    _, pre_b = conv_parts(ci_ref[:, lanes_b], taps_ref, lanes_b, mask_ref)
    _, pre_c = conv_parts(ci_ref[:, lanes_c], taps_ref, lanes_c, mask_ref)
    score_setup(
        pre_b * sigmoid(pre_b), pre_c * sigmoid(pre_c),
        segc_ref, segr_ref, sd_ref, so_ref, None, None,
    )

    def body(t, carry):
        lanes = pl.ds(pl.multiple_of(t * BLK, BLK), BLK)
        _, pre = conv_parts(ci_ref[:, lanes], taps_ref, lanes, mask_ref)
        v = pre * sigmoid(pre)
        low = iota((1, BLK), 1) < BLK // 2
        shift = lax.rem(BLK - 2 * t, BLK)
        vt = (v * pair_lanes(step_ref, shift, low)).astype(BF16)
        vp = (v * pair_lanes(wq_ref, shift, low)).astype(BF16)
        al2 = pair_lanes(al_ref, shift, low)
        c2 = pltpu.roll(cc_ref[...], shift, axis=1)
        r2 = pltpu.roll(cct_ref[...], lax.rem(cct_ref.shape[0] - 2 * t, cct_ref.shape[0]), axis=0)
        for i in range(length // BLK):
            rows = slice(i * BLK, (i + 1) * BLK)
            before = slice((i - 1) * BLK, i * BLK)
            ms = []
            for k in range(2):
                row = r2[k : k + 1, rows]
                d = jnp.exp2(jnp.minimum(c2[rows, k : k + 1] - row, 0.0))
                ms.append((sd_ref[i] * d).astype(BF16))
            yd = mm(jnp.concatenate(ms, axis=1), block_diag(vt[rows], low))
            yd_ref[rows, lanes] = yd
            y = yd + skip_ref[:, lanes] * v[rows]
            if i > 0:
                y = y + al2[rows] * mm(so_ref[i], vp[before])
            sc_ref[rows, lanes] = y
        return carry

    lax.fori_loop(0, inner // BLK, body, 0)


def mid_kernel(pieces, *refs):
    gw_refs, ow_refs = refs[:pieces], refs[pieces : 2 * pieces]
    (
        order_ref, xn_ref, sc_ref, gains_ref, cot_ref,
        lo_ref, hi_ref, g_ref, dgate_ref, mixed_ref, ginner_ref, wo_ref,
        gate_ref, dm_ref, nat_ref,
    ) = refs[2 * pieces :]
    devices = order_ref.shape[0]
    share = wo_ref.shape[0] // devices
    per = ow_refs[0].shape[0] // share
    gain = slice(xn_ref.shape[1], gains_ref.shape[1])
    inner = sc_ref.shape[1]
    width = cot_ref.shape[1]
    rows_in = xn_ref.shape[1] // devices
    xn = xn_ref[...]
    gate_ref[...] = mm(xn, rows_of(gw_refs))
    if share % 16:
        wo_ref[...] = rows_of(ow_refs)
    else:
        for p in range(devices):
            at = pl.multiple_of(order_ref[p] * share, 16)
            row = (p % per) * share
            wo_ref[pl.ds(at, share), :] = ow_refs[p // per][row : row + share, :]
    dm_ref[...] = mm_nt(cot_ref[...], wo_ref[...])
    length = xn_ref.shape[0]
    sub = 32
    ginner_ref[...] = jnp.zeros_like(ginner_ref)

    def body(k, carry):
        rows = pl.ds(pl.multiple_of(k * sub, sub), sub)
        gate = gate_ref[rows, :]
        sig = sigmoid(gate)
        silu = gate * sig
        scanned = sc_ref[rows, :]
        gated = scanned * silu
        scale = lax.rsqrt(jnp.mean(gated * gated, axis=-1, keepdims=True) + 1e-05)
        dm = dm_ref[rows, :]
        unit = gated * scale
        mixed_ref[rows, :] = (unit * gains_ref[:, gain]).astype(BF16)
        ginner_ref[...] += jnp.sum((dm * unit).reshape(sub // 8, 8, -1), axis=0)
        dunit = dm * gains_ref[:, gain]
        dot = jnp.mean(unit * dunit, axis=-1, keepdims=True)
        du = scale * (dunit - unit * dot)
        g_ref[rows, :] = du * silu
        dgate_ref[rows, :] = (du * scanned * (sig * (1.0 + gate * (1.0 - sig)))).astype(BF16)
        return carry

    lax.fori_loop(0, length // sub, body, 0)
    if rows_in % 8:
        lo_ref[...] = mm_tn(xn, dgate_ref[...]).astype(BF16)
        hi_ref[...] = mm_tn(mixed_ref[...], cot_ref[...]).astype(BF16)
        return
    gg = mm_tn(xn, dgate_ref[...]).astype(BF16)
    half = gg.shape[0] // 2
    lo_ref[:, :inner] = gg[:half]
    hi_ref[:, :inner] = gg[half:]
    nat_ref[...] = mm_tn(mixed_ref[...], cot_ref[...])
    for p in range(0, devices, 2):
        target = lo_ref if p < devices // 2 else hi_ref
        row = (p % (devices // 2)) * rows_in
        for k in range(2):
            both = [
                nat_ref[pl.ds(pl.multiple_of(order_ref[q] * share + k * rows_in, 8), rows_in), :]
                for q in (p, p + 1)
            ]
            lanes = slice(inner + k * width, inner + (k + 1) * width)
            target[row : row + 2 * rows_in, lanes] = jnp.concatenate(both, axis=0).astype(BF16)


def branch_kernel(mixed_ref, wo_ref, hid_ref, out_ref):
    out_ref[...] = (hid_ref[...].astype(F32) + mm(mixed_ref[...], wo_ref[...])).astype(BF16)


def conv_back(dpre, x, taps_ref, lanes, mask_ref, dtaps_ref, dp_ref, to):
    kernel = mask_ref.shape[0] + 1
    length = dpre.shape[0]

    def total(z):
        return jnp.sum(z, axis=0, keepdims=True)

    dtaps_ref[kernel : kernel + 1, to] = total(dpre)
    dtaps_ref[kernel - 1 : kernel, to] = total(dpre * x)
    dx = taps_ref[kernel - 1 : kernel, lanes] * dpre
    for j in range(1, kernel):
        masked = dpre * mask_ref[j - 1]
        tap = slice(kernel - 1 - j, kernel - j)
        dtaps_ref[tap, to] = total(masked * pltpu.roll(x, j, axis=0))
        dx = dx + taps_ref[tap, lanes] * pltpu.roll(masked, length - j, axis=0)
    dp_ref[:, to] = dx.astype(BF16)


def silu_and_slope(pre):
    sig = sigmoid(pre)
    return pre * sig, sig * (1.0 + pre * (1.0 - sig))


def scan_bwd_kernel(
    g_ref, yd_ref, ci_ref, dt_ref, taps_ref, segc_ref, segr_ref, heads_ref, skip_ref,
    dp_ref, dtaps_ref, dskip_ref, dheads_ref,
    step_ref, cc_ref, al_ref, ew_ref, wq_ref, cct_ref, mask_ref,
    sdt_ref, so_ref, sot_ref, dsdt_ref, dso_ref, acc_ref, dpre_ref,
):
    length = ci_ref.shape[0]
    blocks = length // BLK
    channels = ci_ref.shape[1]
    states = BLK
    inner = channels - 2 * states
    nheads = inner // (BLK // 2)
    lanes_b = slice(inner, inner + states)
    lanes_c = slice(inner + states, channels)

    head_setup(dt_ref[...], heads_ref, step_ref, cc_ref, al_ref, ew_ref, wq_ref, cct_ref)
    mask_setup(segc_ref, mask_ref)
    dheads_ref[...] = jnp.zeros_like(dheads_ref)
    dtaps_ref[...] = jnp.zeros_like(dtaps_ref)
    _, pre_b = conv_parts(ci_ref[:, lanes_b], taps_ref, lanes_b, mask_ref)
    _, pre_c = conv_parts(ci_ref[:, lanes_c], taps_ref, lanes_c, mask_ref)
    score_setup(
        pre_b * sigmoid(pre_b), pre_c * sigmoid(pre_c),
        segc_ref, segr_ref, None, so_ref, sdt_ref, sot_ref,
    )
    dsdt_ref[...] = jnp.zeros_like(dsdt_ref)
    dso_ref[...] = jnp.zeros_like(dso_ref)
    acc_ref[...] = jnp.zeros_like(acc_ref)

    def body(t, carry):
        lanes = pl.ds(pl.multiple_of(t * BLK, BLK), BLK)
        x = ci_ref[:, lanes]
        _, pre = conv_parts(x, taps_ref, lanes, mask_ref)
        v, slope = silu_and_slope(pre)
        low = iota((1, BLK), 1) < BLK // 2
        shift = lax.rem(BLK - 2 * t, BLK)
        st2 = pair_lanes(step_ref, shift, low)
        wq2 = pair_lanes(wq_ref, shift, low)
        ew2 = pair_lanes(ew_ref, shift, low)
        al2 = pair_lanes(al_ref, shift, low)
        c2 = pltpu.roll(cc_ref[...], shift, axis=1)
        r2 = pltpu.roll(cct_ref[...], lax.rem(cct_ref.shape[0] - 2 * t, cct_ref.shape[0]), axis=0)
        vtb = (v * st2).astype(BF16)
        vpb = (v * wq2).astype(BF16)
        g = g_ref[:, lanes]
        gb = g.astype(BF16)
        gpb = (al2 * g).astype(BF16)
        dskip_ref[:, lanes] = jnp.sum(g * v, axis=0, keepdims=True)
        k_row = iota((4 * BLK, BLK), 0)
        target = jnp.where(k_row >= 2 * BLK, BLK // 2, 0) + 2 * t
        target = target + jnp.where((k_row & (BLK - 1)) >= BLK // 2, 1, 0)
        collect = (iota((4 * BLK, BLK), 1) == target).astype(F32).astype(BF16)
        for i in range(blocks):
            rows = slice(i * BLK, (i + 1) * BLK)
            before = slice((i - 1) * BLK, i * BLK)
            after = slice((i + 1) * BLK, (i + 2) * BLK)
            gdiag = block_diag(gb[rows], low)
            both = mm_nt(vtb[rows], gdiag)
            ms = []
            part = jnp.zeros((BLK, BLK), F32)
            for k in range(2):
                row = r2[k : k + 1, rows]
                d = jnp.exp2(jnp.minimum(row - c2[rows, k : k + 1], 0.0))
                ms.append((sdt_ref[i] * d).astype(BF16))
                part = part + both[:, k * BLK : (k + 1) * BLK] * d
            dsdt_ref[i] += part
            dvt = mm(jnp.concatenate(ms, axis=1), gdiag)
            x1 = gb[rows].astype(F32) * yd_ref[rows, lanes] - dvt * vtb[rows].astype(F32)
            dv = st2[rows] * dvt + skip_ref[:, lanes] * g[rows]
            dstep = dvt
            if i > 0:
                z = mm(so_ref[i], vpb[before])
                x1 = x1 + gpb[rows].astype(F32) * z
                dso_ref[i] += mm_nt(gpb[rows], vpb[before])
            if i + 1 < blocks:
                dvp = mm(sot_ref[i + 1], gpb[after])
                x1 = x1 - dvp * vpb[rows].astype(F32)
                dv = dv + wq2[rows] * dvp
                dstep = dstep + ew2[rows] * dvp
            h1, l1 = split2(x1)
            h2, l2 = split2(dstep * v[rows])
            acc_ref[rows, :] += mm(jnp.concatenate([h1, l1, h2, l2], axis=1), collect)
            dpre_ref[rows, :] = dv * slope[rows]
        conv_back(dpre_ref[...], x, taps_ref, lanes, mask_ref, dtaps_ref, dp_ref, lanes)
        return carry

    lax.fori_loop(0, inner // BLK, body, 0)
    xb, xc = ci_ref[:, lanes_b], ci_ref[:, lanes_c]
    _, pre_b = conv_parts(xb, taps_ref, lanes_b, mask_ref)
    _, pre_c = conv_parts(xc, taps_ref, lanes_c, mask_ref)
    bmat, slope_b = silu_and_slope(pre_b)
    cmat, slope_c = silu_and_slope(pre_c)
    bb, cb = bmat.astype(BF16), cmat.astype(BF16)
    causal_t = iota((BLK, BLK), 1) >= iota((BLK, BLK), 0)
    upper = causal_t.astype(F32)
    dst, dso = [], [None]
    for i in range(blocks):
        rows = slice(i * BLK, (i + 1) * BLK)
        before = slice((i - 1) * BLK, i * BLK)
        same = (segc_ref[rows, :] == segr_ref[:, rows]) & causal_t
        dst.append(jnp.where(same, dsdt_ref[i], 0.0))
        if i > 0:
            linked = segc_ref[rows, :] == segr_ref[:, before]
            dso.append(jnp.where(linked, dso_ref[i], 0.0))
    for i in range(blocks):
        rows = slice(i * BLK, (i + 1) * BLK)
        before = slice((i - 1) * BLK, i * BLK)
        after = slice((i + 1) * BLK, (i + 2) * BLK)
        dc = mm(dst[i].T.astype(BF16), bb[rows])
        if i > 0:
            dc = dc + mm(dso[i].astype(BF16), bb[before])
        dpre_ref[rows, :] = dc * slope_c[rows]
    conv_back(dpre_ref[...], xc, taps_ref, lanes_c, mask_ref, dtaps_ref, dp_ref, lanes_c)
    for i in range(blocks):
        rows = slice(i * BLK, (i + 1) * BLK)
        after = slice((i + 1) * BLK, (i + 2) * BLK)
        db = mm(dst[i].astype(BF16), cb[rows])
        if i + 1 < blocks:
            db = db + mm(dso[i + 1].T.astype(BF16), cb[after])
        dpre_ref[rows, :] = db * slope_b[rows]
    conv_back(dpre_ref[...], xb, taps_ref, lanes_b, mask_ref, dtaps_ref, dp_ref, lanes_b)

    decay = jnp.exp(heads_ref[0:1, :])
    later = jnp.zeros((1, BLK), F32)
    dalog = jnp.zeros((1, BLK), F32)
    dbias = jnp.zeros((1, BLK), F32)
    for i in reversed(range(blocks)):
        rows = slice(i * BLK, (i + 1) * BLK)
        dcum = acc_ref[rows, :]
        drate = later + jnp.dot(upper, dcum, precision=HIGH, preferred_element_type=F32)
        later = drate[0:1, :]
        step = step_ref[rows, :]
        dalog = dalog - jnp.sum(drate * step, axis=0, keepdims=True) * decay
        dstep = pltpu.roll(dcum, BLK // 2, axis=1) - drate * decay
        ddt = dstep * sigmoid(dt_ref[rows, :] + heads_ref[2:3, :])
        dbias = dbias + jnp.sum(ddt, axis=0, keepdims=True)
        dp_ref[rows, channels:] = jnp.where(iota((1, BLK), 1) < nheads, ddt, 0.0).astype(BF16)
    dheads_ref[0:1, :] = dalog
    dheads_ref[1:2, :] = dbias


def grad_in_kernel(xn_ref, dp_ref, lo_ref, hi_ref):
    grad = mm_tn(xn_ref[...], dp_ref[...]).astype(BF16)
    half = grad.shape[0] // 2
    lo_ref[...] = grad[:half]
    hi_ref[...] = grad[half:]


def input_kernel(pieces, *refs):
    cw_refs, gw_refs = refs[:pieces], refs[pieces : 2 * pieces]
    (
        dp_ref, dgate_ref, dvec_ref, hid_ref, cot_ref, gains_ref,
        dtaps_ref, ginner_ref, dskip_ref, dheads_ref,
        ig_ref, sums_ref,
    ) = refs[2 * pieces :]
    dn = mm_nt(dp_ref[...], rows_of(cw_refs)) + mm_nt(dgate_ref[...], rows_of(gw_refs))
    perm = perm_matrix(dvec_ref[...], dn.shape[1])
    hi, lo = split2(dn)
    dn = mm_nt(hi, perm) + mm_nt(lo, perm)
    tokens = hid_ref[...].astype(F32)
    scale = lax.rsqrt(jnp.mean(tokens * tokens, axis=-1, keepdims=True) + 1e-05)
    unit = tokens * scale
    width = tokens.shape[1]
    sums_ref[...] = jnp.zeros_like(sums_ref)
    sums_ref[0:5, : dtaps_ref.shape[1]] = dtaps_ref[0:5, :]
    sums_ref[5:6, :width] = jnp.sum(dn * unit, axis=0, keepdims=True)
    sums_ref[5:6, width:] = jnp.sum(ginner_ref[...], axis=0, keepdims=True)
    sums_ref[6:7, : dskip_ref.shape[1]] = dskip_ref[...]
    sums_ref[7:8, :BLK] = dheads_ref[0:1, :]
    sums_ref[7:8, BLK : 2 * BLK] = dheads_ref[1:2, :]
    dunit = dn * gains_ref[:, :width]
    inner = jnp.mean(unit * dunit, axis=-1, keepdims=True)
    ig_ref[...] = cot_ref[...].astype(F32) + scale * (dunit - unit * inner)


def stack_kernel(*refs):
    rows = jnp.concatenate([ref[...].astype(F32) for ref in refs[:-1]], axis=0)
    refs[-1][...] = rows.astype(BF16)


def fold_kernel(count, *refs):
    total = refs[0][...].astype(F32)
    for ref in refs[1:count]:
        total = total + ref[...].astype(F32)
    size = total.shape[0] // len(refs[count:])
    for k, ref in enumerate(refs[count:]):
        ref[...] = total[k * size : (k + 1) * size].astype(ref.dtype)


def last_out_kernel(a_ref, b_ref, c_ref, d_ref, gate_ref, out_ref):
    total = a_ref[...].astype(F32) + b_ref[...].astype(F32) + c_ref[...].astype(F32) + d_ref[...].astype(F32)
    inner = gate_ref.shape[1]
    rows, width = a_ref.shape[0], out_ref.shape[1]
    gate_ref[...] = total[:, :inner]
    out_ref[:rows, :] = total[:, inner : inner + width]
    out_ref[rows:, :] = total[:, inner + width :]


def last_in_kernel(a_ref, b_ref, c_ref, d_ref, gate_ref, in_ref):
    total = a_ref[...].astype(F32) + b_ref[...].astype(F32) + c_ref[...].astype(F32) + d_ref[...].astype(F32)
    inner = gate_ref.shape[1]
    in_ref[:, :inner] = gate_ref[...]
    in_ref[:, inner:] = total[:, : in_ref.shape[1] - inner]


def sds(shape, dtype):
    return jax.ShapeDtypeStruct(shape, dtype)


def held(shape, dtype):
    return pltpu.VMEM(shape, dtype)


PARAMS = dict(compiler_params=pltpu.CompilerParams(vmem_limit_bytes=20 * 1024 * 1024))


def head_scratch(length, inner):
    nheads = -(-2 * inner // (8 * BLK)) * 8
    return [pltpu.VMEM((length, BLK), F32)] * 5 + [pltpu.VMEM((nheads, length), F32)]


def scan_scratch(length, inner, taps):
    return head_scratch(length, inner) + [pltpu.VMEM((taps - 1, length, BLK), F32)]


def scan_fwd(weights, taps_n, xn, taps, segc, segr, heads, skip_row):
    length = xn.shape[0]
    channels, inner = taps.shape[1], skip_row.shape[1]
    blocks = length // BLK
    count = len(weights)
    return call(
        lambda *refs: scan_fwd_kernel(count, *refs),
        (
            held((length, channels), F32), held((length, BLK), F32),
            held((length, inner), F32), held((length, inner), F32),
        ),
        *weights, xn, taps, segc, segr, heads, skip_row,
        scratch=scan_scratch(length, inner, taps_n - 1) + [
            pltpu.VMEM((blocks, BLK, BLK), F32),
            pltpu.VMEM((blocks, BLK, BLK), BF16),
        ],
    )


def scan_bwd(taps_n, g, yd, ci, dt, taps, segc, segr, heads, skip_row):
    length, channels = ci.shape
    inner = skip_row.shape[1]
    score = (length // BLK, BLK, BLK)
    return call(
        scan_bwd_kernel,
        (
            held((length, channels + BLK), BF16), held(taps.shape, F32), held((1, inner), F32),
            held((8, BLK), F32),
        ),
        g, yd, ci, dt, taps, segc, segr, heads, skip_row,
        scratch=scan_scratch(length, inner, taps_n - 1) + [
            pltpu.VMEM(score, F32),
            pltpu.VMEM(score, BF16),
            pltpu.VMEM(score, BF16),
            pltpu.VMEM(score, F32),
            pltpu.VMEM(score, F32),
            pltpu.VMEM((length, BLK), F32),
            pltpu.VMEM((length, BLK), F32),
        ],
    )


def prep(at, taps_n, hidden, dvec, owner, where, pieces, channels, width):
    return call(
        lambda *refs: prep_kernel(at, taps_n, *refs),
        (held(hidden.shape, BF16), held((8, channels), F32), held((1, width), F32)),
        hidden, dvec, owner, where, *pieces,
    )


def call(kernel, outs, *ins, scratch=(), scalar=None):
    specs = [
        pl.BlockSpec(memory_space=pltpu.SMEM if k == scalar else pltpu.VMEM) for k in range(len(ins))
    ]
    near = [a if k == scalar else pltpu.with_memory_space_constraint(a, pltpu.VMEM) for k, a in enumerate(ins)]
    many = isinstance(outs, (tuple, list))
    out_specs = [pl.BlockSpec(memory_space=pltpu.VMEM) for _ in outs] if many else pl.BlockSpec(memory_space=pltpu.VMEM)
    return pl.pallas_call(
        kernel, out_shape=outs, in_specs=specs, out_specs=out_specs, scratch_shapes=list(scratch), **PARAMS
    )(*near)


def stages(devices):
    masks = [1 << b for b in range(devices.bit_length() - 1)]
    groups = []
    for end in range(len(masks), 1, -2):
        part = masks[max(end - 2, 1) : end]
        groups.append(part if len(part) == 1 else [part[0], part[1], part[0] | part[1]])
    return groups + [masks[:1]]


def order_table(devices):
    table = np.zeros((1,), np.int32)
    for group in stages(devices):
        table = np.concatenate([table] + [table ^ m for m in group])
    return table


def send(x, devices, mask):
    return lax.ppermute(x, "fsdp", [(i, i ^ mask) for i in range(devices)])


def send_all(parts, devices, stage):
    return [send(part, devices, m) for part, m in zip(parts, stages(devices)[stage])]


def stack(pieces):
    size, rest = pieces[0].shape[0], pieces[0].shape[1:]
    if size % 8 or len(rest) != 1:
        return jnp.concatenate(pieces, axis=0)
    return call(stack_kernel, held((len(pieces) * size,) + rest, BF16), *pieces)


def gather(x, devices):
    groups = stages(devices)
    core = len(groups) - 1
    pieces = [x]
    for stage in range(core):
        x = pieces[0] if len(pieces) == 1 else stack(pieces)
        pieces = [x] + send_all([x] * len(groups[stage]), devices, stage)
    return pieces + [send(a, devices, 1) for a in pieces]


def fold(parts, fan, dtype):
    rows, cols = parts[0].shape
    size = rows // fan
    if size % 8:
        total = sum(part.astype(F32) for part in parts).astype(dtype)
        return [total[k * size : (k + 1) * size] for k in range(fan)]
    count = len(parts)
    return call(lambda *refs: fold_kernel(count, *refs), tuple(held((size, cols), dtype) for _ in range(fan)), *parts)


def reduce_shares(lo, hi, devices):
    groups = stages(devices)
    parts = [lo, hi]
    for stage in reversed(range(len(groups))):
        parts = [parts[0]] + send_all(parts[1:], devices, stage)
        if stage:
            parts = fold(parts, len(groups[stage - 1]) + 1, BF16)
    return parts


def total_of(x, devices):
    for stage in reversed(range(len(stages(devices)))):
        group = stages(devices)[stage]
        got = send_all([x] * len(group), devices, stage)
        x = x + got[0] if len(got) == 1 else (x + got[0]) + (got[1] + got[2])
    return x


def layer(
    hidden, segment_ids, cot, w_in, w_out, conv_taps, gains, a_log, d_skip, dt_bias
):
    length = segment_ids.shape[1]
    width = hidden.shape[1]
    devices = lax.axis_size("fsdp")
    me = lax.axis_index("fsdp")
    nheads = a_log.shape[0]
    taps_n, tap_share = conv_taps.shape
    channels = tap_share * devices
    gain_share = gains.shape[0]
    inner = w_out.shape[0] * devices
    proj = w_in.shape[1]
    rows_in, rows_out = w_in.shape[0], w_out.shape[0]

    table = order_table(devices)
    inverse = np.argsort(table).astype(np.int32)
    order = jnp.asarray(table) ^ me
    place = jnp.asarray(inverse)[me ^ jnp.arange(devices)]
    dvec = (order[:, None] * rows_in + jnp.arange(rows_in)[None, :]).reshape(1, width)

    spare = BLK - (proj - inner - channels)
    packed = rows_in > taps_n and max(tap_share, gain_share) <= spare
    small = jnp.zeros((rows_in if packed else 8, BLK if not packed else spare), BF16)
    small = small.at[:taps_n, :tap_share].set(conv_taps)
    small = small.at[taps_n, :gain_share].set(gains)
    if packed:
        w_conv = jnp.concatenate([w_in[:, inner:], small], axis=1)
    else:
        w_conv = jnp.pad(w_in[:, inner:], ((0, 0), (0, spare)))
    cw = gather(w_conv, devices)
    gw = gather(w_in[:, :inner], devices)
    ow = gather(w_out, devices)
    count = len(cw)

    heads = jnp.zeros((8, BLK), F32)
    heads = heads.at[0, :nheads].set(a_log).at[1, :nheads].set(d_skip).at[2, :nheads].set(dt_bias)
    skip_row = jnp.repeat(d_skip, inner // nheads)[None]
    segc = segment_ids.reshape(length, 1)

    if packed:
        at = np.arange(width + inner)
        where = np.stack([at % tap_share, at // tap_share, at % gain_share, at // gain_share])
        where = jnp.asarray(np.pad(where, ((0, 4), (0, 0))).astype(np.int32))
        xn, taps, gains_all = prep(
            proj - inner - channels, taps_n, hidden, dvec, order.reshape(devices, 1), where, cw,
            channels, width + inner,
        )
    else:
        rows = jnp.concatenate(gather(small.astype(F32)[None], devices), axis=0)[place]
        taps = jnp.moveaxis(rows[:, :, :tap_share], 0, 1).reshape(8, channels)
        gains_all = rows[:, taps_n, :gain_share].reshape(1, width + inner)
        xn = call(norm_kernel, sds((length, width), BF16), hidden, gains_all, dvec)
    ci, dt, sc, yd = scan_fwd(cw, taps_n, xn, taps, segc, segment_ids, heads, skip_row)
    if rows_out % 16:
        wo_all = jnp.concatenate(ow, axis=0).reshape(devices, rows_out, width)[place].reshape(inner, width)
        ow = [wo_all[k * (inner // count) : (k + 1) * (inner // count)] for k in range(count)]
    aligned = rows_in % 8 == 0
    if aligned:
        halves = (held((width // 2, inner + 2 * width), BF16), held((width // 2, inner + 2 * width), BF16))
    else:
        halves = (sds((width, inner), BF16), sds((inner, width), BF16))
    lo, hi, g, dgate, mixed, ginner, wo = call(
        lambda *refs: mid_kernel(count, *refs),
        halves + (
            held((length, inner), F32), held((length, inner), BF16), held((length, inner), BF16),
            held((8, inner), F32), held((inner, width), BF16),
        ),
        *gw, *ow, order, xn, sc, gains_all, cot,
        scratch=(
            pltpu.VMEM((length, inner), F32), pltpu.VMEM((length, inner), F32),
            pltpu.VMEM((inner, width), F32),
        ),
        scalar=2 * count,
    )
    if not aligned:
        gwo = hi.reshape(devices, 2, rows_in, width)[order]
        both = jnp.concatenate([lo, gwo[:, 0].reshape(width, width), gwo[:, 1].reshape(width, width)], axis=1)
        lo, hi = both[: width // 2], both[width // 2 :]
    mid_parts = reduce_shares(lo, hi, devices)
    output = call(branch_kernel, sds((length, width), BF16), mixed, wo, hidden)
    dp, dtaps, dskip, dheads = scan_bwd(taps_n, g, yd, ci, dt, taps, segc, segment_ids, heads, skip_row)
    half = held((width // 2, dp.shape[1]), BF16)
    clo, chi = call(grad_in_kernel, (half, half), xn, dp)
    conv_parts_in = reduce_shares(clo, chi, devices)
    input_grad, sums = call(
        lambda *refs: input_kernel(count, *refs),
        (sds((length, width), F32), sds((8, width + inner), F32)),
        *cw, *gw, dp, dgate, dvec, hidden, cot, gains_all, dtaps, ginner, dskip, dheads,
    )
    if aligned and len(mid_parts) == 4:
        gate_share, out_share = call(
            last_out_kernel,
            (sds((rows_in, inner), F32), sds((rows_out, width), F32)), *mid_parts,
        )
        in_share = call(last_in_kernel, sds((rows_in, proj), F32), *conv_parts_in, gate_share)
    else:
        total = sum(part.astype(F32) for part in mid_parts)
        out_share = jnp.concatenate([total[:, inner : inner + width], total[:, inner + width :]], axis=0)
        conv_total = sum(part.astype(F32) for part in conv_parts_in)
        in_share = jnp.concatenate([total[:, :inner], conv_total], axis=1)[:, :proj]

    sums = total_of(sums, devices)
    taps_share = lax.dynamic_slice_in_dim(sums[:taps_n, :channels], me * tap_share, tap_share, axis=1)
    gains_share = lax.dynamic_slice_in_dim(sums[5], me * gain_share, gain_share)
    return (
        output, input_grad, in_share, out_share, taps_share, gains_share,
        sums[7, :nheads], sums[6, :inner].reshape(nheads, -1).sum(axis=1), sums[7, BLK : BLK + nheads],
    )


def solution(mesh):
    axis = P("fsdp")
    rows = P("fsdp", None)
    cols = P(None, "fsdp")
    return jax.shard_map(
        layer,
        mesh=mesh,
        in_specs=(rows, rows, rows, rows, rows, cols, axis, P(), P(), P()),
        out_specs=(rows, rows, rows, rows, cols, axis, P(), P(), P()),
        check_vma=False,
    )
```

```python
import jax
import jax.numpy as jnp
import numpy as np
from jax import lax
from jax.experimental import pallas as pl
from jax.experimental.pallas import tpu as pltpu
from jax.sharding import PartitionSpec as P


BLK = 128
LOG2E = 1.4426950408889634
F32 = jnp.float32
BF16 = jnp.bfloat16
HIGH = lax.Precision.HIGHEST


def mm(a, b):
    return lax.dot_general(a, b, (((1,), (0,)), ((), ())), preferred_element_type=F32)


def mm_nt(a, b):
    return lax.dot_general(a, b, (((1,), (1,)), ((), ())), preferred_element_type=F32)


def mm_tn(a, b):
    return lax.dot_general(a, b, (((0,), (0,)), ((), ())), preferred_element_type=F32)


def split2(x):
    hi = x.astype(BF16)
    return hi, (x - hi.astype(F32)).astype(BF16)


def iota(shape, dim):
    return lax.broadcasted_iota(jnp.int32, shape, dim)


def perm_matrix(me, tab_ref, width):
    dvec = (tab_ref[0:1, :] ^ me) * tab_ref[2:3, 0:1] + tab_ref[1:2, :]
    return (iota((width, width), 0) == dvec).astype(F32).astype(BF16)


def rows_of(refs, lanes=slice(None)):
    return jnp.concatenate([ref[:, lanes] for ref in refs], axis=0)


def normed_of(hid_ref, gain, me, tab_ref, xn_ref):
    tokens = hid_ref[...].astype(F32)
    scale = lax.rsqrt(jnp.mean(tokens * tokens, axis=-1, keepdims=True) + 1e-05)
    normed = (tokens * scale * gain).astype(BF16)
    perm = perm_matrix(me, tab_ref, tokens.shape[1])
    xn_ref[...] = mm(normed, perm).astype(BF16)


def pack_kernel(inner, w_ref, taps_in, gains_in, conv_ref, gate_ref):
    gate_ref[...] = w_ref[:, :inner]
    body = conv_ref.shape[1] - BLK
    conv_ref[:, :body] = w_ref[:, inner : inner + body]
    tail = w_ref[:, inner + body :]
    spare = tail.shape[1]
    rows, taps_n = w_ref.shape[0], taps_in.shape[0]

    def onto(x, at):
        return mm(x, (iota((x.shape[1], BLK), 1) == iota((x.shape[1], BLK), 0) + at).astype(F32).astype(BF16))

    row = iota((rows, BLK), 0)
    tile_of = onto(tail, 0)
    taps_wide, gains_wide = onto(taps_in[...], spare), onto(gains_in[...], spare)
    for j in range(taps_n):
        tile_of = tile_of + jnp.where(row == j, taps_wide[j : j + 1, :], 0.0)
    tile_of = tile_of + jnp.where(row == taps_n, gains_wide, 0.0)
    conv_ref[:, body:] = tile_of.astype(BF16)


def unpack(at, taps_n, pieces, me, owner_ref, where_ref, taps_ref, gains_ref):
    last = pieces[0].shape[1] - BLK
    tail = rows_of(pieces, slice(last, last + BLK))
    devices = owner_ref.shape[0]
    rows_in = tail.shape[0] // devices
    row = iota((8 * devices, tail.shape[0]), 0)
    bits = devices.bit_length() - 1
    source = (row & (devices - 1)) * rows_in + lax.shift_right_logical(row, bits)
    pick = (iota(row.shape, 1) == source).astype(F32).astype(BF16)
    small = mm(pick, tail).astype(BF16)

    def spread(part, line, width):
        lane, owner = where_ref[line : line + 1, :width], where_ref[line + 1 : line + 2, :width]
        chosen = (iota((BLK, width), 0) == lane + at).astype(F32).astype(BF16)
        wide = mm(part, chosen)
        return jnp.sum(jnp.where((owner_ref[...] ^ me) == owner, wide, 0.0), axis=0, keepdims=True)

    channels, width = taps_ref.shape[1], gains_ref.shape[1]
    taps_ref[...] = jnp.zeros_like(taps_ref)
    for j in range(taps_n):
        taps_ref[j : j + 1, :] = spread(small[j * devices : (j + 1) * devices], 0, channels)
    gains_ref[...] = spread(small[taps_n * devices : (taps_n + 1) * devices], 2, width)


def split3(x):
    hi, rest = split2(x)
    lo = (x - hi.astype(F32) - rest.astype(F32)).astype(BF16)
    return hi, rest, lo


def head_setup(dt_raw, rows_in, segr, heads_ref, step_ref, cc_ref, wide_ref, cct_ref, segb_ref):
    length = dt_raw.shape[0]
    heads_ref[...] = jnp.zeros_like(heads_ref)
    for k, ref in enumerate(rows_in):
        heads_ref[k : k + 1, : ref.shape[1]] = ref[...]
    segb_ref[...] = jnp.broadcast_to(segr, (BLK, length)).T
    biased = dt_raw + heads_ref[2:3, :]
    step = jnp.maximum(biased, 0.0) + jnp.log1p(jnp.exp(-jnp.abs(biased)))
    step_ref[...] = step
    rate = step * (jnp.exp(heads_ref[0:1, :]) * (-LOG2E))
    lower = (iota((BLK, BLK), 0) >= iota((BLK, BLK), 1)).astype(F32)
    for i in range(length // BLK):
        rows = slice(i * BLK, (i + 1) * BLK)
        cc = jnp.dot(lower, rate[rows], precision=HIGH, preferred_element_type=F32)
        cc_ref[rows, :] = jnp.concatenate(split3(cc), axis=1)
        ew = jnp.exp2(jnp.minimum(cc[BLK - 1 : BLK, :] - cc, 0.0))
        for k, x in enumerate((step[rows], ew * step[rows], jnp.exp2(cc), ew)):
            wide_ref[k, rows, :] = jnp.concatenate(split2(x), axis=1)
        cct_ref[:, rows] = cc.T[: cct_ref.shape[0]]


def mask_setup(segb_ref, mask_ref):
    segb = segb_ref[...]
    pos = iota(segb.shape, 0)
    for j in range(1, mask_ref.shape[0] + 1):
        prev = pltpu.roll(segb, j, axis=0)
        mask_ref[j - 1] = ((prev == segb) & (pos >= j)).astype(F32)


def conv_parts(x, taps_ref, lanes, mask_ref):
    kernel = mask_ref.shape[0] + 1
    shifts = [x] + [pltpu.roll(x, j, axis=0) * mask_ref[j - 1] for j in range(1, kernel)]
    pre = taps_ref[kernel : kernel + 1, lanes] + taps_ref[kernel - 1 : kernel, lanes] * x
    for j in range(1, kernel):
        pre = pre + taps_ref[kernel - 1 - j : kernel - j, lanes] * shifts[j]
    return shifts, pre


def sigmoid(x):
    return 0.5 * jnp.tanh(0.5 * x) + 0.5


def score_setup(bmat, cmat, segb_ref, segr, sd_ref, so_ref, sdt_ref, sot_ref):
    length = bmat.shape[0]
    bb, cb = bmat.astype(BF16), cmat.astype(BF16)
    causal = iota((BLK, BLK), 0) >= iota((BLK, BLK), 1)
    for i in range(length // BLK):
        rows = slice(i * BLK, (i + 1) * BLK)
        before = slice((i - 1) * BLK, i * BLK)
        same = (segb_ref[rows, :] == segr[:, rows]) & causal
        diag = jnp.where(same, mm_nt(cb[rows], bb[rows]), 0.0)
        if sd_ref is not None:
            sd_ref[i] = diag
        if sdt_ref is not None:
            sdt_ref[i] = diag.T
        if i > 0:
            linked = segb_ref[rows, :] == segr[:, before]
            off = jnp.where(linked, mm_nt(cb[rows], bb[before]), 0.0)
            so_ref[i] = off.astype(BF16)
            if sot_ref is not None:
                sot_ref[i] = off.T.astype(BF16)


def pair_setup(t, heads_ref, wide_ref, cc_ref, cct_ref, count):
    head = iota((2 * BLK, BLK), 0) & (BLK - 1)
    pick = (head == 2 * t + jnp.where(iota((2 * BLK, BLK), 1) < BLK // 2, 0, 1)).astype(F32).astype(BF16)
    spread = [mm(wide_ref[k], pick) for k in range(count)]
    head = iota((3 * BLK, 2 * BLK), 0) & (BLK - 1)
    each = (head == 2 * t + jnp.where(iota((3 * BLK, 2 * BLK), 1) < BLK, 0, 1)).astype(F32).astype(BF16)
    c2 = mm(cc_ref[...], each)
    r2 = pltpu.roll(cct_ref[...], lax.rem(cct_ref.shape[0] - 2 * t, cct_ref.shape[0]), axis=0)
    h2 = pltpu.roll(heads_ref[...], lax.rem(BLK - 2 * t, BLK), axis=1)
    skip = jnp.where(iota((1, BLK), 1) < BLK // 2, h2[1:2, 0:1], h2[1:2, 1:2])
    return spread, c2, r2, skip


def block_diag(x, low):
    zero = jnp.zeros_like(x)
    return jnp.concatenate([jnp.where(low, x, zero), jnp.where(low, zero, x)], axis=0)


def scan_fwd_kernel(pieces, packed, *refs):
    w_refs = refs[:pieces]
    (
        me_ref, tab_ref, hid_ref, first_ref, second_ref, segr_ref, alog_ref, skip_ref, bias_ref,
        xn_ref, taps_ref, gains_ref, wc_ref, ci_ref, dt_ref, sc_ref, yd_ref, v_ref, slope_ref,
        heads_ref, step_ref, cc_ref, wide_ref, cct_ref, segb_ref, mask_ref, sd_ref, so_ref,
    ) = refs[pieces:]
    me = me_ref[0]
    segr = segr_ref[...].astype(F32)
    length = xn_ref.shape[0]
    channels = ci_ref.shape[1]
    states = BLK
    inner = channels - 2 * states
    if packed:
        unpack(packed[0], packed[1], w_refs, me, first_ref, second_ref, taps_ref, gains_ref)
    else:
        taps_ref[...] = first_ref[...]
        gains_ref[...] = second_ref[...]
    normed_of(hid_ref, gains_ref[:, : hid_ref.shape[1]], me, tab_ref, xn_ref)
    xn = xn_ref[...]
    wc_ref[...] = rows_of(w_refs)
    ci_ref[...] = mm(xn, wc_ref[:, :channels])
    dt_ref[...] = mm(xn, wc_ref[:, channels:])
    head_setup(
        dt_ref[...], (alog_ref, skip_ref, bias_ref), segr, heads_ref, step_ref, cc_ref, wide_ref, cct_ref, segb_ref
    )
    mask_setup(segb_ref, mask_ref)
    lanes_b = slice(inner, inner + states)
    lanes_c = slice(inner + states, channels)
    _, pre_b = conv_parts(ci_ref[:, lanes_b], taps_ref, lanes_b, mask_ref)
    _, pre_c = conv_parts(ci_ref[:, lanes_c], taps_ref, lanes_c, mask_ref)
    score_setup(
        pre_b * sigmoid(pre_b), pre_c * sigmoid(pre_c),
        segb_ref, segr, sd_ref, so_ref, None, None,
    )

    def body(t, carry):
        lanes = pl.ds(pl.multiple_of(t * BLK, BLK), BLK)
        _, pre = conv_parts(ci_ref[:, lanes], taps_ref, lanes, mask_ref)
        v, slope = silu_and_slope(pre)
        v_ref[:, lanes] = v
        slope_ref[:, lanes] = slope
        low = iota((1, BLK), 1) < BLK // 2
        (st2, wq2, al2), c2, r2, skip = pair_setup(t, heads_ref, wide_ref, cc_ref, cct_ref, 3)
        vt = (v * st2).astype(BF16)
        vp = (v * wq2).astype(BF16)
        for i in range(length // BLK):
            rows = slice(i * BLK, (i + 1) * BLK)
            before = slice((i - 1) * BLK, i * BLK)
            ms = []
            for k in range(2):
                row = r2[k : k + 1, rows]
                d = jnp.exp2(jnp.minimum(c2[rows, k * BLK : (k + 1) * BLK] - row, 0.0))
                ms.append((sd_ref[i] * d).astype(BF16))
            yd = mm(jnp.concatenate(ms, axis=1), block_diag(vt[rows], low))
            yd_ref[rows, lanes] = yd
            y = yd + skip * v[rows]
            if i > 0:
                y = y + al2[rows] * mm(so_ref[i], vp[before])
            sc_ref[rows, lanes] = y
        return carry

    lax.fori_loop(0, inner // BLK, body, 0)


def mid_kernel(pieces, table, *refs):
    gw_refs, ow_refs = refs[:pieces], refs[pieces : 2 * pieces]
    (
        me_ref, xn_ref, sc_ref, gains_ref, cot_ref,
        lo_ref, hi_ref, g_ref, dgate_ref, mixed_ref, ginner_ref, wo_ref, wg_ref,
        dm_ref, nat_ref,
    ) = refs[2 * pieces :]
    me = me_ref[0]
    devices = len(table)
    share = wo_ref.shape[0] // devices
    per = ow_refs[0].shape[0] // share
    gain = slice(xn_ref.shape[1], gains_ref.shape[1])
    inner = sc_ref.shape[1]
    width = cot_ref.shape[1]
    rows_in = xn_ref.shape[1] // devices
    xn = xn_ref[...]
    wg_ref[...] = rows_of(gw_refs)
    g_ref[...] = mm(xn, wg_ref[...])
    if share % 16:
        wo_ref[...] = rows_of(ow_refs)
    else:
        for p in range(devices):
            at = pl.multiple_of((me ^ int(table[p])) * share, 16)
            row = (p % per) * share
            wo_ref[pl.ds(at, share), :] = ow_refs[p // per][row : row + share, :]
    dm_ref[...] = mm_nt(cot_ref[...], wo_ref[...])
    length = xn_ref.shape[0]
    sub = 32
    ginner_ref[...] = jnp.zeros_like(ginner_ref)

    def body(k, carry):
        rows = pl.ds(pl.multiple_of(k * sub, sub), sub)
        gate = g_ref[rows, :]
        sig = sigmoid(gate)
        silu = gate * sig
        scanned = sc_ref[rows, :]
        gated = scanned * silu
        scale = lax.rsqrt(jnp.mean(gated * gated, axis=-1, keepdims=True) + 1e-05)
        dm = dm_ref[rows, :]
        unit = gated * scale
        mixed_ref[rows, :] = (unit * gains_ref[:, gain]).astype(BF16)
        ginner_ref[...] += jnp.sum((dm * unit).reshape(sub // 8, 8, -1), axis=0)
        dunit = dm * gains_ref[:, gain]
        dot = jnp.mean(unit * dunit, axis=-1, keepdims=True)
        du = scale * (dunit - unit * dot)
        g_ref[rows, :] = du * silu
        dgate_ref[rows, :] = (du * scanned * (sig * (1.0 + gate * (1.0 - sig)))).astype(BF16)
        return carry

    lax.fori_loop(0, length // sub, body, 0)
    if rows_in % 8:
        lo_ref[...] = mm_tn(xn, dgate_ref[...]).astype(BF16)
        hi_ref[...] = mm_tn(mixed_ref[...], cot_ref[...]).astype(BF16)
        return
    gg = mm_tn(xn, dgate_ref[...]).astype(BF16)
    half = gg.shape[0] // 2
    lo_ref[:, :inner] = gg[:half]
    hi_ref[:, :inner] = gg[half:]
    nat_ref[...] = mm_tn(mixed_ref[...], cot_ref[...])
    for p in range(0, devices, 2):
        target = lo_ref if p < devices // 2 else hi_ref
        row = (p % (devices // 2)) * rows_in
        for k in range(2):
            both = [
                nat_ref[pl.ds(pl.multiple_of((me ^ int(table[q])) * share + k * rows_in, 8), rows_in), :]
                for q in (p, p + 1)
            ]
            lanes = slice(inner + k * width, inner + (k + 1) * width)
            target[row : row + 2 * rows_in, lanes] = jnp.concatenate(both, axis=0).astype(BF16)


def branch_kernel(mixed_ref, wo_ref, hid_ref, dgate_ref, wg_ref, out_ref, dn_ref):
    out_ref[...] = (hid_ref[...].astype(F32) + mm(mixed_ref[...], wo_ref[...])).astype(BF16)
    dn_ref[...] = mm_nt(dgate_ref[...], wg_ref[...])


def conv_back(dpre, x, taps_ref, lanes, mask_ref, dtaps_ref, dp_ref, to):
    kernel = mask_ref.shape[0] + 1
    length = dpre.shape[0]

    def total(z):
        return jnp.sum(z, axis=0, keepdims=True)

    dtaps_ref[kernel : kernel + 1, to] = total(dpre)
    dtaps_ref[kernel - 1 : kernel, to] = total(dpre * x)
    dx = taps_ref[kernel - 1 : kernel, lanes] * dpre
    for j in range(1, kernel):
        masked = dpre * mask_ref[j - 1]
        tap = slice(kernel - 1 - j, kernel - j)
        dtaps_ref[tap, to] = total(masked * pltpu.roll(x, j, axis=0))
        dx = dx + taps_ref[tap, lanes] * pltpu.roll(masked, length - j, axis=0)
    dp_ref[:, to] = dx.astype(BF16)


def silu_and_slope(pre):
    sig = sigmoid(pre)
    return pre * sig, sig * (1.0 + pre * (1.0 - sig))


def scan_bwd_kernel(
    g_ref, yd_ref, v_ref, slope_ref, ci_ref, dt_ref, taps_ref, segr_ref, alog_ref, skip_ref, bias_ref,
    dp_ref, dtaps_ref, dskip_ref, dheads_ref,
    heads_ref, step_ref, cc_ref, wide_ref, cct_ref, segb_ref, mask_ref,
    sdt_ref, so_ref, sot_ref, dsdt_ref, dso_ref, acc_ref, dpre_ref,
):
    length = ci_ref.shape[0]
    segr = segr_ref[...].astype(F32)
    blocks = length // BLK
    channels = ci_ref.shape[1]
    states = BLK
    inner = channels - 2 * states
    nheads = inner // (BLK // 2)
    lanes_b = slice(inner, inner + states)
    lanes_c = slice(inner + states, channels)

    head_setup(
        dt_ref[...], (alog_ref, skip_ref, bias_ref), segr, heads_ref, step_ref, cc_ref, wide_ref, cct_ref, segb_ref
    )
    mask_setup(segb_ref, mask_ref)
    dheads_ref[...] = jnp.zeros_like(dheads_ref)
    dtaps_ref[...] = jnp.zeros_like(dtaps_ref)
    _, pre_b = conv_parts(ci_ref[:, lanes_b], taps_ref, lanes_b, mask_ref)
    _, pre_c = conv_parts(ci_ref[:, lanes_c], taps_ref, lanes_c, mask_ref)
    score_setup(
        pre_b * sigmoid(pre_b), pre_c * sigmoid(pre_c),
        segb_ref, segr, None, so_ref, sdt_ref, sot_ref,
    )
    dsdt_ref[...] = jnp.zeros_like(dsdt_ref)
    dso_ref[...] = jnp.zeros_like(dso_ref)
    acc_ref[...] = jnp.zeros_like(acc_ref)

    def body(t, carry):
        lanes = pl.ds(pl.multiple_of(t * BLK, BLK), BLK)
        x = ci_ref[:, lanes]
        v = v_ref[:, lanes]
        low = iota((1, BLK), 1) < BLK // 2
        (st2, wq2, al2, ew2), c2, r2, skip = pair_setup(t, heads_ref, wide_ref, cc_ref, cct_ref, 4)
        vtb = (v * st2).astype(BF16)
        vpb = (v * wq2).astype(BF16)
        g = g_ref[:, lanes]
        gb = g.astype(BF16)
        gpb = (al2 * g).astype(BF16)
        dskip_ref[:, lanes] = jnp.sum(g * v, axis=0, keepdims=True)
        k_row = iota((3 * BLK, BLK), 0)
        target = jnp.where(k_row >= 2 * BLK, BLK // 2, 0) + 2 * t
        target = target + jnp.where((k_row & (BLK - 1)) >= BLK // 2, 1, 0)
        collect = (iota((3 * BLK, BLK), 1) == target).astype(F32).astype(BF16)
        for i in range(blocks):
            rows = slice(i * BLK, (i + 1) * BLK)
            before = slice((i - 1) * BLK, i * BLK)
            after = slice((i + 1) * BLK, (i + 2) * BLK)
            gdiag = block_diag(gb[rows], low)
            both = mm_nt(vtb[rows], gdiag)
            ms = []
            part = jnp.zeros((BLK, BLK), F32)
            for k in range(2):
                row = r2[k : k + 1, rows]
                d = jnp.exp2(jnp.minimum(row - c2[rows, k * BLK : (k + 1) * BLK], 0.0))
                ms.append((sdt_ref[i] * d).astype(BF16))
                part = part + both[:, k * BLK : (k + 1) * BLK] * d
            dsdt_ref[i] += part
            dvt = mm(jnp.concatenate(ms, axis=1), gdiag)
            x1 = gb[rows].astype(F32) * yd_ref[rows, lanes] - dvt * vtb[rows].astype(F32)
            dv = st2[rows] * dvt + skip * g[rows]
            dstep = dvt
            if i > 0:
                z = mm(so_ref[i], vpb[before])
                x1 = x1 + gpb[rows].astype(F32) * z
                dso_ref[i] += mm_nt(gpb[rows], vpb[before])
            if i + 1 < blocks:
                dvp = mm(sot_ref[i + 1], gpb[after])
                x1 = x1 - dvp * vpb[rows].astype(F32)
                dv = dv + wq2[rows] * dvp
                dstep = dstep + ew2[rows] * dvp
            h1, l1 = split2(x1)
            h2 = (dstep * v[rows]).astype(BF16)
            acc_ref[rows, :] += mm(jnp.concatenate([h1, l1, h2], axis=1), collect)
            dpre_ref[rows, :] = dv * slope_ref[rows, lanes]
        conv_back(dpre_ref[...], x, taps_ref, lanes, mask_ref, dtaps_ref, dp_ref, lanes)
        return carry

    lax.fori_loop(0, inner // BLK, body, 0)
    xb, xc = ci_ref[:, lanes_b], ci_ref[:, lanes_c]
    _, pre_b = conv_parts(xb, taps_ref, lanes_b, mask_ref)
    _, pre_c = conv_parts(xc, taps_ref, lanes_c, mask_ref)
    bmat, slope_b = silu_and_slope(pre_b)
    cmat, slope_c = silu_and_slope(pre_c)
    bb, cb = bmat.astype(BF16), cmat.astype(BF16)
    causal_t = iota((BLK, BLK), 1) >= iota((BLK, BLK), 0)
    upper = causal_t.astype(F32)
    dst, dso = [], [None]
    for i in range(blocks):
        rows = slice(i * BLK, (i + 1) * BLK)
        before = slice((i - 1) * BLK, i * BLK)
        same = (segb_ref[rows, :] == segr[:, rows]) & causal_t
        dst.append(jnp.where(same, dsdt_ref[i], 0.0))
        if i > 0:
            linked = segb_ref[rows, :] == segr[:, before]
            dso.append(jnp.where(linked, dso_ref[i], 0.0))
    for i in range(blocks):
        rows = slice(i * BLK, (i + 1) * BLK)
        before = slice((i - 1) * BLK, i * BLK)
        after = slice((i + 1) * BLK, (i + 2) * BLK)
        dc = mm(dst[i].T.astype(BF16), bb[rows])
        if i > 0:
            dc = dc + mm(dso[i].astype(BF16), bb[before])
        dpre_ref[rows, :] = dc * slope_c[rows]
    conv_back(dpre_ref[...], xc, taps_ref, lanes_c, mask_ref, dtaps_ref, dp_ref, lanes_c)
    for i in range(blocks):
        rows = slice(i * BLK, (i + 1) * BLK)
        after = slice((i + 1) * BLK, (i + 2) * BLK)
        db = mm(dst[i].astype(BF16), cb[rows])
        if i + 1 < blocks:
            db = db + mm(dso[i + 1].T.astype(BF16), cb[after])
        dpre_ref[rows, :] = db * slope_b[rows]
    conv_back(dpre_ref[...], xb, taps_ref, lanes_b, mask_ref, dtaps_ref, dp_ref, lanes_b)

    decay = jnp.exp(heads_ref[0:1, :])
    later = jnp.zeros((1, BLK), F32)
    dalog = jnp.zeros((1, BLK), F32)
    dbias = jnp.zeros((1, BLK), F32)
    for i in reversed(range(blocks)):
        rows = slice(i * BLK, (i + 1) * BLK)
        dcum = acc_ref[rows, :]
        drate = later + jnp.dot(upper, dcum, precision=HIGH, preferred_element_type=F32)
        later = drate[0:1, :]
        step = step_ref[rows, :]
        dalog = dalog - jnp.sum(drate * step, axis=0, keepdims=True) * decay
        dstep = pltpu.roll(dcum, BLK // 2, axis=1) - drate * decay
        ddt = dstep * sigmoid(dt_ref[rows, :] + heads_ref[2:3, :])
        dbias = dbias + jnp.sum(ddt, axis=0, keepdims=True)
        dp_ref[rows, channels:] = jnp.where(iota((1, BLK), 1) < nheads, ddt, 0.0).astype(BF16)
    dheads_ref[0:1, :] = dalog
    dheads_ref[1:2, :] = dbias


def grad_in_kernel(xn_ref, dp_ref, lo_ref, hi_ref):
    grad = mm_tn(xn_ref[...], dp_ref[...]).astype(BF16)
    half = grad.shape[0] // 2
    lo_ref[...] = grad[:half]
    hi_ref[...] = grad[half:]


def input_kernel(
    wc_ref, dng_ref, dp_ref, me_ref, tab_ref, hid_ref, cot_ref, gains_ref,
    dtaps_ref, ginner_ref, dskip_ref, dheads_ref,
    ig_ref, sums_ref,
):
    dn = mm_nt(dp_ref[...], wc_ref[...]) + dng_ref[...]
    perm = perm_matrix(me_ref[0], tab_ref, dn.shape[1])
    hi, lo = split2(dn)
    dn = mm_nt(hi, perm) + mm_nt(lo, perm)
    tokens = hid_ref[...].astype(F32)
    scale = lax.rsqrt(jnp.mean(tokens * tokens, axis=-1, keepdims=True) + 1e-05)
    unit = tokens * scale
    width = tokens.shape[1]
    sums_ref[...] = jnp.zeros_like(sums_ref)
    sums_ref[0:5, : dtaps_ref.shape[1]] = dtaps_ref[0:5, :]
    sums_ref[5:6, :width] = jnp.sum(dn * unit, axis=0, keepdims=True)
    sums_ref[5:6, width:] = jnp.sum(ginner_ref[...], axis=0, keepdims=True)
    sums_ref[6:7, : dskip_ref.shape[1]] = dskip_ref[...]
    sums_ref[7:8, :BLK] = dheads_ref[0:1, :]
    sums_ref[7:8, BLK : 2 * BLK] = dheads_ref[1:2, :]
    dunit = dn * gains_ref[:, :width]
    inner = jnp.mean(unit * dunit, axis=-1, keepdims=True)
    ig_ref[...] = cot_ref[...].astype(F32) + scale * (dunit - unit * inner)


def stack_kernel(*refs):
    rows = jnp.concatenate([ref[...].astype(F32) for ref in refs[:-1]], axis=0)
    refs[-1][...] = rows.astype(BF16)


def fold_kernel(count, *refs):
    total = refs[0][...].astype(F32)
    for ref in refs[1:count]:
        total = total + ref[...].astype(F32)
    size = total.shape[0] // len(refs[count:])
    for k, ref in enumerate(refs[count:]):
        ref[...] = total[k * size : (k + 1) * size].astype(ref.dtype)


def last_out_kernel(a_ref, b_ref, c_ref, d_ref, gate_ref, out_ref):
    total = a_ref[...].astype(F32) + b_ref[...].astype(F32) + c_ref[...].astype(F32) + d_ref[...].astype(F32)
    inner = gate_ref.shape[1]
    rows, width = a_ref.shape[0], out_ref.shape[1]
    gate_ref[...] = total[:, :inner]
    out_ref[:rows, :] = total[:, inner : inner + width]
    out_ref[rows:, :] = total[:, inner + width :]


def last_in_kernel(a_ref, b_ref, c_ref, d_ref, gate_ref, in_ref):
    total = a_ref[...].astype(F32) + b_ref[...].astype(F32) + c_ref[...].astype(F32) + d_ref[...].astype(F32)
    inner = gate_ref.shape[1]
    in_ref[:, :inner] = gate_ref[...]
    in_ref[:, inner:] = total[:, : in_ref.shape[1] - inner]


def sds(shape, dtype):
    return jax.ShapeDtypeStruct(shape, dtype)


def held(shape, dtype):
    return pltpu.VMEM(shape, dtype)


def scan_scratch(length, inner, taps):
    nheads = -(-2 * inner // (8 * BLK)) * 8
    return [
        pltpu.VMEM((8, BLK), F32), pltpu.VMEM((length, BLK), F32), pltpu.VMEM((length, 3 * BLK), BF16),
        pltpu.VMEM((4, length, 2 * BLK), BF16), pltpu.VMEM((nheads, length), F32), pltpu.VMEM((length, BLK), F32),
        pltpu.VMEM((taps - 1, length, BLK), F32),
    ]


def scan_fwd(weights, packed, taps_n, widths, mine, tab, hidden, first, second, segr, *heads):
    length, width = hidden.shape
    channels, inner = widths
    blocks = length // BLK
    count = len(weights)
    rows = held((length, inner), F32)
    return call(
        lambda *refs: scan_fwd_kernel(count, packed, *refs),
        (
            held((length, width), BF16), held((8, channels), F32), held((1, width + inner), F32),
            held((width, channels + BLK), BF16),
            held((length, channels), F32), held((length, BLK), F32), rows, rows, rows, rows,
        ),
        *weights, mine, tab, hidden, first, second, segr, *heads, scalar=count,
        leave=(tab, first, second, segr) + heads,
        scratch=scan_scratch(length, inner, taps_n - 1) + [
            pltpu.VMEM((blocks, BLK, BLK), F32),
            pltpu.VMEM((blocks, BLK, BLK), BF16),
        ],
    )


def scan_bwd(taps_n, g, yd, v, slope, ci, dt, taps, segr, *heads):
    length, channels = ci.shape
    inner = g.shape[1]
    score = (length // BLK, BLK, BLK)
    return call(
        scan_bwd_kernel,
        (
            held((length, channels + BLK), BF16), held(taps.shape, F32), held((1, inner), F32),
            held((8, BLK), F32),
        ),
        g, yd, v, slope, ci, dt, taps, segr, *heads, leave=(segr,) + heads,
        scratch=scan_scratch(length, inner, taps_n - 1) + [
            pltpu.VMEM(score, F32),
            pltpu.VMEM(score, BF16),
            pltpu.VMEM(score, BF16),
            pltpu.VMEM(score, F32),
            pltpu.VMEM(score, F32),
            pltpu.VMEM((length, BLK), F32),
            pltpu.VMEM((length, BLK), F32),
        ],
    )


def call(kernel, outs, *ins, scratch=(), scalar=None, leave=()):
    specs = [
        pl.BlockSpec(memory_space=pltpu.SMEM if k == scalar else pltpu.VMEM) for k in range(len(ins))
    ]
    near = [
        a if k == scalar else pltpu.with_memory_space_constraint(a, pltpu.HBM if any(a is b for b in leave) else pltpu.VMEM)
        for k, a in enumerate(ins)
    ]
    many = isinstance(outs, (tuple, list))
    out_specs = [pl.BlockSpec(memory_space=pltpu.VMEM) for _ in outs] if many else pl.BlockSpec(memory_space=pltpu.VMEM)
    return pl.pallas_call(
        kernel, out_shape=outs, in_specs=specs, out_specs=out_specs, scratch_shapes=list(scratch),
        compiler_params=pltpu.CompilerParams(vmem_limit_bytes=(20 if scratch else 8) * 1024 * 1024),
    )(*near)


def stages(devices):
    masks = [1 << b for b in range(devices.bit_length() - 1)]
    groups = []
    for end in range(len(masks), 1, -2):
        part = masks[max(end - 2, 1) : end]
        groups.append(part if len(part) == 1 else [part[0], part[1], part[0] | part[1]])
    return groups + [masks[:1]]


def order_table(devices):
    table = np.zeros((1,), np.int32)
    for group in stages(devices):
        table = np.concatenate([table] + [table ^ m for m in group])
    return table


def send(x, devices, mask):
    return lax.ppermute(x, "fsdp", [(i, i ^ mask) for i in range(devices)])


def send_all(parts, devices, stage):
    return [send(part, devices, m) for part, m in zip(parts, stages(devices)[stage])]


def stack(pieces):
    size, rest = pieces[0].shape[0], pieces[0].shape[1:]
    if size % 8 or len(rest) != 1:
        return jnp.concatenate(pieces, axis=0)
    return call(stack_kernel, held((len(pieces) * size,) + rest, BF16), *pieces)


def gather(x, devices):
    groups = stages(devices)
    core = len(groups) - 1
    pieces = [x]
    for stage in range(core):
        x = pieces[0] if len(pieces) == 1 else stack(pieces)
        pieces = [x] + send_all([x] * len(groups[stage]), devices, stage)
    return pieces + [send(a, devices, 1) for a in pieces]


def fold(parts, fan, dtype):
    rows, cols = parts[0].shape
    size = rows // fan
    if size % 8:
        total = sum(part.astype(F32) for part in parts).astype(dtype)
        return [total[k * size : (k + 1) * size] for k in range(fan)]
    count = len(parts)
    return call(lambda *refs: fold_kernel(count, *refs), tuple(held((size, cols), dtype) for _ in range(fan)), *parts)


def reduce_shares(lo, hi, devices):
    groups = stages(devices)
    parts = [lo, hi]
    for stage in reversed(range(len(groups))):
        parts = [parts[0]] + send_all(parts[1:], devices, stage)
        if stage:
            parts = fold(parts, len(groups[stage - 1]) + 1, BF16)
    return parts


def total_of(x, devices):
    for stage in reversed(range(len(stages(devices)))):
        group = stages(devices)[stage]
        got = send_all([x] * len(group), devices, stage)
        x = x + got[0] if len(got) == 1 else (x + got[0]) + (got[1] + got[2])
    return x


def layer(
    hidden, segment_ids, cot, w_in, w_out, conv_taps, gains, a_log, d_skip, dt_bias
):
    length = segment_ids.shape[1]
    width = hidden.shape[1]
    devices = lax.axis_size("fsdp")
    me = lax.axis_index("fsdp")
    nheads = a_log.shape[0]
    taps_n, tap_share = conv_taps.shape
    channels = tap_share * devices
    gain_share = gains.shape[0]
    inner = w_out.shape[0] * devices
    proj = w_in.shape[1]
    rows_in, rows_out = w_in.shape[0], w_out.shape[0]
    pairs = inner // BLK
    first = pairs // 2

    table = order_table(devices)
    inverse = np.argsort(table).astype(np.int32)
    order = jnp.asarray(table) ^ me
    place = jnp.asarray(inverse)[me ^ jnp.arange(devices)]
    mine = me.reshape(1).astype(jnp.int32)
    tab = np.zeros((8, width), np.int32)
    tab[0], tab[1], tab[2] = np.repeat(table, rows_in), np.tile(np.arange(rows_in), devices), rows_in
    tab = jnp.asarray(tab)

    spare = BLK - (proj - inner - channels)
    packed = rows_in > taps_n and max(tap_share, gain_share) <= spare
    if packed:
        gain_row = gains.reshape(1, gain_share)
        w_conv, w_gate = call(
            lambda *refs: pack_kernel(inner, *refs),
            (held((rows_in, channels + BLK), BF16), held((rows_in, inner), BF16)),
            w_in, conv_taps, gain_row, leave=(w_in, conv_taps, gain_row),
        )
    else:
        w_conv = jnp.pad(w_in[:, inner:], ((0, 0), (0, spare)))
        w_gate = w_in[:, :inner]
    cw = gather(w_conv, devices)
    gw = gather(w_gate, devices)
    ow = gather(w_out, devices)
    count = len(cw)

    heads = [x.reshape(1, nheads) for x in (a_log, d_skip, dt_bias)]

    if packed:
        at = np.arange(width + inner)
        where = np.stack([at % tap_share, at // tap_share, at % gain_share, at // gain_share])
        second = jnp.asarray(np.pad(where, ((0, 4), (0, 0))).astype(np.int32))
        first = jnp.asarray(table.reshape(devices, 1))
    else:
        small = jnp.zeros((8, BLK), F32)
        small = small.at[:taps_n, :tap_share].set(conv_taps.astype(F32))
        small = small.at[taps_n, :gain_share].set(gains.astype(F32))
        rows = jnp.concatenate(gather(small[None], devices), axis=0)[place]
        first = jnp.moveaxis(rows[:, :, :tap_share], 0, 1).reshape(8, channels)
        second = rows[:, taps_n, :gain_share].reshape(1, width + inner)
    xn, taps, gains_all, wc, ci, dt, sc, yd, v, slope = scan_fwd(
        cw, (proj - inner - channels, taps_n) if packed else None, taps_n, (channels, inner),
        mine, tab, hidden, first, second, segment_ids, *heads,
    )
    if rows_out % 16:
        wo_all = jnp.concatenate(ow, axis=0).reshape(devices, rows_out, width)[place].reshape(inner, width)
        ow = [wo_all[k * (inner // count) : (k + 1) * (inner // count)] for k in range(count)]
    aligned = rows_in % 8 == 0
    if aligned:
        halves = (held((width // 2, inner + 2 * width), BF16), held((width // 2, inner + 2 * width), BF16))
    else:
        halves = (sds((width, inner), BF16), sds((inner, width), BF16))
    lo, hi, g, dgate, mixed, ginner, wo, wg = call(
        lambda *refs: mid_kernel(count, table, *refs),
        halves + (
            held((length, inner), F32), held((length, inner), BF16), held((length, inner), BF16),
            held((8, inner), F32), held((inner, width), BF16), held((width, inner), BF16),
        ),
        *gw, *ow, mine, xn, sc, gains_all, cot,
        scratch=(
            pltpu.VMEM((length, inner), F32), pltpu.VMEM((inner, width), F32),
        ),
        scalar=2 * count,
    )
    if not aligned:
        gwo = hi.reshape(devices, 2, rows_in, width)[order]
        both = jnp.concatenate([lo, gwo[:, 0].reshape(width, width), gwo[:, 1].reshape(width, width)], axis=1)
        lo, hi = both[: width // 2], both[width // 2 :]
    mid_parts = reduce_shares(lo, hi, devices)
    output, dng = call(
        branch_kernel, (sds((length, width), BF16), held((length, width), F32)),
        mixed, wo, hidden, dgate, wg,
    )
    dp, dtaps, dskip, dheads = scan_bwd(taps_n, g, yd, v, slope, ci, dt, taps, segment_ids, *heads)
    half = held((width // 2, dp.shape[1]), BF16)
    clo, chi = call(grad_in_kernel, (half, half), xn, dp)
    conv_parts_in = reduce_shares(clo, chi, devices)
    input_grad, sums = call(
        input_kernel,
        (sds((length, width), F32), held((8, width + inner), F32)),
        wc, dng, dp, mine, tab, hidden, cot, gains_all, dtaps, ginner, dskip, dheads, scalar=3, leave=(tab,),
    )
    if aligned and len(mid_parts) == 4:
        gate_share, out_share = call(
            last_out_kernel,
            (sds((rows_in, inner), F32), sds((rows_out, width), F32)), *mid_parts,
        )
        in_share = call(last_in_kernel, sds((rows_in, proj), F32), *conv_parts_in, gate_share)
    else:
        total = sum(part.astype(F32) for part in mid_parts)
        out_share = jnp.concatenate([total[:, inner : inner + width], total[:, inner + width :]], axis=0)
        conv_total = sum(part.astype(F32) for part in conv_parts_in)
        in_share = jnp.concatenate([total[:, :inner], conv_total], axis=1)[:, :proj]

    sums = total_of(sums, devices)
    taps_share = lax.dynamic_slice_in_dim(sums[:taps_n, :channels], me * tap_share, tap_share, axis=1)
    gains_share = lax.dynamic_slice_in_dim(sums[5], me * gain_share, gain_share)
    return (
        output, input_grad, in_share, out_share, taps_share, gains_share,
        sums[7, :nheads], sums[6, :inner].reshape(nheads, -1).sum(axis=1), sums[7, BLK : BLK + nheads],
    )


def solution(mesh):
    axis = P("fsdp")
    rows = P("fsdp", None)
    cols = P(None, "fsdp")
    return jax.shard_map(
        layer,
        mesh=mesh,
        in_specs=(rows, rows, rows, rows, rows, cols, axis, P(), P(), P()),
        out_specs=(rows, rows, rows, rows, cols, axis, P(), P(), P()),
        check_vma=False,
    )
```

```python
import jax
import jax.numpy as jnp
import numpy as np
from jax import lax
from jax.experimental import pallas as pl
from jax.experimental.pallas import tpu as pltpu
from jax.sharding import PartitionSpec as P


BLK = 128
LOG2E = 1.4426950408889634
F32 = jnp.float32
BF16 = jnp.bfloat16
HIGH = lax.Precision.HIGHEST


def mm(a, b):
    return lax.dot_general(a, b, (((1,), (0,)), ((), ())), preferred_element_type=F32)


def mm_nt(a, b):
    return lax.dot_general(a, b, (((1,), (1,)), ((), ())), preferred_element_type=F32)


def mm_tn(a, b):
    return lax.dot_general(a, b, (((0,), (0,)), ((), ())), preferred_element_type=F32)


def split2(x):
    hi = x.astype(BF16)
    return hi, (x - hi.astype(F32)).astype(BF16)


def iota(shape, dim):
    return lax.broadcasted_iota(jnp.int32, shape, dim)


def perm_matrix(me, tab_ref, width):
    dvec = (tab_ref[0:1, :] ^ me) * tab_ref[2:3, 0:1] + tab_ref[1:2, :]
    return (iota((width, width), 0) == dvec).astype(F32).astype(BF16)


def rows_of(refs, lanes=slice(None)):
    return jnp.concatenate([ref[:, lanes] for ref in refs], axis=0)


def normed_of(hid_ref, gain, me, tab_ref, xn_ref):
    tokens = hid_ref[...].astype(F32)
    scale = lax.rsqrt(jnp.mean(tokens * tokens, axis=-1, keepdims=True) + 1e-05)
    normed = (tokens * scale * gain).astype(BF16)
    perm = perm_matrix(me, tab_ref, tokens.shape[1])
    xn_ref[...] = mm(normed, perm).astype(BF16)


def pack_kernel(inner, w_ref, taps_in, gains_in, conv_ref, gate_ref):
    gate_ref[...] = w_ref[:, :inner]
    body = conv_ref.shape[1] - BLK
    conv_ref[:, :body] = w_ref[:, inner : inner + body]
    tail = w_ref[:, inner + body :]
    spare = tail.shape[1]
    rows, taps_n = w_ref.shape[0], taps_in.shape[0]

    def onto(x, at):
        return mm(x, (iota((x.shape[1], BLK), 1) == iota((x.shape[1], BLK), 0) + at).astype(F32).astype(BF16))

    row = iota((rows, BLK), 0)
    tile_of = onto(tail, 0)
    taps_wide, gains_wide = onto(taps_in[...], spare), onto(gains_in[...], spare)
    for j in range(taps_n):
        tile_of = tile_of + jnp.where(row == j, taps_wide[j : j + 1, :], 0.0)
    tile_of = tile_of + jnp.where(row == taps_n, gains_wide, 0.0)
    conv_ref[:, body:] = tile_of.astype(BF16)


def unpack(at, taps_n, pieces, me, owner_ref, where_ref, taps_ref, gains_ref):
    last = pieces[0].shape[1] - BLK
    tail = rows_of(pieces, slice(last, last + BLK))
    devices = owner_ref.shape[0]
    rows_in = tail.shape[0] // devices
    row = iota((8 * devices, tail.shape[0]), 0)
    bits = devices.bit_length() - 1
    source = (row & (devices - 1)) * rows_in + lax.shift_right_logical(row, bits)
    pick = (iota(row.shape, 1) == source).astype(F32).astype(BF16)
    small = mm(pick, tail).astype(BF16)

    def spread(part, line, width):
        lane, owner = where_ref[line : line + 1, :width], where_ref[line + 1 : line + 2, :width]
        chosen = (iota((BLK, width), 0) == lane + at).astype(F32).astype(BF16)
        wide = mm(part, chosen)
        return jnp.sum(jnp.where((owner_ref[...] ^ me) == owner, wide, 0.0), axis=0, keepdims=True)

    channels, width = taps_ref.shape[1], gains_ref.shape[1]
    taps_ref[...] = jnp.zeros_like(taps_ref)
    for j in range(taps_n):
        taps_ref[j : j + 1, :] = spread(small[j * devices : (j + 1) * devices], 0, channels)
    gains_ref[...] = spread(small[taps_n * devices : (taps_n + 1) * devices], 2, width)


def head_setup(dt_raw, rows_in, segr, heads_ref, step_ref, cc_ref, wide_ref, cct_ref, segb_ref):
    length = dt_raw.shape[0]
    heads_ref[...] = jnp.zeros_like(heads_ref)
    for k, ref in enumerate(rows_in):
        heads_ref[k : k + 1, : ref.shape[1]] = ref[...]
    segb_ref[...] = jnp.broadcast_to(segr, (BLK, length)).T
    biased = dt_raw + heads_ref[2:3, :]
    step = jnp.maximum(biased, 0.0) + jnp.log1p(jnp.exp(-jnp.abs(biased)))
    step_ref[...] = step
    rate = step * (jnp.exp(heads_ref[0:1, :]) * (-LOG2E))
    lower = (iota((BLK, BLK), 0) >= iota((BLK, BLK), 1)).astype(F32)
    for i in range(length // BLK):
        rows = slice(i * BLK, (i + 1) * BLK)
        cc = jnp.dot(lower, rate[rows], precision=HIGH, preferred_element_type=F32)
        cc_ref[rows, :] = cc
        ew = jnp.exp2(jnp.minimum(cc[BLK - 1 : BLK, :] - cc, 0.0))
        for k, x in enumerate((step[rows], ew, jnp.exp2(cc))):
            wide_ref[k, rows, :] = jnp.concatenate(split2(x), axis=1)
        cct_ref[:, rows] = cc.T[: cct_ref.shape[0]]


def mask_setup(segb_ref, mask_ref):
    segb = segb_ref[...]
    pos = iota(segb.shape, 0)
    for j in range(1, mask_ref.shape[0] + 1):
        prev = pltpu.roll(segb, j, axis=0)
        mask_ref[j - 1] = ((prev == segb) & (pos >= j)).astype(F32)


def conv_parts(x, taps_ref, lanes, mask_ref):
    kernel = mask_ref.shape[0] + 1
    shifts = [x] + [pltpu.roll(x, j, axis=0) * mask_ref[j - 1] for j in range(1, kernel)]
    pre = taps_ref[kernel : kernel + 1, lanes] + taps_ref[kernel - 1 : kernel, lanes] * x
    for j in range(1, kernel):
        pre = pre + taps_ref[kernel - 1 - j : kernel - j, lanes] * shifts[j]
    return shifts, pre


def sigmoid(x):
    return 0.5 * jnp.tanh(0.5 * x) + 0.5


def score_setup(bmat, cmat, segb_ref, segr, sd_ref, so_ref, sdt_ref, sot_ref):
    length = bmat.shape[0]
    bb, cb = bmat.astype(BF16), cmat.astype(BF16)
    causal = iota((BLK, BLK), 0) >= iota((BLK, BLK), 1)
    for i in range(length // BLK):
        rows = slice(i * BLK, (i + 1) * BLK)
        before = slice((i - 1) * BLK, i * BLK)
        same = (segb_ref[rows, :] == segr[:, rows]) & causal
        diag = jnp.where(same, mm_nt(cb[rows], bb[rows]), 0.0)
        if sd_ref is not None:
            sd_ref[i] = diag
        if sdt_ref is not None:
            sdt_ref[i] = diag.T
        if i > 0:
            linked = segb_ref[rows, :] == segr[:, before]
            off = jnp.where(linked, mm_nt(cb[rows], bb[before]), 0.0)
            so_ref[i] = off.astype(BF16)
            if sot_ref is not None:
                sot_ref[i] = off.T.astype(BF16)


def pair_setup(t, heads_ref, wide_ref, cc_ref, cct_ref):
    head = iota((2 * BLK, BLK), 0) & (BLK - 1)
    pick = (head == 2 * t + jnp.where(iota((2 * BLK, BLK), 1) < BLK // 2, 0, 1)).astype(F32).astype(BF16)
    st2, ew2, al2 = [mm(wide_ref[k], pick) for k in range(3)]
    c2 = pltpu.roll(cc_ref[...], lax.rem(BLK - 2 * t, BLK), axis=1)
    r2 = pltpu.roll(cct_ref[...], lax.rem(cct_ref.shape[0] - 2 * t, cct_ref.shape[0]), axis=0)
    h2 = pltpu.roll(heads_ref[...], lax.rem(BLK - 2 * t, BLK), axis=1)
    skip = jnp.where(iota((1, BLK), 1) < BLK // 2, h2[1:2, 0:1], h2[1:2, 1:2])
    return st2, ew2, ew2 * st2, al2, c2, r2, skip


def block_diag(x, low):
    zero = jnp.zeros_like(x)
    return jnp.concatenate([jnp.where(low, x, zero), jnp.where(low, zero, x)], axis=0)


def scan_fwd_kernel(pieces, packed, *refs):
    w_refs = refs[:pieces]
    (
        me_ref, tab_ref, hid_ref, first_ref, second_ref, segr_ref, alog_ref, skip_ref, bias_ref,
        xn_ref, taps_ref, gains_ref, wc_ref, ci_ref, dt_ref, sc_ref, yd_ref, v_ref, slope_ref,
        heads_ref, step_ref, cc_ref, wide_ref, cct_ref, segb_ref, mask_ref, sd_ref, so_ref,
    ) = refs[pieces:]
    me = me_ref[0]
    segr = segr_ref[...].astype(F32)
    length = xn_ref.shape[0]
    channels = ci_ref.shape[1]
    states = BLK
    inner = channels - 2 * states
    if packed:
        unpack(packed[0], packed[1], w_refs, me, first_ref, second_ref, taps_ref, gains_ref)
    else:
        taps_ref[...] = first_ref[...]
        gains_ref[...] = second_ref[...]
    normed_of(hid_ref, gains_ref[:, : hid_ref.shape[1]], me, tab_ref, xn_ref)
    xn = xn_ref[...]
    wc_ref[...] = rows_of(w_refs)
    ci_ref[...] = mm(xn, wc_ref[:, :channels])
    dt_ref[...] = mm(xn, wc_ref[:, channels:])
    head_setup(
        dt_ref[...], (alog_ref, skip_ref, bias_ref), segr, heads_ref, step_ref, cc_ref, wide_ref, cct_ref, segb_ref
    )
    mask_setup(segb_ref, mask_ref)
    lanes_b = slice(inner, inner + states)
    lanes_c = slice(inner + states, channels)
    _, pre_b = conv_parts(ci_ref[:, lanes_b], taps_ref, lanes_b, mask_ref)
    _, pre_c = conv_parts(ci_ref[:, lanes_c], taps_ref, lanes_c, mask_ref)
    score_setup(
        pre_b * sigmoid(pre_b), pre_c * sigmoid(pre_c),
        segb_ref, segr, sd_ref, so_ref, None, None,
    )

    def body(t, carry):
        lanes = pl.ds(pl.multiple_of(t * BLK, BLK), BLK)
        _, pre = conv_parts(ci_ref[:, lanes], taps_ref, lanes, mask_ref)
        v, slope = silu_and_slope(pre)
        v_ref[:, lanes] = v
        slope_ref[:, lanes] = slope
        low = iota((1, BLK), 1) < BLK // 2
        st2, _, wq2, al2, c2, r2, skip = pair_setup(t, heads_ref, wide_ref, cc_ref, cct_ref)
        vt = (v * st2).astype(BF16)
        vp = (v * wq2).astype(BF16)
        for i in range(length // BLK):
            rows = slice(i * BLK, (i + 1) * BLK)
            before = slice((i - 1) * BLK, i * BLK)
            ms = []
            for k in range(2):
                row = r2[k : k + 1, rows]
                d = jnp.exp2(jnp.minimum(c2[rows, k : k + 1] - row, 0.0))
                ms.append((sd_ref[i] * d).astype(BF16))
            yd = mm(jnp.concatenate(ms, axis=1), block_diag(vt[rows], low))
            yd_ref[rows, lanes] = yd
            y = yd + skip * v[rows]
            if i > 0:
                y = y + al2[rows] * mm(so_ref[i], vp[before])
            sc_ref[rows, lanes] = y
        return carry

    lax.fori_loop(0, inner // BLK, body, 0)


def mid_kernel(pieces, table, *refs):
    gw_refs, ow_refs = refs[:pieces], refs[pieces : 2 * pieces]
    (
        me_ref, xn_ref, sc_ref, gains_ref, cot_ref,
        lo_ref, hi_ref, g_ref, dgate_ref, mixed_ref, ginner_ref, wo_ref, wg_ref,
        dm_ref, nat_ref,
    ) = refs[2 * pieces :]
    me = me_ref[0]
    devices = len(table)
    share = wo_ref.shape[0] // devices
    per = ow_refs[0].shape[0] // share
    gain = slice(xn_ref.shape[1], gains_ref.shape[1])
    inner = sc_ref.shape[1]
    width = cot_ref.shape[1]
    rows_in = xn_ref.shape[1] // devices
    xn = xn_ref[...]
    wg_ref[...] = rows_of(gw_refs)
    g_ref[...] = mm(xn, wg_ref[...])
    if share % 16:
        wo_ref[...] = rows_of(ow_refs)
    else:
        for p in range(devices):
            at = pl.multiple_of((me ^ int(table[p])) * share, 16)
            row = (p % per) * share
            wo_ref[pl.ds(at, share), :] = ow_refs[p // per][row : row + share, :]
    dm_ref[...] = mm_nt(cot_ref[...], wo_ref[...])
    length = xn_ref.shape[0]
    sub = 32
    ginner_ref[...] = jnp.zeros_like(ginner_ref)

    def body(k, carry):
        rows = pl.ds(pl.multiple_of(k * sub, sub), sub)
        gate = g_ref[rows, :]
        sig = sigmoid(gate)
        silu = gate * sig
        scanned = sc_ref[rows, :]
        gated = scanned * silu
        scale = lax.rsqrt(jnp.mean(gated * gated, axis=-1, keepdims=True) + 1e-05)
        dm = dm_ref[rows, :]
        unit = gated * scale
        mixed_ref[rows, :] = (unit * gains_ref[:, gain]).astype(BF16)
        ginner_ref[...] += jnp.sum((dm * unit).reshape(sub // 8, 8, -1), axis=0)
        dunit = dm * gains_ref[:, gain]
        dot = jnp.mean(unit * dunit, axis=-1, keepdims=True)
        du = scale * (dunit - unit * dot)
        g_ref[rows, :] = du * silu
        dgate_ref[rows, :] = (du * scanned * (sig * (1.0 + gate * (1.0 - sig)))).astype(BF16)
        return carry

    lax.fori_loop(0, length // sub, body, 0)
    if rows_in % 8:
        lo_ref[...] = mm_tn(xn, dgate_ref[...]).astype(BF16)
        hi_ref[...] = mm_tn(mixed_ref[...], cot_ref[...]).astype(BF16)
        return
    gg = mm_tn(xn, dgate_ref[...]).astype(BF16)
    half = gg.shape[0] // 2
    lo_ref[:, :inner] = gg[:half]
    hi_ref[:, :inner] = gg[half:]
    nat_ref[...] = mm_tn(mixed_ref[...], cot_ref[...])
    for p in range(0, devices, 2):
        target = lo_ref if p < devices // 2 else hi_ref
        row = (p % (devices // 2)) * rows_in
        for k in range(2):
            both = [
                nat_ref[pl.ds(pl.multiple_of((me ^ int(table[q])) * share + k * rows_in, 8), rows_in), :]
                for q in (p, p + 1)
            ]
            lanes = slice(inner + k * width, inner + (k + 1) * width)
            target[row : row + 2 * rows_in, lanes] = jnp.concatenate(both, axis=0).astype(BF16)


def branch_kernel(mixed_ref, wo_ref, hid_ref, dgate_ref, wg_ref, out_ref, dn_ref):
    out_ref[...] = (hid_ref[...].astype(F32) + mm(mixed_ref[...], wo_ref[...])).astype(BF16)
    dn_ref[...] = mm_nt(dgate_ref[...], wg_ref[...])


def conv_back(dpre, x, taps_ref, lanes, mask_ref, dtaps_ref, dp_ref, to):
    kernel = mask_ref.shape[0] + 1
    length = dpre.shape[0]

    def total(z):
        return jnp.sum(z, axis=0, keepdims=True)

    dtaps_ref[kernel : kernel + 1, to] = total(dpre)
    dtaps_ref[kernel - 1 : kernel, to] = total(dpre * x)
    dx = taps_ref[kernel - 1 : kernel, lanes] * dpre
    for j in range(1, kernel):
        masked = dpre * mask_ref[j - 1]
        tap = slice(kernel - 1 - j, kernel - j)
        dtaps_ref[tap, to] = total(masked * pltpu.roll(x, j, axis=0))
        dx = dx + taps_ref[tap, lanes] * pltpu.roll(masked, length - j, axis=0)
    dp_ref[:, to] = dx.astype(BF16)


def silu_and_slope(pre):
    sig = sigmoid(pre)
    return pre * sig, sig * (1.0 + pre * (1.0 - sig))


def scan_bwd_kernel(
    g_ref, yd_ref, v_ref, slope_ref, ci_ref, dt_ref, taps_ref, segr_ref, alog_ref, skip_ref, bias_ref,
    dp_ref, dtaps_ref, dskip_ref, dheads_ref,
    heads_ref, step_ref, cc_ref, wide_ref, cct_ref, segb_ref, mask_ref,
    sdt_ref, so_ref, sot_ref, dsdt_ref, dso_ref, acc_ref, dpre_ref,
):
    length = ci_ref.shape[0]
    segr = segr_ref[...].astype(F32)
    blocks = length // BLK
    channels = ci_ref.shape[1]
    states = BLK
    inner = channels - 2 * states
    nheads = inner // (BLK // 2)
    lanes_b = slice(inner, inner + states)
    lanes_c = slice(inner + states, channels)

    head_setup(
        dt_ref[...], (alog_ref, skip_ref, bias_ref), segr, heads_ref, step_ref, cc_ref, wide_ref, cct_ref, segb_ref
    )
    mask_setup(segb_ref, mask_ref)
    dheads_ref[...] = jnp.zeros_like(dheads_ref)
    dtaps_ref[...] = jnp.zeros_like(dtaps_ref)
    _, pre_b = conv_parts(ci_ref[:, lanes_b], taps_ref, lanes_b, mask_ref)
    _, pre_c = conv_parts(ci_ref[:, lanes_c], taps_ref, lanes_c, mask_ref)
    score_setup(
        pre_b * sigmoid(pre_b), pre_c * sigmoid(pre_c),
        segb_ref, segr, None, so_ref, sdt_ref, sot_ref,
    )
    dsdt_ref[...] = jnp.zeros_like(dsdt_ref)
    dso_ref[...] = jnp.zeros_like(dso_ref)
    acc_ref[...] = jnp.zeros_like(acc_ref)

    def body(t, carry):
        lanes = pl.ds(pl.multiple_of(t * BLK, BLK), BLK)
        x = ci_ref[:, lanes]
        v = v_ref[:, lanes]
        low = iota((1, BLK), 1) < BLK // 2
        st2, ew2, wq2, al2, c2, r2, skip = pair_setup(t, heads_ref, wide_ref, cc_ref, cct_ref)
        vtb = (v * st2).astype(BF16)
        vpb = (v * wq2).astype(BF16)
        g = g_ref[:, lanes]
        gb = g.astype(BF16)
        gpb = (al2 * g).astype(BF16)
        dskip_ref[:, lanes] = jnp.sum(g * v, axis=0, keepdims=True)
        k_row = iota((3 * BLK, BLK), 0)
        target = jnp.where(k_row >= 2 * BLK, BLK // 2, 0) + 2 * t
        target = target + jnp.where((k_row & (BLK - 1)) >= BLK // 2, 1, 0)
        collect = (iota((3 * BLK, BLK), 1) == target).astype(F32).astype(BF16)
        for i in range(blocks):
            rows = slice(i * BLK, (i + 1) * BLK)
            before = slice((i - 1) * BLK, i * BLK)
            after = slice((i + 1) * BLK, (i + 2) * BLK)
            gdiag = block_diag(gb[rows], low)
            both = mm_nt(vtb[rows], gdiag)
            ms = []
            part = jnp.zeros((BLK, BLK), F32)
            for k in range(2):
                row = r2[k : k + 1, rows]
                d = jnp.exp2(jnp.minimum(row - c2[rows, k : k + 1], 0.0))
                ms.append((sdt_ref[i] * d).astype(BF16))
                part = part + both[:, k * BLK : (k + 1) * BLK] * d
            dsdt_ref[i] += part
            dvt = mm(jnp.concatenate(ms, axis=1), gdiag)
            x1 = gb[rows].astype(F32) * yd_ref[rows, lanes] - dvt * vtb[rows].astype(F32)
            dv = st2[rows] * dvt + skip * g[rows]
            dstep = dvt
            if i > 0:
                z = mm(so_ref[i], vpb[before])
                x1 = x1 + gpb[rows].astype(F32) * z
                dso_ref[i] += mm_nt(gpb[rows], vpb[before])
            if i + 1 < blocks:
                dvp = mm(sot_ref[i + 1], gpb[after])
                x1 = x1 - dvp * vpb[rows].astype(F32)
                dv = dv + wq2[rows] * dvp
                dstep = dstep + ew2[rows] * dvp
            h1, l1 = split2(x1)
            h2 = (dstep * v[rows]).astype(BF16)
            acc_ref[rows, :] += mm(jnp.concatenate([h1, l1, h2], axis=1), collect)
            dpre_ref[rows, :] = dv * slope_ref[rows, lanes]
        conv_back(dpre_ref[...], x, taps_ref, lanes, mask_ref, dtaps_ref, dp_ref, lanes)
        return carry

    lax.fori_loop(0, inner // BLK, body, 0)
    xb, xc = ci_ref[:, lanes_b], ci_ref[:, lanes_c]
    _, pre_b = conv_parts(xb, taps_ref, lanes_b, mask_ref)
    _, pre_c = conv_parts(xc, taps_ref, lanes_c, mask_ref)
    bmat, slope_b = silu_and_slope(pre_b)
    cmat, slope_c = silu_and_slope(pre_c)
    bb, cb = bmat.astype(BF16), cmat.astype(BF16)
    causal_t = iota((BLK, BLK), 1) >= iota((BLK, BLK), 0)
    upper = causal_t.astype(F32)
    dst, dso = [], [None]
    for i in range(blocks):
        rows = slice(i * BLK, (i + 1) * BLK)
        before = slice((i - 1) * BLK, i * BLK)
        same = (segb_ref[rows, :] == segr[:, rows]) & causal_t
        dst.append(jnp.where(same, dsdt_ref[i], 0.0))
        if i > 0:
            linked = segb_ref[rows, :] == segr[:, before]
            dso.append(jnp.where(linked, dso_ref[i], 0.0))
    for i in range(blocks):
        rows = slice(i * BLK, (i + 1) * BLK)
        before = slice((i - 1) * BLK, i * BLK)
        after = slice((i + 1) * BLK, (i + 2) * BLK)
        dc = mm(dst[i].T.astype(BF16), bb[rows])
        if i > 0:
            dc = dc + mm(dso[i].astype(BF16), bb[before])
        dpre_ref[rows, :] = dc * slope_c[rows]
    conv_back(dpre_ref[...], xc, taps_ref, lanes_c, mask_ref, dtaps_ref, dp_ref, lanes_c)
    for i in range(blocks):
        rows = slice(i * BLK, (i + 1) * BLK)
        after = slice((i + 1) * BLK, (i + 2) * BLK)
        db = mm(dst[i].astype(BF16), cb[rows])
        if i + 1 < blocks:
            db = db + mm(dso[i + 1].T.astype(BF16), cb[after])
        dpre_ref[rows, :] = db * slope_b[rows]
    conv_back(dpre_ref[...], xb, taps_ref, lanes_b, mask_ref, dtaps_ref, dp_ref, lanes_b)

    decay = jnp.exp(heads_ref[0:1, :])
    later = jnp.zeros((1, BLK), F32)
    dalog = jnp.zeros((1, BLK), F32)
    dbias = jnp.zeros((1, BLK), F32)
    for i in reversed(range(blocks)):
        rows = slice(i * BLK, (i + 1) * BLK)
        dcum = acc_ref[rows, :]
        drate = later + jnp.dot(upper, dcum, precision=HIGH, preferred_element_type=F32)
        later = drate[0:1, :]
        step = step_ref[rows, :]
        dalog = dalog - jnp.sum(drate * step, axis=0, keepdims=True) * decay
        dstep = pltpu.roll(dcum, BLK // 2, axis=1) - drate * decay
        ddt = dstep * sigmoid(dt_ref[rows, :] + heads_ref[2:3, :])
        dbias = dbias + jnp.sum(ddt, axis=0, keepdims=True)
        dp_ref[rows, channels:] = jnp.where(iota((1, BLK), 1) < nheads, ddt, 0.0).astype(BF16)
    dheads_ref[0:1, :] = dalog
    dheads_ref[1:2, :] = dbias


def grad_in_kernel(xn_ref, dp_ref, lo_ref, hi_ref):
    grad = mm_tn(xn_ref[...], dp_ref[...]).astype(BF16)
    half = grad.shape[0] // 2
    lo_ref[...] = grad[:half]
    hi_ref[...] = grad[half:]


def input_kernel(
    wc_ref, dng_ref, dp_ref, me_ref, tab_ref, hid_ref, cot_ref, gains_ref,
    dtaps_ref, ginner_ref, dskip_ref, dheads_ref,
    ig_ref, sums_ref,
):
    dn = mm_nt(dp_ref[...], wc_ref[...]) + dng_ref[...]
    perm = perm_matrix(me_ref[0], tab_ref, dn.shape[1])
    hi, lo = split2(dn)
    dn = mm_nt(hi, perm) + mm_nt(lo, perm)
    tokens = hid_ref[...].astype(F32)
    scale = lax.rsqrt(jnp.mean(tokens * tokens, axis=-1, keepdims=True) + 1e-05)
    unit = tokens * scale
    width = tokens.shape[1]
    sums_ref[...] = jnp.zeros_like(sums_ref)
    sums_ref[0:5, : dtaps_ref.shape[1]] = dtaps_ref[0:5, :]
    sums_ref[5:6, :width] = jnp.sum(dn * unit, axis=0, keepdims=True)
    sums_ref[5:6, width:] = jnp.sum(ginner_ref[...], axis=0, keepdims=True)
    sums_ref[6:7, : dskip_ref.shape[1]] = dskip_ref[...]
    sums_ref[7:8, :BLK] = dheads_ref[0:1, :]
    sums_ref[7:8, BLK : 2 * BLK] = dheads_ref[1:2, :]
    dunit = dn * gains_ref[:, :width]
    inner = jnp.mean(unit * dunit, axis=-1, keepdims=True)
    ig_ref[...] = cot_ref[...].astype(F32) + scale * (dunit - unit * inner)


def stack_kernel(*refs):
    rows = jnp.concatenate([ref[...].astype(F32) for ref in refs[:-1]], axis=0)
    refs[-1][...] = rows.astype(BF16)


def fold_kernel(count, *refs):
    total = refs[0][...].astype(F32)
    for ref in refs[1:count]:
        total = total + ref[...].astype(F32)
    size = total.shape[0] // len(refs[count:])
    for k, ref in enumerate(refs[count:]):
        ref[...] = total[k * size : (k + 1) * size].astype(ref.dtype)


def last_out_kernel(a_ref, b_ref, c_ref, d_ref, gate_ref, out_ref):
    total = a_ref[...].astype(F32) + b_ref[...].astype(F32) + c_ref[...].astype(F32) + d_ref[...].astype(F32)
    inner = gate_ref.shape[1]
    rows, width = a_ref.shape[0], out_ref.shape[1]
    gate_ref[...] = total[:, :inner]
    out_ref[:rows, :] = total[:, inner : inner + width]
    out_ref[rows:, :] = total[:, inner + width :]


def last_in_kernel(a_ref, b_ref, c_ref, d_ref, gate_ref, in_ref):
    total = a_ref[...].astype(F32) + b_ref[...].astype(F32) + c_ref[...].astype(F32) + d_ref[...].astype(F32)
    inner = gate_ref.shape[1]
    in_ref[:, :inner] = gate_ref[...]
    in_ref[:, inner:] = total[:, : in_ref.shape[1] - inner]


def sds(shape, dtype):
    return jax.ShapeDtypeStruct(shape, dtype)


def held(shape, dtype):
    return pltpu.VMEM(shape, dtype)


def scan_scratch(length, inner, taps):
    nheads = -(-2 * inner // (8 * BLK)) * 8
    return [
        pltpu.VMEM((8, BLK), F32), pltpu.VMEM((length, BLK), F32), pltpu.VMEM((length, BLK), F32),
        pltpu.VMEM((3, length, 2 * BLK), BF16), pltpu.VMEM((nheads, length), F32), pltpu.VMEM((length, BLK), F32),
        pltpu.VMEM((taps - 1, length, BLK), F32),
    ]


def scan_fwd(weights, packed, taps_n, widths, mine, tab, hidden, first, second, segr, *heads):
    length, width = hidden.shape
    channels, inner = widths
    blocks = length // BLK
    count = len(weights)
    rows = held((length, inner), F32)
    return call(
        lambda *refs: scan_fwd_kernel(count, packed, *refs),
        (
            held((length, width), BF16), held((8, channels), F32), held((1, width + inner), F32),
            held((width, channels + BLK), BF16),
            held((length, channels), F32), held((length, BLK), F32), rows, rows, rows, rows,
        ),
        *weights, mine, tab, hidden, first, second, segr, *heads, scalar=count,
        leave=(tab, first, second, segr) + heads,
        scratch=scan_scratch(length, inner, taps_n - 1) + [
            pltpu.VMEM((blocks, BLK, BLK), F32),
            pltpu.VMEM((blocks, BLK, BLK), BF16),
        ],
    )


def scan_bwd(taps_n, g, yd, v, slope, ci, dt, taps, segr, *heads):
    length, channels = ci.shape
    inner = g.shape[1]
    score = (length // BLK, BLK, BLK)
    return call(
        scan_bwd_kernel,
        (
            held((length, channels + BLK), BF16), held(taps.shape, F32), held((1, inner), F32),
            held((8, BLK), F32),
        ),
        g, yd, v, slope, ci, dt, taps, segr, *heads, leave=(segr,) + heads,
        scratch=scan_scratch(length, inner, taps_n - 1) + [
            pltpu.VMEM(score, F32),
            pltpu.VMEM(score, BF16),
            pltpu.VMEM(score, BF16),
            pltpu.VMEM(score, F32),
            pltpu.VMEM(score, F32),
            pltpu.VMEM((length, BLK), F32),
            pltpu.VMEM((length, BLK), F32),
        ],
    )


def call(kernel, outs, *ins, scratch=(), scalar=None, leave=()):
    specs = [
        pl.BlockSpec(memory_space=pltpu.SMEM if k == scalar else pltpu.VMEM) for k in range(len(ins))
    ]
    near = [
        a if k == scalar else pltpu.with_memory_space_constraint(a, pltpu.HBM if any(a is b for b in leave) else pltpu.VMEM)
        for k, a in enumerate(ins)
    ]
    many = isinstance(outs, (tuple, list))
    out_specs = [pl.BlockSpec(memory_space=pltpu.VMEM) for _ in outs] if many else pl.BlockSpec(memory_space=pltpu.VMEM)
    return pl.pallas_call(
        kernel, out_shape=outs, in_specs=specs, out_specs=out_specs, scratch_shapes=list(scratch),
        compiler_params=pltpu.CompilerParams(vmem_limit_bytes=(20 if scratch else 8) * 1024 * 1024),
    )(*near)


def stages(devices):
    masks = [1 << b for b in range(devices.bit_length() - 1)]
    groups = []
    for end in range(len(masks), 1, -2):
        part = masks[max(end - 2, 1) : end]
        groups.append(part if len(part) == 1 else [part[0], part[1], part[0] | part[1]])
    return groups + [masks[:1]]


def order_table(devices):
    table = np.zeros((1,), np.int32)
    for group in stages(devices):
        table = np.concatenate([table] + [table ^ m for m in group])
    return table


def send(x, devices, mask):
    return lax.ppermute(x, "fsdp", [(i, i ^ mask) for i in range(devices)])


def send_all(parts, devices, stage):
    return [send(part, devices, m) for part, m in zip(parts, stages(devices)[stage])]


def stack(pieces, leave):
    size, rest = pieces[0].shape[0], pieces[0].shape[1:]
    if size % 8 or len(rest) != 1:
        return jnp.concatenate(pieces, axis=0)
    return call(stack_kernel, held((len(pieces) * size,) + rest, BF16), *pieces, leave=leave)


def gather(x, devices, leave=()):
    groups = stages(devices)
    core = len(groups) - 1
    pieces = [x]
    for stage in range(core):
        x = pieces[0] if len(pieces) == 1 else stack(pieces, leave)
        pieces = [x] + send_all([x] * len(groups[stage]), devices, stage)
    return pieces + [send(a, devices, 1) for a in pieces]


def fold(parts, fan, dtype):
    rows, cols = parts[0].shape
    size = rows // fan
    if size % 8:
        total = sum(part.astype(F32) for part in parts).astype(dtype)
        return [total[k * size : (k + 1) * size] for k in range(fan)]
    count = len(parts)
    return call(lambda *refs: fold_kernel(count, *refs), tuple(held((size, cols), dtype) for _ in range(fan)), *parts)


def reduce_shares(lo, hi, devices):
    groups = stages(devices)
    parts = [lo, hi]
    for stage in reversed(range(len(groups))):
        parts = [parts[0]] + send_all(parts[1:], devices, stage)
        if stage:
            parts = fold(parts, len(groups[stage - 1]) + 1, BF16)
    return parts


def total_of(x, devices):
    for stage in reversed(range(len(stages(devices)))):
        group = stages(devices)[stage]
        got = send_all([x] * len(group), devices, stage)
        x = x + got[0] if len(got) == 1 else (x + got[0]) + (got[1] + got[2])
    return x


def layer(
    hidden, segment_ids, cot, w_in, w_out, conv_taps, gains, a_log, d_skip, dt_bias
):
    length = segment_ids.shape[1]
    width = hidden.shape[1]
    devices = lax.axis_size("fsdp")
    me = lax.axis_index("fsdp")
    nheads = a_log.shape[0]
    taps_n, tap_share = conv_taps.shape
    channels = tap_share * devices
    gain_share = gains.shape[0]
    inner = w_out.shape[0] * devices
    proj = w_in.shape[1]
    rows_in, rows_out = w_in.shape[0], w_out.shape[0]
    pairs = inner // BLK
    first = pairs // 2

    table = order_table(devices)
    inverse = np.argsort(table).astype(np.int32)
    order = jnp.asarray(table) ^ me
    place = jnp.asarray(inverse)[me ^ jnp.arange(devices)]
    mine = me.reshape(1).astype(jnp.int32)
    tab = np.zeros((8, width), np.int32)
    tab[0], tab[1], tab[2] = np.repeat(table, rows_in), np.tile(np.arange(rows_in), devices), rows_in
    tab = jnp.asarray(tab)

    spare = BLK - (proj - inner - channels)
    packed = rows_in > taps_n and max(tap_share, gain_share) <= spare
    if packed:
        gain_row = gains.reshape(1, gain_share)
        w_conv, w_gate = call(
            lambda *refs: pack_kernel(inner, *refs),
            (held((rows_in, channels + BLK), BF16), held((rows_in, inner), BF16)),
            w_in, conv_taps, gain_row, leave=(w_in, conv_taps, gain_row),
        )
    else:
        w_conv = jnp.pad(w_in[:, inner:], ((0, 0), (0, spare)))
        w_gate = w_in[:, :inner]
    cw = gather(w_conv, devices)
    gw = gather(w_gate, devices)
    ow = gather(w_out, devices, (w_out,))
    count = len(cw)

    heads = [x.reshape(1, nheads) for x in (a_log, d_skip, dt_bias)]

    if packed:
        at = np.arange(width + inner)
        where = np.stack([at % tap_share, at // tap_share, at % gain_share, at // gain_share])
        second = jnp.asarray(np.pad(where, ((0, 4), (0, 0))).astype(np.int32))
        first = jnp.asarray(table.reshape(devices, 1))
    else:
        small = jnp.zeros((8, BLK), F32)
        small = small.at[:taps_n, :tap_share].set(conv_taps.astype(F32))
        small = small.at[taps_n, :gain_share].set(gains.astype(F32))
        rows = jnp.concatenate(gather(small[None], devices), axis=0)[place]
        first = jnp.moveaxis(rows[:, :, :tap_share], 0, 1).reshape(8, channels)
        second = rows[:, taps_n, :gain_share].reshape(1, width + inner)
    xn, taps, gains_all, wc, ci, dt, sc, yd, v, slope = scan_fwd(
        cw, (proj - inner - channels, taps_n) if packed else None, taps_n, (channels, inner),
        mine, tab, hidden, first, second, segment_ids, *heads,
    )
    if rows_out % 16:
        wo_all = jnp.concatenate(ow, axis=0).reshape(devices, rows_out, width)[place].reshape(inner, width)
        ow = [wo_all[k * (inner // count) : (k + 1) * (inner // count)] for k in range(count)]
    aligned = rows_in % 8 == 0
    if aligned:
        halves = (held((width // 2, inner + 2 * width), BF16), held((width // 2, inner + 2 * width), BF16))
    else:
        halves = (sds((width, inner), BF16), sds((inner, width), BF16))
    lo, hi, g, dgate, mixed, ginner, wo, wg = call(
        lambda *refs: mid_kernel(count, table, *refs),
        halves + (
            held((length, inner), F32), held((length, inner), BF16), held((length, inner), BF16),
            held((8, inner), F32), held((inner, width), BF16), held((width, inner), BF16),
        ),
        *gw, *ow, mine, xn, sc, gains_all, cot,
        scratch=(
            pltpu.VMEM((length, inner), F32), pltpu.VMEM((inner, width), F32),
        ),
        scalar=2 * count,
    )
    if not aligned:
        gwo = hi.reshape(devices, 2, rows_in, width)[order]
        both = jnp.concatenate([lo, gwo[:, 0].reshape(width, width), gwo[:, 1].reshape(width, width)], axis=1)
        lo, hi = both[: width // 2], both[width // 2 :]
    mid_parts = reduce_shares(lo, hi, devices)
    output, dng = call(
        branch_kernel, (sds((length, width), BF16), held((length, width), F32)),
        mixed, wo, hidden, dgate, wg,
    )
    dp, dtaps, dskip, dheads = scan_bwd(taps_n, g, yd, v, slope, ci, dt, taps, segment_ids, *heads)
    half = held((width // 2, dp.shape[1]), BF16)
    clo, chi = call(grad_in_kernel, (half, half), xn, dp)
    conv_parts_in = reduce_shares(clo, chi, devices)
    input_grad, sums = call(
        input_kernel,
        (sds((length, width), F32), held((8, width + inner), F32)),
        wc, dng, dp, mine, tab, hidden, cot, gains_all, dtaps, ginner, dskip, dheads, scalar=3, leave=(tab,),
    )
    if aligned and len(mid_parts) == 4:
        gate_share, out_share = call(
            last_out_kernel,
            (sds((rows_in, inner), F32), sds((rows_out, width), F32)), *mid_parts,
        )
        in_share = call(last_in_kernel, sds((rows_in, proj), F32), *conv_parts_in, gate_share)
    else:
        total = sum(part.astype(F32) for part in mid_parts)
        out_share = jnp.concatenate([total[:, inner : inner + width], total[:, inner + width :]], axis=0)
        conv_total = sum(part.astype(F32) for part in conv_parts_in)
        in_share = jnp.concatenate([total[:, :inner], conv_total], axis=1)[:, :proj]

    sums = total_of(sums, devices)
    taps_share = lax.dynamic_slice_in_dim(sums[:taps_n, :channels], me * tap_share, tap_share, axis=1)
    gains_share = lax.dynamic_slice_in_dim(sums[5], me * gain_share, gain_share)
    return (
        output, input_grad, in_share, out_share, taps_share, gains_share,
        sums[7, :nheads], sums[6, :inner].reshape(nheads, -1).sum(axis=1), sums[7, BLK : BLK + nheads],
    )


def solution(mesh):
    axis = P("fsdp")
    rows = P("fsdp", None)
    cols = P(None, "fsdp")
    return jax.shard_map(
        layer,
        mesh=mesh,
        in_specs=(rows, rows, rows, rows, rows, cols, axis, P(), P(), P()),
        out_specs=(rows, rows, rows, rows, cols, axis, P(), P(), P()),
        check_vma=False,
    )
```

```python
import jax
import jax.numpy as jnp
import numpy as np
from jax import lax
from jax.experimental import pallas as pl
from jax.experimental.pallas import tpu as pltpu
from jax.sharding import PartitionSpec as P


BLK = 128
LOG2E = 1.4426950408889634
F32 = jnp.float32
BF16 = jnp.bfloat16
HIGH = lax.Precision.HIGHEST


def mm(a, b):
    return lax.dot_general(a, b, (((1,), (0,)), ((), ())), preferred_element_type=F32)


def mm_nt(a, b):
    return lax.dot_general(a, b, (((1,), (1,)), ((), ())), preferred_element_type=F32)


def mm_tn(a, b):
    return lax.dot_general(a, b, (((0,), (0,)), ((), ())), preferred_element_type=F32)


def split2(x):
    hi = x.astype(BF16)
    return hi, (x - hi.astype(F32)).astype(BF16)


def iota(shape, dim):
    return lax.broadcasted_iota(jnp.int32, shape, dim)


def perm_matrix(me, tab_ref, width):
    dvec = (tab_ref[0:1, :] ^ me) * tab_ref[2:3, 0:1] + tab_ref[1:2, :]
    return (iota((width, width), 0) == dvec).astype(F32).astype(BF16)


def rows_of(refs, lanes=slice(None)):
    return jnp.concatenate([ref[:, lanes] for ref in refs], axis=0)


def normed_of(hid_ref, gain, me, tab_ref, xn_ref):
    tokens = hid_ref[...].astype(F32)
    scale = lax.rsqrt(jnp.mean(tokens * tokens, axis=-1, keepdims=True) + 1e-05)
    normed = (tokens * scale * gain).astype(BF16)
    perm = perm_matrix(me, tab_ref, tokens.shape[1])
    xn_ref[...] = mm(normed, perm).astype(BF16)


def pack_kernel(inner, w_ref, taps_in, gains_in, conv_ref, gate_ref):
    gate_ref[...] = w_ref[:, :inner]
    body = conv_ref.shape[1] - BLK
    conv_ref[:, :body] = w_ref[:, inner : inner + body]
    tail = w_ref[:, inner + body :]
    spare = tail.shape[1]
    rows, taps_n = w_ref.shape[0], taps_in.shape[0]

    def onto(x, at):
        return mm(x, (iota((x.shape[1], BLK), 1) == iota((x.shape[1], BLK), 0) + at).astype(F32).astype(BF16))

    row = iota((rows, BLK), 0)
    tile_of = onto(tail, 0)
    taps_wide, gains_wide = onto(taps_in[...], spare), onto(gains_in[...], spare)
    for j in range(taps_n):
        tile_of = tile_of + jnp.where(row == j, taps_wide[j : j + 1, :], 0.0)
    tile_of = tile_of + jnp.where(row == taps_n, gains_wide, 0.0)
    conv_ref[:, body:] = tile_of.astype(BF16)


def unpack(at, taps_n, pieces, me, owner_ref, where_ref, taps_ref, gains_ref):
    last = pieces[0].shape[1] - BLK
    tail = rows_of(pieces, slice(last, last + BLK))
    devices = owner_ref.shape[0]
    rows_in = tail.shape[0] // devices
    row = iota((8 * devices, tail.shape[0]), 0)
    bits = devices.bit_length() - 1
    source = (row & (devices - 1)) * rows_in + lax.shift_right_logical(row, bits)
    pick = (iota(row.shape, 1) == source).astype(F32).astype(BF16)
    small = mm(pick, tail).astype(BF16)

    def spread(part, line, width):
        lane, owner = where_ref[line : line + 1, :width], where_ref[line + 1 : line + 2, :width]
        chosen = (iota((BLK, width), 0) == lane + at).astype(F32).astype(BF16)
        wide = mm(part, chosen)
        return jnp.sum(jnp.where((owner_ref[...] ^ me) == owner, wide, 0.0), axis=0, keepdims=True)

    channels, width = taps_ref.shape[1], gains_ref.shape[1]
    taps_ref[...] = jnp.zeros_like(taps_ref)
    for j in range(taps_n):
        taps_ref[j : j + 1, :] = spread(small[j * devices : (j + 1) * devices], 0, channels)
    gains_ref[...] = spread(small[taps_n * devices : (taps_n + 1) * devices], 2, width)


def head_setup(dt_raw, rows_in, segr, heads_ref, step_ref, cc_ref, wide_ref, cct_ref, segb_ref):
    length = dt_raw.shape[0]
    heads_ref[...] = jnp.zeros_like(heads_ref)
    for k, ref in enumerate(rows_in):
        heads_ref[k : k + 1, : ref.shape[1]] = ref[...]
    segb_ref[...] = jnp.broadcast_to(segr, (BLK, length)).T
    biased = dt_raw + heads_ref[2:3, :]
    step = jnp.maximum(biased, 0.0) + jnp.log1p(jnp.exp(-jnp.abs(biased)))
    step_ref[...] = step
    rate = step * (jnp.exp(heads_ref[0:1, :]) * (-LOG2E))
    lower = (iota((BLK, BLK), 0) >= iota((BLK, BLK), 1)).astype(F32)
    for i in range(length // BLK):
        rows = slice(i * BLK, (i + 1) * BLK)
        cc = jnp.dot(lower, rate[rows], precision=HIGH, preferred_element_type=F32)
        cc_ref[rows, :] = cc
        ew = jnp.exp2(jnp.minimum(cc[BLK - 1 : BLK, :] - cc, 0.0))
        for k, x in enumerate((step[rows], ew, jnp.exp2(cc))):
            wide_ref[k, rows, :] = jnp.concatenate(split2(x), axis=1)
        cct_ref[:, rows] = cc.T[: cct_ref.shape[0]]


def mask_setup(segb_ref, mask_ref):
    segb = segb_ref[...]
    pos = iota(segb.shape, 0)
    for j in range(1, mask_ref.shape[0] + 1):
        prev = pltpu.roll(segb, j, axis=0)
        mask_ref[j - 1] = ((prev == segb) & (pos >= j)).astype(F32)


def conv_parts(x, taps_ref, lanes, mask_ref):
    kernel = mask_ref.shape[0] + 1
    shifts = [x] + [pltpu.roll(x, j, axis=0) * mask_ref[j - 1] for j in range(1, kernel)]
    pre = taps_ref[kernel : kernel + 1, lanes] + taps_ref[kernel - 1 : kernel, lanes] * x
    for j in range(1, kernel):
        pre = pre + taps_ref[kernel - 1 - j : kernel - j, lanes] * shifts[j]
    return shifts, pre


def sigmoid(x):
    return 0.5 * jnp.tanh(0.5 * x) + 0.5


def score_setup(bmat, cmat, segb_ref, segr, sd_ref, so_ref, sdt_ref, sot_ref):
    length = bmat.shape[0]
    bb, cb = bmat.astype(BF16), cmat.astype(BF16)
    causal = iota((BLK, BLK), 0) >= iota((BLK, BLK), 1)
    for i in range(length // BLK):
        rows = slice(i * BLK, (i + 1) * BLK)
        before = slice((i - 1) * BLK, i * BLK)
        same = (segb_ref[rows, :] == segr[:, rows]) & causal
        diag = jnp.where(same, mm_nt(cb[rows], bb[rows]), 0.0)
        if sd_ref is not None:
            sd_ref[i] = diag
        if sdt_ref is not None:
            sdt_ref[i] = diag.T
        if i > 0:
            linked = segb_ref[rows, :] == segr[:, before]
            off = jnp.where(linked, mm_nt(cb[rows], bb[before]), 0.0)
            so_ref[i] = off.astype(BF16)
            if sot_ref is not None:
                sot_ref[i] = off.T.astype(BF16)


def pair_setup(t, heads_ref, wide_ref, cc_ref, cct_ref):
    head = iota((2 * BLK, BLK), 0) & (BLK - 1)
    pick = (head == 2 * t + jnp.where(iota((2 * BLK, BLK), 1) < BLK // 2, 0, 1)).astype(F32).astype(BF16)
    st2, ew2, al2 = [mm(wide_ref[k], pick) for k in range(3)]
    c2 = pltpu.roll(cc_ref[...], lax.rem(BLK - 2 * t, BLK), axis=1)
    r2 = pltpu.roll(cct_ref[...], lax.rem(cct_ref.shape[0] - 2 * t, cct_ref.shape[0]), axis=0)
    h2 = pltpu.roll(heads_ref[...], lax.rem(BLK - 2 * t, BLK), axis=1)
    skip = jnp.where(iota((1, BLK), 1) < BLK // 2, h2[1:2, 0:1], h2[1:2, 1:2])
    return st2, ew2, ew2 * st2, al2, c2, r2, skip


def block_diag(x, low):
    zero = jnp.zeros_like(x)
    return jnp.concatenate([jnp.where(low, x, zero), jnp.where(low, zero, x)], axis=0)


def scan_fwd_kernel(pieces, packed, *refs):
    w_refs = refs[:pieces]
    (
        me_ref, tab_ref, hid_ref, first_ref, second_ref, segr_ref, alog_ref, skip_ref, bias_ref,
        xn_ref, taps_ref, gains_ref, wc_ref, ci_ref, dt_ref, sc_ref, yd_ref, v_ref, slope_ref,
        heads_ref, step_ref, cc_ref, wide_ref, cct_ref, segb_ref, mask_ref, sd_ref, so_ref,
    ) = refs[pieces:]
    me = me_ref[0]
    segr = segr_ref[...].astype(F32)
    length = xn_ref.shape[0]
    channels = ci_ref.shape[1]
    states = BLK
    inner = channels - 2 * states
    if packed:
        unpack(packed[0], packed[1], w_refs, me, first_ref, second_ref, taps_ref, gains_ref)
    else:
        taps_ref[...] = first_ref[...]
        gains_ref[...] = second_ref[...]
    normed_of(hid_ref, gains_ref[:, : hid_ref.shape[1]], me, tab_ref, xn_ref)
    xn = xn_ref[...]
    wc_ref[...] = rows_of(w_refs)
    ci_ref[...] = mm(xn, wc_ref[:, :channels])
    dt_ref[...] = mm(xn, wc_ref[:, channels:])
    head_setup(
        dt_ref[...], (alog_ref, skip_ref, bias_ref), segr, heads_ref, step_ref, cc_ref, wide_ref, cct_ref, segb_ref
    )
    mask_setup(segb_ref, mask_ref)
    lanes_b = slice(inner, inner + states)
    lanes_c = slice(inner + states, channels)
    _, pre_b = conv_parts(ci_ref[:, lanes_b], taps_ref, lanes_b, mask_ref)
    _, pre_c = conv_parts(ci_ref[:, lanes_c], taps_ref, lanes_c, mask_ref)
    score_setup(
        pre_b * sigmoid(pre_b), pre_c * sigmoid(pre_c),
        segb_ref, segr, sd_ref, so_ref, None, None,
    )

    def body(t, carry):
        lanes = pl.ds(pl.multiple_of(t * BLK, BLK), BLK)
        _, pre = conv_parts(ci_ref[:, lanes], taps_ref, lanes, mask_ref)
        v, slope = silu_and_slope(pre)
        v_ref[:, lanes] = v
        slope_ref[:, lanes] = slope
        low = iota((1, BLK), 1) < BLK // 2
        st2, _, wq2, al2, c2, r2, skip = pair_setup(t, heads_ref, wide_ref, cc_ref, cct_ref)
        vt = (v * st2).astype(BF16)
        vp = (v * wq2).astype(BF16)
        for i in range(length // BLK):
            rows = slice(i * BLK, (i + 1) * BLK)
            before = slice((i - 1) * BLK, i * BLK)
            ms = []
            for k in range(2):
                row = r2[k : k + 1, rows]
                d = jnp.exp2(jnp.minimum(c2[rows, k : k + 1] - row, 0.0))
                ms.append((sd_ref[i] * d).astype(BF16))
            yd = mm(jnp.concatenate(ms, axis=1), block_diag(vt[rows], low))
            yd_ref[rows, lanes] = yd
            y = yd + skip * v[rows]
            if i > 0:
                y = y + al2[rows] * mm(so_ref[i], vp[before])
            sc_ref[rows, lanes] = y
        return carry

    lax.fori_loop(0, inner // BLK, body, 0)


def mid_kernel(pieces, table, *refs):
    gw_refs, ow_refs = refs[:pieces], refs[pieces : 2 * pieces]
    (
        me_ref, xn_ref, sc_ref, gains_ref, cot_ref,
        lo_ref, hi_ref, g_ref, dgate_ref, mixed_ref, ginner_ref, wo_ref, wg_ref,
        dm_ref, nat_ref,
    ) = refs[2 * pieces :]
    me = me_ref[0]
    devices = len(table)
    share = wo_ref.shape[0] // devices
    per = ow_refs[0].shape[0] // share
    gain = slice(xn_ref.shape[1], gains_ref.shape[1])
    inner = sc_ref.shape[1]
    width = cot_ref.shape[1]
    rows_in = xn_ref.shape[1] // devices
    xn = xn_ref[...]
    wg_ref[...] = rows_of(gw_refs)
    g_ref[...] = mm(xn, wg_ref[...])
    if share % 16:
        wo_ref[...] = rows_of(ow_refs)
    else:
        for p in range(devices):
            at = pl.multiple_of((me ^ int(table[p])) * share, 16)
            row = (p % per) * share
            wo_ref[pl.ds(at, share), :] = ow_refs[p // per][row : row + share, :]
    dm_ref[...] = mm_nt(cot_ref[...], wo_ref[...])
    length = xn_ref.shape[0]
    sub = 32
    ginner_ref[...] = jnp.zeros_like(ginner_ref)

    def body(k, carry):
        rows = pl.ds(pl.multiple_of(k * sub, sub), sub)
        gate = g_ref[rows, :]
        sig = sigmoid(gate)
        silu = gate * sig
        scanned = sc_ref[rows, :]
        gated = scanned * silu
        scale = lax.rsqrt(jnp.mean(gated * gated, axis=-1, keepdims=True) + 1e-05)
        dm = dm_ref[rows, :]
        unit = gated * scale
        mixed_ref[rows, :] = (unit * gains_ref[:, gain]).astype(BF16)
        ginner_ref[...] += jnp.sum((dm * unit).reshape(sub // 8, 8, -1), axis=0)
        dunit = dm * gains_ref[:, gain]
        dot = jnp.mean(unit * dunit, axis=-1, keepdims=True)
        du = scale * (dunit - unit * dot)
        g_ref[rows, :] = du * silu
        dgate_ref[rows, :] = (du * scanned * (sig * (1.0 + gate * (1.0 - sig)))).astype(BF16)
        return carry

    lax.fori_loop(0, length // sub, body, 0)
    if rows_in % 8:
        lo_ref[...] = mm_tn(xn, dgate_ref[...]).astype(BF16)
        hi_ref[...] = mm_tn(mixed_ref[...], cot_ref[...]).astype(BF16)
        return
    gg = mm_tn(xn, dgate_ref[...]).astype(BF16)
    half = gg.shape[0] // 2
    lo_ref[:, :inner] = gg[:half]
    hi_ref[:, :inner] = gg[half:]
    nat_ref[...] = mm_tn(mixed_ref[...], cot_ref[...])
    for p in range(0, devices, 2):
        target = lo_ref if p < devices // 2 else hi_ref
        row = (p % (devices // 2)) * rows_in
        for k in range(2):
            both = [
                nat_ref[pl.ds(pl.multiple_of((me ^ int(table[q])) * share + k * rows_in, 8), rows_in), :]
                for q in (p, p + 1)
            ]
            lanes = slice(inner + k * width, inner + (k + 1) * width)
            target[row : row + 2 * rows_in, lanes] = jnp.concatenate(both, axis=0).astype(BF16)


def branch_kernel(mixed_ref, wo_ref, hid_ref, dgate_ref, wg_ref, out_ref, dn_ref):
    out_ref[...] = (hid_ref[...].astype(F32) + mm(mixed_ref[...], wo_ref[...])).astype(BF16)
    dn_ref[...] = mm_nt(dgate_ref[...], wg_ref[...])


def conv_back(dpre, x, taps_ref, lanes, mask_ref, dtaps_ref, dp_ref, to):
    kernel = mask_ref.shape[0] + 1
    length = dpre.shape[0]

    def total(z):
        return jnp.sum(z, axis=0, keepdims=True)

    dtaps_ref[kernel : kernel + 1, to] = total(dpre)
    dtaps_ref[kernel - 1 : kernel, to] = total(dpre * x)
    dx = taps_ref[kernel - 1 : kernel, lanes] * dpre
    for j in range(1, kernel):
        masked = dpre * mask_ref[j - 1]
        tap = slice(kernel - 1 - j, kernel - j)
        dtaps_ref[tap, to] = total(masked * pltpu.roll(x, j, axis=0))
        dx = dx + taps_ref[tap, lanes] * pltpu.roll(masked, length - j, axis=0)
    dp_ref[:, to] = dx.astype(BF16)


def silu_and_slope(pre):
    sig = sigmoid(pre)
    return pre * sig, sig * (1.0 + pre * (1.0 - sig))


def scan_bwd_kernel(
    g_ref, yd_ref, v_ref, slope_ref, ci_ref, dt_ref, taps_ref, segr_ref, alog_ref, skip_ref, bias_ref,
    dp_ref, dtaps_ref, dskip_ref, dheads_ref,
    heads_ref, step_ref, cc_ref, wide_ref, cct_ref, segb_ref, mask_ref,
    sdt_ref, so_ref, sot_ref, dsdt_ref, dso_ref, acc_ref, dpre_ref,
):
    length = ci_ref.shape[0]
    segr = segr_ref[...].astype(F32)
    blocks = length // BLK
    channels = ci_ref.shape[1]
    states = BLK
    inner = channels - 2 * states
    nheads = inner // (BLK // 2)
    lanes_b = slice(inner, inner + states)
    lanes_c = slice(inner + states, channels)

    head_setup(
        dt_ref[...], (alog_ref, skip_ref, bias_ref), segr, heads_ref, step_ref, cc_ref, wide_ref, cct_ref, segb_ref
    )
    mask_setup(segb_ref, mask_ref)
    dheads_ref[...] = jnp.zeros_like(dheads_ref)
    dtaps_ref[...] = jnp.zeros_like(dtaps_ref)
    _, pre_b = conv_parts(ci_ref[:, lanes_b], taps_ref, lanes_b, mask_ref)
    _, pre_c = conv_parts(ci_ref[:, lanes_c], taps_ref, lanes_c, mask_ref)
    score_setup(
        pre_b * sigmoid(pre_b), pre_c * sigmoid(pre_c),
        segb_ref, segr, None, so_ref, sdt_ref, sot_ref,
    )
    dsdt_ref[...] = jnp.zeros_like(dsdt_ref)
    dso_ref[...] = jnp.zeros_like(dso_ref)
    acc_ref[...] = jnp.zeros_like(acc_ref)

    def body(t, carry):
        lanes = pl.ds(pl.multiple_of(t * BLK, BLK), BLK)
        x = ci_ref[:, lanes]
        v = v_ref[:, lanes]
        low = iota((1, BLK), 1) < BLK // 2
        st2, ew2, wq2, al2, c2, r2, skip = pair_setup(t, heads_ref, wide_ref, cc_ref, cct_ref)
        vtb = (v * st2).astype(BF16)
        vpb = (v * wq2).astype(BF16)
        g = g_ref[:, lanes]
        gb = g.astype(BF16)
        gpb = (al2 * g).astype(BF16)
        dskip_ref[:, lanes] = jnp.sum(g * v, axis=0, keepdims=True)
        k_row = iota((3 * BLK, BLK), 0)
        target = jnp.where(k_row >= 2 * BLK, BLK // 2, 0) + 2 * t
        target = target + jnp.where((k_row & (BLK - 1)) >= BLK // 2, 1, 0)
        collect = (iota((3 * BLK, BLK), 1) == target).astype(F32).astype(BF16)
        for i in range(blocks):
            rows = slice(i * BLK, (i + 1) * BLK)
            before = slice((i - 1) * BLK, i * BLK)
            after = slice((i + 1) * BLK, (i + 2) * BLK)
            gdiag = block_diag(gb[rows], low)
            both = mm_nt(vtb[rows], gdiag)
            ms = []
            part = jnp.zeros((BLK, BLK), F32)
            for k in range(2):
                row = r2[k : k + 1, rows]
                d = jnp.exp2(jnp.minimum(row - c2[rows, k : k + 1], 0.0))
                ms.append((sdt_ref[i] * d).astype(BF16))
                part = part + both[:, k * BLK : (k + 1) * BLK] * d
            dsdt_ref[i] += part
            dvt = mm(jnp.concatenate(ms, axis=1), gdiag)
            x1 = gb[rows].astype(F32) * yd_ref[rows, lanes] - dvt * vtb[rows].astype(F32)
            dv = st2[rows] * dvt + skip * g[rows]
            dstep = dvt
            if i > 0:
                z = mm(so_ref[i], vpb[before])
                x1 = x1 + gpb[rows].astype(F32) * z
                dso_ref[i] += mm_nt(gpb[rows], vpb[before])
            if i + 1 < blocks:
                dvp = mm(sot_ref[i + 1], gpb[after])
                x1 = x1 - dvp * vpb[rows].astype(F32)
                dv = dv + wq2[rows] * dvp
                dstep = dstep + ew2[rows] * dvp
            h1, l1 = split2(x1)
            h2 = (dstep * v[rows]).astype(BF16)
            acc_ref[rows, :] += mm(jnp.concatenate([h1, l1, h2], axis=1), collect)
            dpre_ref[rows, :] = dv * slope_ref[rows, lanes]
        conv_back(dpre_ref[...], x, taps_ref, lanes, mask_ref, dtaps_ref, dp_ref, lanes)
        return carry

    lax.fori_loop(0, inner // BLK, body, 0)
    xb, xc = ci_ref[:, lanes_b], ci_ref[:, lanes_c]
    _, pre_b = conv_parts(xb, taps_ref, lanes_b, mask_ref)
    _, pre_c = conv_parts(xc, taps_ref, lanes_c, mask_ref)
    bmat, slope_b = silu_and_slope(pre_b)
    cmat, slope_c = silu_and_slope(pre_c)
    bb, cb = bmat.astype(BF16), cmat.astype(BF16)
    causal_t = iota((BLK, BLK), 1) >= iota((BLK, BLK), 0)
    upper = causal_t.astype(F32)
    dst, dso = [], [None]
    for i in range(blocks):
        rows = slice(i * BLK, (i + 1) * BLK)
        before = slice((i - 1) * BLK, i * BLK)
        same = (segb_ref[rows, :] == segr[:, rows]) & causal_t
        dst.append(jnp.where(same, dsdt_ref[i], 0.0))
        if i > 0:
            linked = segb_ref[rows, :] == segr[:, before]
            dso.append(jnp.where(linked, dso_ref[i], 0.0))
    for i in range(blocks):
        rows = slice(i * BLK, (i + 1) * BLK)
        before = slice((i - 1) * BLK, i * BLK)
        after = slice((i + 1) * BLK, (i + 2) * BLK)
        dc = mm(dst[i].T.astype(BF16), bb[rows])
        if i > 0:
            dc = dc + mm(dso[i].astype(BF16), bb[before])
        dpre_ref[rows, :] = dc * slope_c[rows]
    conv_back(dpre_ref[...], xc, taps_ref, lanes_c, mask_ref, dtaps_ref, dp_ref, lanes_c)
    for i in range(blocks):
        rows = slice(i * BLK, (i + 1) * BLK)
        after = slice((i + 1) * BLK, (i + 2) * BLK)
        db = mm(dst[i].astype(BF16), cb[rows])
        if i + 1 < blocks:
            db = db + mm(dso[i + 1].T.astype(BF16), cb[after])
        dpre_ref[rows, :] = db * slope_b[rows]
    conv_back(dpre_ref[...], xb, taps_ref, lanes_b, mask_ref, dtaps_ref, dp_ref, lanes_b)

    decay = jnp.exp(heads_ref[0:1, :])
    later = jnp.zeros((1, BLK), F32)
    dalog = jnp.zeros((1, BLK), F32)
    dbias = jnp.zeros((1, BLK), F32)
    for i in reversed(range(blocks)):
        rows = slice(i * BLK, (i + 1) * BLK)
        dcum = acc_ref[rows, :]
        drate = later + jnp.dot(upper, dcum, precision=HIGH, preferred_element_type=F32)
        later = drate[0:1, :]
        step = step_ref[rows, :]
        dalog = dalog - jnp.sum(drate * step, axis=0, keepdims=True) * decay
        dstep = pltpu.roll(dcum, BLK // 2, axis=1) - drate * decay
        ddt = dstep * sigmoid(dt_ref[rows, :] + heads_ref[2:3, :])
        dbias = dbias + jnp.sum(ddt, axis=0, keepdims=True)
        dp_ref[rows, channels:] = jnp.where(iota((1, BLK), 1) < nheads, ddt, 0.0).astype(BF16)
    dheads_ref[0:1, :] = dalog
    dheads_ref[1:2, :] = dbias


def grad_in_kernel(xn_ref, dp_ref, lo_ref, hi_ref):
    grad = mm_tn(xn_ref[...], dp_ref[...]).astype(BF16)
    half = grad.shape[0] // 2
    lo_ref[...] = grad[:half]
    hi_ref[...] = grad[half:]


def input_kernel(
    wc_ref, dng_ref, dp_ref, me_ref, tab_ref, hid_ref, cot_ref, gains_ref,
    dtaps_ref, ginner_ref, dskip_ref, dheads_ref,
    ig_ref, sums_ref,
):
    dn = mm_nt(dp_ref[...], wc_ref[...]) + dng_ref[...]
    perm = perm_matrix(me_ref[0], tab_ref, dn.shape[1])
    hi, lo = split2(dn)
    dn = mm_nt(hi, perm) + mm_nt(lo, perm)
    tokens = hid_ref[...].astype(F32)
    scale = lax.rsqrt(jnp.mean(tokens * tokens, axis=-1, keepdims=True) + 1e-05)
    unit = tokens * scale
    width = tokens.shape[1]
    sums_ref[...] = jnp.zeros_like(sums_ref)
    sums_ref[0:5, : dtaps_ref.shape[1]] = dtaps_ref[0:5, :]
    sums_ref[5:6, :width] = jnp.sum(dn * unit, axis=0, keepdims=True)
    sums_ref[5:6, width:] = jnp.sum(ginner_ref[...], axis=0, keepdims=True)
    inner_n = dskip_ref.shape[1]
    lane = iota((inner_n, BLK), 1) * (BLK // 2)
    channel = iota((inner_n, BLK), 0)
    group = ((channel >= lane) & (channel < lane + BLK // 2)).astype(F32)
    sums_ref[6:7, :BLK] = jnp.dot(dskip_ref[...], group, precision=HIGH, preferred_element_type=F32)
    sums_ref[7:8, :BLK] = dheads_ref[0:1, :]
    sums_ref[7:8, BLK : 2 * BLK] = dheads_ref[1:2, :]
    dunit = dn * gains_ref[:, :width]
    inner = jnp.mean(unit * dunit, axis=-1, keepdims=True)
    ig_ref[...] = cot_ref[...].astype(F32) + scale * (dunit - unit * inner)


def stack_kernel(*refs):
    rows = jnp.concatenate([ref[...].astype(F32) for ref in refs[:-1]], axis=0)
    refs[-1][...] = rows.astype(BF16)


def fold_kernel(count, *refs):
    total = refs[0][...].astype(F32)
    for ref in refs[1:count]:
        total = total + ref[...].astype(F32)
    size = total.shape[0] // len(refs[count:])
    for k, ref in enumerate(refs[count:]):
        ref[...] = total[k * size : (k + 1) * size].astype(ref.dtype)


def last_out_kernel(a_ref, b_ref, c_ref, d_ref, gate_ref, out_ref):
    total = a_ref[...].astype(F32) + b_ref[...].astype(F32) + c_ref[...].astype(F32) + d_ref[...].astype(F32)
    inner = gate_ref.shape[1]
    rows, width = a_ref.shape[0], out_ref.shape[1]
    gate_ref[...] = total[:, :inner]
    out_ref[:rows, :] = total[:, inner : inner + width]
    out_ref[rows:, :] = total[:, inner + width :]


def last_in_kernel(a_ref, b_ref, c_ref, d_ref, gate_ref, in_ref):
    total = a_ref[...].astype(F32) + b_ref[...].astype(F32) + c_ref[...].astype(F32) + d_ref[...].astype(F32)
    inner = gate_ref.shape[1]
    in_ref[:, :inner] = gate_ref[...]
    in_ref[:, inner:] = total[:, : in_ref.shape[1] - inner]


def ends_kernel(me_ref, *refs):
    taps_ref, gains_ref, alog_ref, skip_ref, bias_ref = refs[-5:]
    parts = [ref[...] for ref in refs[:-5]]
    sums = parts[0] + parts[1]
    if len(parts) == 4:
        sums = sums + (parts[2] + parts[3])
    me, width = me_ref[0], sums.shape[1]
    taps_n, tap_share = taps_ref.shape
    gain_share, nheads = gains_ref.shape[1], alog_ref.shape[1]
    taps_ref[...] = pltpu.roll(sums, lax.rem(width - me * tap_share, width), axis=1)[:taps_n, :tap_share]
    gains_ref[...] = pltpu.roll(sums, lax.rem(width - me * gain_share, width), axis=1)[taps_n : taps_n + 1, :gain_share]
    skip_ref[...] = sums[6:7, :nheads]
    alog_ref[...] = sums[7:8, :nheads]
    bias_ref[...] = sums[7:8, BLK : BLK + nheads]


def sds(shape, dtype):
    return jax.ShapeDtypeStruct(shape, dtype)


def held(shape, dtype):
    return pltpu.VMEM(shape, dtype)


def scan_scratch(length, inner, taps):
    nheads = -(-2 * inner // (8 * BLK)) * 8
    return [
        pltpu.VMEM((8, BLK), F32), pltpu.VMEM((length, BLK), F32), pltpu.VMEM((length, BLK), F32),
        pltpu.VMEM((3, length, 2 * BLK), BF16), pltpu.VMEM((nheads, length), F32), pltpu.VMEM((length, BLK), F32),
        pltpu.VMEM((taps - 1, length, BLK), F32),
    ]


def scan_fwd(weights, packed, taps_n, widths, mine, tab, hidden, first, second, segr, *heads):
    length, width = hidden.shape
    channels, inner = widths
    blocks = length // BLK
    count = len(weights)
    rows = held((length, inner), F32)
    return call(
        lambda *refs: scan_fwd_kernel(count, packed, *refs),
        (
            held((length, width), BF16), held((8, channels), F32), held((1, width + inner), F32),
            held((width, channels + BLK), BF16),
            held((length, channels), F32), held((length, BLK), F32), rows, rows, rows, rows,
        ),
        *weights, mine, tab, hidden, first, second, segr, *heads, scalar=count,
        leave=(tab, first, second, segr) + heads,
        scratch=scan_scratch(length, inner, taps_n - 1) + [
            pltpu.VMEM((blocks, BLK, BLK), F32),
            pltpu.VMEM((blocks, BLK, BLK), BF16),
        ],
    )


def scan_bwd(taps_n, g, yd, v, slope, ci, dt, taps, segr, *heads):
    length, channels = ci.shape
    inner = g.shape[1]
    score = (length // BLK, BLK, BLK)
    return call(
        scan_bwd_kernel,
        (
            held((length, channels + BLK), BF16), held(taps.shape, F32), held((1, inner), F32),
            held((8, BLK), F32),
        ),
        g, yd, v, slope, ci, dt, taps, segr, *heads, leave=(segr,) + heads,
        scratch=scan_scratch(length, inner, taps_n - 1) + [
            pltpu.VMEM(score, F32),
            pltpu.VMEM(score, BF16),
            pltpu.VMEM(score, BF16),
            pltpu.VMEM(score, F32),
            pltpu.VMEM(score, F32),
            pltpu.VMEM((length, BLK), F32),
            pltpu.VMEM((length, BLK), F32),
        ],
    )


def call(kernel, outs, *ins, scratch=(), scalar=None, leave=()):
    specs = [
        pl.BlockSpec(memory_space=pltpu.SMEM if k == scalar else pltpu.VMEM) for k in range(len(ins))
    ]
    near = [
        a if k == scalar else pltpu.with_memory_space_constraint(a, pltpu.HBM if any(a is b for b in leave) else pltpu.VMEM)
        for k, a in enumerate(ins)
    ]
    many = isinstance(outs, (tuple, list))
    out_specs = [pl.BlockSpec(memory_space=pltpu.VMEM) for _ in outs] if many else pl.BlockSpec(memory_space=pltpu.VMEM)
    return pl.pallas_call(
        kernel, out_shape=outs, in_specs=specs, out_specs=out_specs, scratch_shapes=list(scratch),
        compiler_params=pltpu.CompilerParams(vmem_limit_bytes=(20 if scratch else 8) * 1024 * 1024),
    )(*near)


def stages(devices):
    masks = [1 << b for b in range(devices.bit_length() - 1)]
    groups = []
    for end in range(len(masks), 1, -2):
        part = masks[max(end - 2, 1) : end]
        groups.append(part if len(part) == 1 else [part[0], part[1], part[0] | part[1]])
    return groups + [masks[:1]]


def order_table(devices):
    table = np.zeros((1,), np.int32)
    for group in stages(devices):
        table = np.concatenate([table] + [table ^ m for m in group])
    return table


def send(x, devices, mask):
    return lax.ppermute(x, "fsdp", [(i, i ^ mask) for i in range(devices)])


def send_all(parts, devices, stage):
    return [send(part, devices, m) for part, m in zip(parts, stages(devices)[stage])]


def stack(pieces, leave):
    size, rest = pieces[0].shape[0], pieces[0].shape[1:]
    if size % 8 or len(rest) != 1:
        return jnp.concatenate(pieces, axis=0)
    return call(stack_kernel, held((len(pieces) * size,) + rest, BF16), *pieces, leave=leave)


def gather(x, devices, leave=()):
    groups = stages(devices)
    core = len(groups) - 1
    pieces = [x]
    for stage in range(core):
        x = pieces[0] if len(pieces) == 1 else stack(pieces, leave)
        pieces = [x] + send_all([x] * len(groups[stage]), devices, stage)
    return pieces + [send(a, devices, 1) for a in pieces]


def fold(parts, fan, dtype):
    rows, cols = parts[0].shape
    size = rows // fan
    if size % 8:
        total = sum(part.astype(F32) for part in parts).astype(dtype)
        return [total[k * size : (k + 1) * size] for k in range(fan)]
    count = len(parts)
    return call(lambda *refs: fold_kernel(count, *refs), tuple(held((size, cols), dtype) for _ in range(fan)), *parts)


def reduce_shares(lo, hi, devices):
    groups = stages(devices)
    parts = [lo, hi]
    for stage in reversed(range(len(groups))):
        parts = [parts[0]] + send_all(parts[1:], devices, stage)
        if stage:
            parts = fold(parts, len(groups[stage - 1]) + 1, BF16)
    return parts


def total_of(x, devices):
    for stage in reversed(range(len(stages(devices)))):
        group = stages(devices)[stage]
        got = send_all([x] * len(group), devices, stage)
        if stage == 0:
            return [x] + got
        x = x + got[0] if len(got) == 1 else (x + got[0]) + (got[1] + got[2])


def layer(
    hidden, segment_ids, cot, w_in, w_out, conv_taps, gains, a_log, d_skip, dt_bias
):
    length = segment_ids.shape[1]
    width = hidden.shape[1]
    devices = lax.axis_size("fsdp")
    me = lax.axis_index("fsdp")
    nheads = a_log.shape[0]
    taps_n, tap_share = conv_taps.shape
    channels = tap_share * devices
    gain_share = gains.shape[0]
    inner = w_out.shape[0] * devices
    proj = w_in.shape[1]
    rows_in, rows_out = w_in.shape[0], w_out.shape[0]
    pairs = inner // BLK
    first = pairs // 2

    table = order_table(devices)
    inverse = np.argsort(table).astype(np.int32)
    order = jnp.asarray(table) ^ me
    place = jnp.asarray(inverse)[me ^ jnp.arange(devices)]
    mine = me.reshape(1).astype(jnp.int32)
    tab = np.zeros((8, width), np.int32)
    tab[0], tab[1], tab[2] = np.repeat(table, rows_in), np.tile(np.arange(rows_in), devices), rows_in
    tab = jnp.asarray(tab)

    spare = BLK - (proj - inner - channels)
    packed = rows_in > taps_n and max(tap_share, gain_share) <= spare
    if packed:
        gain_row = gains.reshape(1, gain_share)
        w_conv, w_gate = call(
            lambda *refs: pack_kernel(inner, *refs),
            (held((rows_in, channels + BLK), BF16), held((rows_in, inner), BF16)),
            w_in, conv_taps, gain_row, leave=(w_in, conv_taps, gain_row),
        )
    else:
        w_conv = jnp.pad(w_in[:, inner:], ((0, 0), (0, spare)))
        w_gate = w_in[:, :inner]
    cw = gather(w_conv, devices)
    gw = gather(w_gate, devices)
    ow = gather(w_out, devices, (w_out,))
    count = len(cw)

    heads = [x.reshape(1, nheads) for x in (a_log, d_skip, dt_bias)]

    if packed:
        at = np.arange(width + inner)
        where = np.stack([at % tap_share, at // tap_share, at % gain_share, at // gain_share])
        second = jnp.asarray(np.pad(where, ((0, 4), (0, 0))).astype(np.int32))
        first = jnp.asarray(table.reshape(devices, 1))
    else:
        small = jnp.zeros((8, BLK), F32)
        small = small.at[:taps_n, :tap_share].set(conv_taps.astype(F32))
        small = small.at[taps_n, :gain_share].set(gains.astype(F32))
        rows = jnp.concatenate(gather(small[None], devices), axis=0)[place]
        first = jnp.moveaxis(rows[:, :, :tap_share], 0, 1).reshape(8, channels)
        second = rows[:, taps_n, :gain_share].reshape(1, width + inner)
    xn, taps, gains_all, wc, ci, dt, sc, yd, v, slope = scan_fwd(
        cw, (proj - inner - channels, taps_n) if packed else None, taps_n, (channels, inner),
        mine, tab, hidden, first, second, segment_ids, *heads,
    )
    if rows_out % 16:
        wo_all = jnp.concatenate(ow, axis=0).reshape(devices, rows_out, width)[place].reshape(inner, width)
        ow = [wo_all[k * (inner // count) : (k + 1) * (inner // count)] for k in range(count)]
    aligned = rows_in % 8 == 0
    if aligned:
        halves = (held((width // 2, inner + 2 * width), BF16), held((width // 2, inner + 2 * width), BF16))
    else:
        halves = (sds((width, inner), BF16), sds((inner, width), BF16))
    lo, hi, g, dgate, mixed, ginner, wo, wg = call(
        lambda *refs: mid_kernel(count, table, *refs),
        halves + (
            held((length, inner), F32), held((length, inner), BF16), held((length, inner), BF16),
            held((8, inner), F32), held((inner, width), BF16), held((width, inner), BF16),
        ),
        *gw, *ow, mine, xn, sc, gains_all, cot,
        scratch=(
            pltpu.VMEM((length, inner), F32), pltpu.VMEM((inner, width), F32),
        ),
        scalar=2 * count,
    )
    if not aligned:
        gwo = hi.reshape(devices, 2, rows_in, width)[order]
        both = jnp.concatenate([lo, gwo[:, 0].reshape(width, width), gwo[:, 1].reshape(width, width)], axis=1)
        lo, hi = both[: width // 2], both[width // 2 :]
    mid_parts = reduce_shares(lo, hi, devices)
    output, dng = call(
        branch_kernel, (sds((length, width), BF16), held((length, width), F32)),
        mixed, wo, hidden, dgate, wg,
    )
    dp, dtaps, dskip, dheads = scan_bwd(taps_n, g, yd, v, slope, ci, dt, taps, segment_ids, *heads)
    half = held((width // 2, dp.shape[1]), BF16)
    clo, chi = call(grad_in_kernel, (half, half), xn, dp)
    conv_parts_in = reduce_shares(clo, chi, devices)
    input_grad, sums = call(
        input_kernel,
        (sds((length, width), F32), held((8, width + inner), F32)),
        wc, dng, dp, mine, tab, hidden, cot, gains_all, dtaps, ginner, dskip, dheads, scalar=3, leave=(tab,),
    )
    if aligned and len(mid_parts) == 4:
        gate_share, out_share = call(
            last_out_kernel,
            (sds((rows_in, inner), F32), sds((rows_out, width), F32)), *mid_parts,
        )
        in_share = call(last_in_kernel, sds((rows_in, proj), F32), *conv_parts_in, gate_share)
    else:
        total = sum(part.astype(F32) for part in mid_parts)
        out_share = jnp.concatenate([total[:, inner : inner + width], total[:, inner + width :]], axis=0)
        conv_total = sum(part.astype(F32) for part in conv_parts_in)
        in_share = jnp.concatenate([total[:, :inner], conv_total], axis=1)[:, :proj]

    sums = total_of(sums, devices)
    one = sds((1, nheads), F32)
    taps_share, gains_share, d_alog, d_dskip, d_bias = call(
        ends_kernel, (sds((taps_n, tap_share), F32), sds((1, gain_share), F32), one, one, one),
        mine, *sums, scalar=0,
    )
    return (
        output, input_grad, in_share, out_share, taps_share, gains_share.reshape(gain_share),
        d_alog.reshape(nheads), d_dskip.reshape(nheads), d_bias.reshape(nheads),
    )


def solution(mesh):
    axis = P("fsdp")
    rows = P("fsdp", None)
    cols = P(None, "fsdp")
    return jax.shard_map(
        layer,
        mesh=mesh,
        in_specs=(rows, rows, rows, rows, rows, cols, axis, P(), P(), P()),
        out_specs=(rows, rows, rows, rows, cols, axis, P(), P(), P()),
        check_vma=False,
    )
```

```python
import jax
import jax.numpy as jnp
import numpy as np
from jax import lax
from jax.experimental import pallas as pl
from jax.experimental.pallas import tpu as pltpu
from jax.sharding import PartitionSpec as P


BLK = 128
LOG2E = 1.4426950408889634
F32 = jnp.float32
BF16 = jnp.bfloat16
HIGH = lax.Precision.HIGHEST


def mm(a, b):
    return lax.dot_general(a, b, (((1,), (0,)), ((), ())), preferred_element_type=F32)


def mm_nt(a, b):
    return lax.dot_general(a, b, (((1,), (1,)), ((), ())), preferred_element_type=F32)


def mm_tn(a, b):
    return lax.dot_general(a, b, (((0,), (0,)), ((), ())), preferred_element_type=F32)


def split2(x):
    hi = x.astype(BF16)
    return hi, (x - hi.astype(F32)).astype(BF16)


def iota(shape, dim):
    return lax.broadcasted_iota(jnp.int32, shape, dim)


def perm_matrix(me, tab_ref, width):
    dvec = (tab_ref[0:1, :] ^ me) * tab_ref[2:3, 0:1] + tab_ref[1:2, :]
    return (iota((width, width), 0) == dvec).astype(F32).astype(BF16)


def rows_of(refs, lanes=slice(None)):
    return jnp.concatenate([ref[:, lanes] for ref in refs], axis=0)


def normed_of(hid_ref, gain, me, tab_ref, xn_ref):
    tokens = hid_ref[...].astype(F32)
    scale = lax.rsqrt(jnp.mean(tokens * tokens, axis=-1, keepdims=True) + 1e-05)
    normed = (tokens * scale * gain).astype(BF16)
    perm = perm_matrix(me, tab_ref, tokens.shape[1])
    xn_ref[...] = mm(normed, perm).astype(BF16)


def pack_kernel(inner, w_ref, taps_in, gains_in, conv_ref, gate_ref):
    gate_ref[...] = w_ref[:, :inner]
    body = conv_ref.shape[1] - BLK
    conv_ref[:, :body] = w_ref[:, inner : inner + body]
    tail = w_ref[:, inner + body :]
    spare = tail.shape[1]
    rows, taps_n = w_ref.shape[0], taps_in.shape[0]

    def onto(x, at):
        return mm(x, (iota((x.shape[1], BLK), 1) == iota((x.shape[1], BLK), 0) + at).astype(F32).astype(BF16))

    row = iota((rows, BLK), 0)
    tile_of = onto(tail, 0)
    taps_wide, gains_wide = onto(taps_in[...], spare), onto(gains_in[...], spare)
    for j in range(taps_n):
        tile_of = tile_of + jnp.where(row == j, taps_wide[j : j + 1, :], 0.0)
    tile_of = tile_of + jnp.where(row == taps_n, gains_wide, 0.0)
    conv_ref[:, body:] = tile_of.astype(BF16)


def unpack(at, taps_n, pieces, me, owner_ref, where_ref, taps_ref, gains_ref):
    last = pieces[0].shape[1] - BLK
    tail = rows_of(pieces, slice(last, last + BLK))
    devices = owner_ref.shape[0]
    rows_in = tail.shape[0] // devices
    row = iota((8 * devices, tail.shape[0]), 0)
    bits = devices.bit_length() - 1
    source = (row & (devices - 1)) * rows_in + lax.shift_right_logical(row, bits)
    pick = (iota(row.shape, 1) == source).astype(F32).astype(BF16)
    small = mm(pick, tail).astype(BF16)

    def spread(part, line, width):
        lane, owner = where_ref[line : line + 1, :width], where_ref[line + 1 : line + 2, :width]
        chosen = (iota((BLK, width), 0) == lane + at).astype(F32).astype(BF16)
        wide = mm(part, chosen)
        return jnp.sum(jnp.where((owner_ref[...] ^ me) == owner, wide, 0.0), axis=0, keepdims=True)

    channels, width = taps_ref.shape[1], gains_ref.shape[1]
    taps_ref[...] = jnp.zeros_like(taps_ref)
    for j in range(taps_n):
        taps_ref[j : j + 1, :] = spread(small[j * devices : (j + 1) * devices], 0, channels)
    gains_ref[...] = spread(small[taps_n * devices : (taps_n + 1) * devices], 2, width)


def head_setup(dt_raw, rows_in, segr, heads_ref, step_ref, cc_ref, wide_ref, cct_ref, segb_ref):
    length = dt_raw.shape[0]
    heads_ref[...] = jnp.zeros_like(heads_ref)
    for k, ref in enumerate(rows_in):
        heads_ref[k : k + 1, : ref.shape[1]] = ref[...]
    segb_ref[...] = jnp.broadcast_to(segr, (BLK, length)).T
    biased = dt_raw + heads_ref[2:3, :]
    step = jnp.maximum(biased, 0.0) + jnp.log1p(jnp.exp(-jnp.abs(biased)))
    step_ref[...] = step
    rate = step * (jnp.exp(heads_ref[0:1, :]) * (-LOG2E))
    lower = (iota((BLK, BLK), 0) >= iota((BLK, BLK), 1)).astype(F32)
    for i in range(length // BLK):
        rows = slice(i * BLK, (i + 1) * BLK)
        cc = jnp.dot(lower, rate[rows], precision=HIGH, preferred_element_type=F32)
        cc_ref[rows, :] = cc
        ew = jnp.exp2(jnp.minimum(cc[BLK - 1 : BLK, :] - cc, 0.0))
        for k, x in enumerate((step[rows], ew, jnp.exp2(cc))):
            wide_ref[k, rows, :] = jnp.concatenate(split2(x), axis=1)
        cct_ref[:, rows] = cc.T[: cct_ref.shape[0]]


def mask_setup(segb_ref, mask_ref):
    segb = segb_ref[...]
    pos = iota(segb.shape, 0)
    for j in range(1, mask_ref.shape[0] + 1):
        prev = pltpu.roll(segb, j, axis=0)
        mask_ref[j - 1] = ((prev == segb) & (pos >= j)).astype(F32)


def conv_parts(x, taps_ref, lanes, mask_ref):
    kernel = mask_ref.shape[0] + 1
    shifts = [x] + [pltpu.roll(x, j, axis=0) * mask_ref[j - 1] for j in range(1, kernel)]
    pre = taps_ref[kernel : kernel + 1, lanes] + taps_ref[kernel - 1 : kernel, lanes] * x
    for j in range(1, kernel):
        pre = pre + taps_ref[kernel - 1 - j : kernel - j, lanes] * shifts[j]
    return shifts, pre


def sigmoid(x):
    return 0.5 * jnp.tanh(0.5 * x) + 0.5


def score_setup(bmat, cmat, segb_ref, segr, sd_ref, so_ref, sdt_ref, sot_ref):
    length = bmat.shape[0]
    bb, cb = bmat.astype(BF16), cmat.astype(BF16)
    causal = iota((BLK, BLK), 0) >= iota((BLK, BLK), 1)
    for i in range(length // BLK):
        rows = slice(i * BLK, (i + 1) * BLK)
        before = slice((i - 1) * BLK, i * BLK)
        same = (segb_ref[rows, :] == segr[:, rows]) & causal
        diag = jnp.where(same, mm_nt(cb[rows], bb[rows]), 0.0)
        if sd_ref is not None:
            sd_ref[i] = diag
        if sdt_ref is not None:
            sdt_ref[i] = diag.T
        if i > 0:
            linked = segb_ref[rows, :] == segr[:, before]
            off = jnp.where(linked, mm_nt(cb[rows], bb[before]), 0.0)
            so_ref[i] = off.astype(BF16)
            if sot_ref is not None:
                sot_ref[i] = off.T.astype(BF16)


def pair_setup(t, heads_ref, wide_ref, cc_ref, cct_ref):
    head = iota((2 * BLK, BLK), 0) & (BLK - 1)
    pick = (head == 2 * t + jnp.where(iota((2 * BLK, BLK), 1) < BLK // 2, 0, 1)).astype(F32).astype(BF16)
    st2, ew2, al2 = [mm(wide_ref[k], pick) for k in range(3)]
    c2 = pltpu.roll(cc_ref[...], lax.rem(BLK - 2 * t, BLK), axis=1)
    r2 = pltpu.roll(cct_ref[...], lax.rem(cct_ref.shape[0] - 2 * t, cct_ref.shape[0]), axis=0)
    h2 = pltpu.roll(heads_ref[...], lax.rem(BLK - 2 * t, BLK), axis=1)
    skip = jnp.where(iota((1, BLK), 1) < BLK // 2, h2[1:2, 0:1], h2[1:2, 1:2])
    return st2, ew2, ew2 * st2, al2, c2, r2, skip


def block_diag(x, low):
    zero = jnp.zeros_like(x)
    return jnp.concatenate([jnp.where(low, x, zero), jnp.where(low, zero, x)], axis=0)


def scan_fwd_kernel(pieces, packed, *refs):
    w_refs = refs[:pieces]
    (
        me_ref, tab_ref, hid_ref, first_ref, second_ref, segr_ref, alog_ref, skip_ref, bias_ref,
        xn_ref, taps_ref, gains_ref, wc_ref, ci_ref, dt_ref, sc_ref, yd_ref, v_ref, slope_ref,
        heads_ref, step_ref, cc_ref, wide_ref, cct_ref, segb_ref, mask_ref, sd_ref, so_ref,
    ) = refs[pieces:]
    me = me_ref[0]
    segr = segr_ref[...].astype(F32)
    length = xn_ref.shape[0]
    channels = ci_ref.shape[1]
    states = BLK
    inner = channels - 2 * states
    if packed:
        unpack(packed[0], packed[1], w_refs, me, first_ref, second_ref, taps_ref, gains_ref)
    else:
        taps_ref[...] = first_ref[...]
        gains_ref[...] = second_ref[...]
    normed_of(hid_ref, gains_ref[:, : hid_ref.shape[1]], me, tab_ref, xn_ref)
    xn = xn_ref[...]
    wc_ref[...] = rows_of(w_refs)
    ci_ref[...] = mm(xn, wc_ref[:, :channels])
    dt_ref[...] = mm(xn, wc_ref[:, channels:])
    head_setup(
        dt_ref[...], (alog_ref, skip_ref, bias_ref), segr, heads_ref, step_ref, cc_ref, wide_ref, cct_ref, segb_ref
    )
    mask_setup(segb_ref, mask_ref)
    lanes_b = slice(inner, inner + states)
    lanes_c = slice(inner + states, channels)
    _, pre_b = conv_parts(ci_ref[:, lanes_b], taps_ref, lanes_b, mask_ref)
    _, pre_c = conv_parts(ci_ref[:, lanes_c], taps_ref, lanes_c, mask_ref)
    score_setup(
        pre_b * sigmoid(pre_b), pre_c * sigmoid(pre_c),
        segb_ref, segr, sd_ref, so_ref, None, None,
    )

    def body(t, carry):
        lanes = pl.ds(pl.multiple_of(t * BLK, BLK), BLK)
        _, pre = conv_parts(ci_ref[:, lanes], taps_ref, lanes, mask_ref)
        v, slope = silu_and_slope(pre)
        v_ref[:, lanes] = v
        slope_ref[:, lanes] = slope
        low = iota((1, BLK), 1) < BLK // 2
        st2, _, wq2, al2, c2, r2, skip = pair_setup(t, heads_ref, wide_ref, cc_ref, cct_ref)
        vt = (v * st2).astype(BF16)
        vp = (v * wq2).astype(BF16)
        for i in range(length // BLK):
            rows = slice(i * BLK, (i + 1) * BLK)
            before = slice((i - 1) * BLK, i * BLK)
            ms = []
            for k in range(2):
                row = r2[k : k + 1, rows]
                d = jnp.exp2(jnp.minimum(c2[rows, k : k + 1] - row, 0.0))
                ms.append((sd_ref[i] * d).astype(BF16))
            yd = mm(jnp.concatenate(ms, axis=1), block_diag(vt[rows], low))
            yd_ref[rows, lanes] = yd
            y = yd + skip * v[rows]
            if i > 0:
                y = y + al2[rows] * mm(so_ref[i], vp[before])
            sc_ref[rows, lanes] = y
        return carry

    lax.fori_loop(0, inner // BLK, body, 0)


def gate_kernel(pieces, *refs):
    xn_ref, gate_ref, wg_ref = refs[pieces:]
    wg_ref[...] = rows_of(refs[:pieces])
    gate_ref[...] = mm(xn_ref[...], wg_ref[...])


def mid_kernel(pieces, table, *refs):
    ow_refs = refs[:pieces]
    (
        me_ref, xn_ref, gate_ref, sc_ref, gains_ref, cot_ref,
        lo_ref, hi_ref, g_ref, dgate_ref, mixed_ref, ginner_ref, wo_ref,
        dm_ref, nat_ref,
    ) = refs[pieces:]
    me = me_ref[0]
    devices = len(table)
    share = wo_ref.shape[0] // devices
    per = ow_refs[0].shape[0] // share
    gain = slice(xn_ref.shape[1], gains_ref.shape[1])
    inner = sc_ref.shape[1]
    width = cot_ref.shape[1]
    rows_in = xn_ref.shape[1] // devices
    xn = xn_ref[...]
    if share % 16:
        wo_ref[...] = rows_of(ow_refs)
    else:
        for p in range(devices):
            at = pl.multiple_of((me ^ int(table[p])) * share, 16)
            row = (p % per) * share
            wo_ref[pl.ds(at, share), :] = ow_refs[p // per][row : row + share, :]
    dm_ref[...] = mm_nt(cot_ref[...], wo_ref[...])
    length = xn_ref.shape[0]
    sub = 32
    ginner_ref[...] = jnp.zeros_like(ginner_ref)

    def body(k, carry):
        rows = pl.ds(pl.multiple_of(k * sub, sub), sub)
        gate = gate_ref[rows, :]
        sig = sigmoid(gate)
        silu = gate * sig
        scanned = sc_ref[rows, :]
        gated = scanned * silu
        scale = lax.rsqrt(jnp.mean(gated * gated, axis=-1, keepdims=True) + 1e-05)
        dm = dm_ref[rows, :]
        unit = gated * scale
        mixed_ref[rows, :] = (unit * gains_ref[:, gain]).astype(BF16)
        ginner_ref[...] += jnp.sum((dm * unit).reshape(sub // 8, 8, -1), axis=0)
        dunit = dm * gains_ref[:, gain]
        dot = jnp.mean(unit * dunit, axis=-1, keepdims=True)
        du = scale * (dunit - unit * dot)
        g_ref[rows, :] = du * silu
        dgate_ref[rows, :] = (du * scanned * (sig * (1.0 + gate * (1.0 - sig)))).astype(BF16)
        return carry

    lax.fori_loop(0, length // sub, body, 0)
    if rows_in % 8:
        lo_ref[...] = mm_tn(xn, dgate_ref[...]).astype(BF16)
        hi_ref[...] = mm_tn(mixed_ref[...], cot_ref[...]).astype(BF16)
        return
    gg = mm_tn(xn, dgate_ref[...]).astype(BF16)
    half = gg.shape[0] // 2
    lo_ref[:, :inner] = gg[:half]
    hi_ref[:, :inner] = gg[half:]
    nat_ref[...] = mm_tn(mixed_ref[...], cot_ref[...])
    for p in range(0, devices, 2):
        target = lo_ref if p < devices // 2 else hi_ref
        row = (p % (devices // 2)) * rows_in
        for k in range(2):
            both = [
                nat_ref[pl.ds(pl.multiple_of((me ^ int(table[q])) * share + k * rows_in, 8), rows_in), :]
                for q in (p, p + 1)
            ]
            lanes = slice(inner + k * width, inner + (k + 1) * width)
            target[row : row + 2 * rows_in, lanes] = jnp.concatenate(both, axis=0).astype(BF16)


def branch_kernel(mixed_ref, wo_ref, hid_ref, dgate_ref, wg_ref, out_ref, dn_ref):
    out_ref[...] = (hid_ref[...].astype(F32) + mm(mixed_ref[...], wo_ref[...])).astype(BF16)
    dn_ref[...] = mm_nt(dgate_ref[...], wg_ref[...])


def conv_back(dpre, x, taps_ref, lanes, mask_ref, dtaps_ref, dp_ref, to):
    kernel = mask_ref.shape[0] + 1
    length = dpre.shape[0]

    def total(z):
        return jnp.sum(z, axis=0, keepdims=True)

    dtaps_ref[kernel : kernel + 1, to] = total(dpre)
    dtaps_ref[kernel - 1 : kernel, to] = total(dpre * x)
    dx = taps_ref[kernel - 1 : kernel, lanes] * dpre
    for j in range(1, kernel):
        masked = dpre * mask_ref[j - 1]
        tap = slice(kernel - 1 - j, kernel - j)
        dtaps_ref[tap, to] = total(masked * pltpu.roll(x, j, axis=0))
        dx = dx + taps_ref[tap, lanes] * pltpu.roll(masked, length - j, axis=0)
    dp_ref[:, to] = dx.astype(BF16)


def silu_and_slope(pre):
    sig = sigmoid(pre)
    return pre * sig, sig * (1.0 + pre * (1.0 - sig))


def scan_bwd_kernel(
    g_ref, yd_ref, v_ref, slope_ref, ci_ref, dt_ref, taps_ref, segr_ref, alog_ref, skip_ref, bias_ref,
    dp_ref, dtaps_ref, dskip_ref, dheads_ref,
    heads_ref, step_ref, cc_ref, wide_ref, cct_ref, segb_ref, mask_ref,
    sdt_ref, so_ref, sot_ref, dsdt_ref, dso_ref, acc_ref, dpre_ref,
):
    length = ci_ref.shape[0]
    segr = segr_ref[...].astype(F32)
    blocks = length // BLK
    channels = ci_ref.shape[1]
    states = BLK
    inner = channels - 2 * states
    nheads = inner // (BLK // 2)
    lanes_b = slice(inner, inner + states)
    lanes_c = slice(inner + states, channels)

    head_setup(
        dt_ref[...], (alog_ref, skip_ref, bias_ref), segr, heads_ref, step_ref, cc_ref, wide_ref, cct_ref, segb_ref
    )
    mask_setup(segb_ref, mask_ref)
    dheads_ref[...] = jnp.zeros_like(dheads_ref)
    dtaps_ref[...] = jnp.zeros_like(dtaps_ref)
    _, pre_b = conv_parts(ci_ref[:, lanes_b], taps_ref, lanes_b, mask_ref)
    _, pre_c = conv_parts(ci_ref[:, lanes_c], taps_ref, lanes_c, mask_ref)
    score_setup(
        pre_b * sigmoid(pre_b), pre_c * sigmoid(pre_c),
        segb_ref, segr, None, so_ref, sdt_ref, sot_ref,
    )
    dsdt_ref[...] = jnp.zeros_like(dsdt_ref)
    dso_ref[...] = jnp.zeros_like(dso_ref)
    acc_ref[...] = jnp.zeros_like(acc_ref)

    def body(t, carry):
        lanes = pl.ds(pl.multiple_of(t * BLK, BLK), BLK)
        x = ci_ref[:, lanes]
        v = v_ref[:, lanes]
        low = iota((1, BLK), 1) < BLK // 2
        st2, ew2, wq2, al2, c2, r2, skip = pair_setup(t, heads_ref, wide_ref, cc_ref, cct_ref)
        vtb = (v * st2).astype(BF16)
        vpb = (v * wq2).astype(BF16)
        g = g_ref[:, lanes]
        gb = g.astype(BF16)
        gpb = (al2 * g).astype(BF16)
        dskip_ref[:, lanes] = jnp.sum(g * v, axis=0, keepdims=True)
        k_row = iota((3 * BLK, BLK), 0)
        target = jnp.where(k_row >= 2 * BLK, BLK // 2, 0) + 2 * t
        target = target + jnp.where((k_row & (BLK - 1)) >= BLK // 2, 1, 0)
        collect = (iota((3 * BLK, BLK), 1) == target).astype(F32).astype(BF16)
        for i in range(blocks):
            rows = slice(i * BLK, (i + 1) * BLK)
            before = slice((i - 1) * BLK, i * BLK)
            after = slice((i + 1) * BLK, (i + 2) * BLK)
            gdiag = block_diag(gb[rows], low)
            both = mm_nt(vtb[rows], gdiag)
            ms = []
            part = jnp.zeros((BLK, BLK), F32)
            for k in range(2):
                row = r2[k : k + 1, rows]
                d = jnp.exp2(jnp.minimum(row - c2[rows, k : k + 1], 0.0))
                ms.append((sdt_ref[i] * d).astype(BF16))
                part = part + both[:, k * BLK : (k + 1) * BLK] * d
            dsdt_ref[i] += part
            dvt = mm(jnp.concatenate(ms, axis=1), gdiag)
            x1 = gb[rows].astype(F32) * yd_ref[rows, lanes] - dvt * vtb[rows].astype(F32)
            dv = st2[rows] * dvt + skip * g[rows]
            dstep = dvt
            if i > 0:
                z = mm(so_ref[i], vpb[before])
                x1 = x1 + gpb[rows].astype(F32) * z
                dso_ref[i] += mm_nt(gpb[rows], vpb[before])
            if i + 1 < blocks:
                dvp = mm(sot_ref[i + 1], gpb[after])
                x1 = x1 - dvp * vpb[rows].astype(F32)
                dv = dv + wq2[rows] * dvp
                dstep = dstep + ew2[rows] * dvp
            h1, l1 = split2(x1)
            h2 = (dstep * v[rows]).astype(BF16)
            acc_ref[rows, :] += mm(jnp.concatenate([h1, l1, h2], axis=1), collect)
            dpre_ref[rows, :] = dv * slope_ref[rows, lanes]
        conv_back(dpre_ref[...], x, taps_ref, lanes, mask_ref, dtaps_ref, dp_ref, lanes)
        return carry

    lax.fori_loop(0, inner // BLK, body, 0)
    xb, xc = ci_ref[:, lanes_b], ci_ref[:, lanes_c]
    _, pre_b = conv_parts(xb, taps_ref, lanes_b, mask_ref)
    _, pre_c = conv_parts(xc, taps_ref, lanes_c, mask_ref)
    bmat, slope_b = silu_and_slope(pre_b)
    cmat, slope_c = silu_and_slope(pre_c)
    bb, cb = bmat.astype(BF16), cmat.astype(BF16)
    causal_t = iota((BLK, BLK), 1) >= iota((BLK, BLK), 0)
    upper = causal_t.astype(F32)
    dst, dso = [], [None]
    for i in range(blocks):
        rows = slice(i * BLK, (i + 1) * BLK)
        before = slice((i - 1) * BLK, i * BLK)
        same = (segb_ref[rows, :] == segr[:, rows]) & causal_t
        dst.append(jnp.where(same, dsdt_ref[i], 0.0))
        if i > 0:
            linked = segb_ref[rows, :] == segr[:, before]
            dso.append(jnp.where(linked, dso_ref[i], 0.0))
    for i in range(blocks):
        rows = slice(i * BLK, (i + 1) * BLK)
        before = slice((i - 1) * BLK, i * BLK)
        after = slice((i + 1) * BLK, (i + 2) * BLK)
        dc = mm(dst[i].T.astype(BF16), bb[rows])
        if i > 0:
            dc = dc + mm(dso[i].astype(BF16), bb[before])
        dpre_ref[rows, :] = dc * slope_c[rows]
    conv_back(dpre_ref[...], xc, taps_ref, lanes_c, mask_ref, dtaps_ref, dp_ref, lanes_c)
    for i in range(blocks):
        rows = slice(i * BLK, (i + 1) * BLK)
        after = slice((i + 1) * BLK, (i + 2) * BLK)
        db = mm(dst[i].astype(BF16), cb[rows])
        if i + 1 < blocks:
            db = db + mm(dso[i + 1].T.astype(BF16), cb[after])
        dpre_ref[rows, :] = db * slope_b[rows]
    conv_back(dpre_ref[...], xb, taps_ref, lanes_b, mask_ref, dtaps_ref, dp_ref, lanes_b)

    decay = jnp.exp(heads_ref[0:1, :])
    later = jnp.zeros((1, BLK), F32)
    dalog = jnp.zeros((1, BLK), F32)
    dbias = jnp.zeros((1, BLK), F32)
    for i in reversed(range(blocks)):
        rows = slice(i * BLK, (i + 1) * BLK)
        dcum = acc_ref[rows, :]
        drate = later + jnp.dot(upper, dcum, precision=HIGH, preferred_element_type=F32)
        later = drate[0:1, :]
        step = step_ref[rows, :]
        dalog = dalog - jnp.sum(drate * step, axis=0, keepdims=True) * decay
        dstep = pltpu.roll(dcum, BLK // 2, axis=1) - drate * decay
        ddt = dstep * sigmoid(dt_ref[rows, :] + heads_ref[2:3, :])
        dbias = dbias + jnp.sum(ddt, axis=0, keepdims=True)
        dp_ref[rows, channels:] = jnp.where(iota((1, BLK), 1) < nheads, ddt, 0.0).astype(BF16)
    dheads_ref[0:1, :] = dalog
    dheads_ref[1:2, :] = dbias


def grad_in_kernel(xn_ref, dp_ref, lo_ref, hi_ref):
    grad = mm_tn(xn_ref[...], dp_ref[...]).astype(BF16)
    half = grad.shape[0] // 2
    lo_ref[...] = grad[:half]
    hi_ref[...] = grad[half:]


def input_kernel(
    wc_ref, dng_ref, dp_ref, me_ref, tab_ref, hid_ref, cot_ref, gains_ref,
    dtaps_ref, ginner_ref, dskip_ref, dheads_ref,
    ig_ref, sums_ref,
):
    dn = mm_nt(dp_ref[...], wc_ref[...]) + dng_ref[...]
    perm = perm_matrix(me_ref[0], tab_ref, dn.shape[1])
    hi, lo = split2(dn)
    dn = mm_nt(hi, perm) + mm_nt(lo, perm)
    tokens = hid_ref[...].astype(F32)
    scale = lax.rsqrt(jnp.mean(tokens * tokens, axis=-1, keepdims=True) + 1e-05)
    unit = tokens * scale
    width = tokens.shape[1]
    sums_ref[...] = jnp.zeros_like(sums_ref)
    sums_ref[0:5, : dtaps_ref.shape[1]] = dtaps_ref[0:5, :]
    sums_ref[5:6, :width] = jnp.sum(dn * unit, axis=0, keepdims=True)
    sums_ref[5:6, width:] = jnp.sum(ginner_ref[...], axis=0, keepdims=True)
    inner_n = dskip_ref.shape[1]
    lane = iota((inner_n, BLK), 1) * (BLK // 2)
    channel = iota((inner_n, BLK), 0)
    group = ((channel >= lane) & (channel < lane + BLK // 2)).astype(F32)
    sums_ref[6:7, :BLK] = jnp.dot(dskip_ref[...], group, precision=HIGH, preferred_element_type=F32)
    sums_ref[7:8, :BLK] = dheads_ref[0:1, :]
    sums_ref[7:8, BLK : 2 * BLK] = dheads_ref[1:2, :]
    dunit = dn * gains_ref[:, :width]
    inner = jnp.mean(unit * dunit, axis=-1, keepdims=True)
    ig_ref[...] = cot_ref[...].astype(F32) + scale * (dunit - unit * inner)


def stack_kernel(*refs):
    rows = jnp.concatenate([ref[...].astype(F32) for ref in refs[:-1]], axis=0)
    refs[-1][...] = rows.astype(BF16)


def fold_kernel(count, *refs):
    total = refs[0][...].astype(F32)
    for ref in refs[1:count]:
        total = total + ref[...].astype(F32)
    size = total.shape[0] // len(refs[count:])
    for k, ref in enumerate(refs[count:]):
        ref[...] = total[k * size : (k + 1) * size].astype(ref.dtype)


def last_out_kernel(a_ref, b_ref, c_ref, d_ref, gate_ref, out_ref):
    total = a_ref[...].astype(F32) + b_ref[...].astype(F32) + c_ref[...].astype(F32) + d_ref[...].astype(F32)
    inner = gate_ref.shape[1]
    rows, width = a_ref.shape[0], out_ref.shape[1]
    gate_ref[...] = total[:, :inner]
    out_ref[:rows, :] = total[:, inner : inner + width]
    out_ref[rows:, :] = total[:, inner + width :]


def last_in_kernel(a_ref, b_ref, c_ref, d_ref, gate_ref, in_ref):
    total = a_ref[...].astype(F32) + b_ref[...].astype(F32) + c_ref[...].astype(F32) + d_ref[...].astype(F32)
    inner = gate_ref.shape[1]
    in_ref[:, :inner] = gate_ref[...]
    in_ref[:, inner:] = total[:, : in_ref.shape[1] - inner]


def ends_kernel(me_ref, *refs):
    taps_ref, gains_ref, alog_ref, skip_ref, bias_ref = refs[-5:]
    parts = [ref[...] for ref in refs[:-5]]
    sums = parts[0] + parts[1]
    if len(parts) == 4:
        sums = sums + (parts[2] + parts[3])
    me, width = me_ref[0], sums.shape[1]
    taps_n, tap_share = taps_ref.shape
    gain_share, nheads = gains_ref.shape[1], alog_ref.shape[1]
    taps_ref[...] = pltpu.roll(sums, lax.rem(width - me * tap_share, width), axis=1)[:taps_n, :tap_share]
    gains_ref[...] = pltpu.roll(sums, lax.rem(width - me * gain_share, width), axis=1)[taps_n : taps_n + 1, :gain_share]
    skip_ref[...] = sums[6:7, :nheads]
    alog_ref[...] = sums[7:8, :nheads]
    bias_ref[...] = sums[7:8, BLK : BLK + nheads]


def sds(shape, dtype):
    return jax.ShapeDtypeStruct(shape, dtype)


def held(shape, dtype):
    return pltpu.VMEM(shape, dtype)


def scan_scratch(length, inner, taps):
    nheads = -(-2 * inner // (8 * BLK)) * 8
    return [
        pltpu.VMEM((8, BLK), F32), pltpu.VMEM((length, BLK), F32), pltpu.VMEM((length, BLK), F32),
        pltpu.VMEM((3, length, 2 * BLK), BF16), pltpu.VMEM((nheads, length), F32), pltpu.VMEM((length, BLK), F32),
        pltpu.VMEM((taps - 1, length, BLK), F32),
    ]


def scan_fwd(weights, packed, taps_n, widths, mine, tab, hidden, first, second, segr, *heads):
    length, width = hidden.shape
    channels, inner = widths
    blocks = length // BLK
    count = len(weights)
    rows = held((length, inner), F32)
    return call(
        lambda *refs: scan_fwd_kernel(count, packed, *refs),
        (
            held((length, width), BF16), held((8, channels), F32), held((1, width + inner), F32),
            held((width, channels + BLK), BF16),
            held((length, channels), F32), held((length, BLK), F32), rows, rows, rows, rows,
        ),
        *weights, mine, tab, hidden, first, second, segr, *heads, scalar=count,
        leave=(tab, first, second, segr) + heads,
        scratch=scan_scratch(length, inner, taps_n - 1) + [
            pltpu.VMEM((blocks, BLK, BLK), F32),
            pltpu.VMEM((blocks, BLK, BLK), BF16),
        ],
    )


def scan_bwd(taps_n, g, yd, v, slope, ci, dt, taps, segr, *heads):
    length, channels = ci.shape
    inner = g.shape[1]
    score = (length // BLK, BLK, BLK)
    return call(
        scan_bwd_kernel,
        (
            held((length, channels + BLK), BF16), held(taps.shape, F32), held((1, inner), F32),
            held((8, BLK), F32),
        ),
        g, yd, v, slope, ci, dt, taps, segr, *heads, leave=(segr,) + heads,
        scratch=scan_scratch(length, inner, taps_n - 1) + [
            pltpu.VMEM(score, F32),
            pltpu.VMEM(score, BF16),
            pltpu.VMEM(score, BF16),
            pltpu.VMEM(score, F32),
            pltpu.VMEM(score, F32),
            pltpu.VMEM((length, BLK), F32),
            pltpu.VMEM((length, BLK), F32),
        ],
    )


def call(kernel, outs, *ins, scratch=(), scalar=None, leave=()):
    specs = [
        pl.BlockSpec(memory_space=pltpu.SMEM if k == scalar else pltpu.VMEM) for k in range(len(ins))
    ]
    near = [
        a if k == scalar else pltpu.with_memory_space_constraint(a, pltpu.HBM if any(a is b for b in leave) else pltpu.VMEM)
        for k, a in enumerate(ins)
    ]
    many = isinstance(outs, (tuple, list))
    out_specs = [pl.BlockSpec(memory_space=pltpu.VMEM) for _ in outs] if many else pl.BlockSpec(memory_space=pltpu.VMEM)
    return pl.pallas_call(
        kernel, out_shape=outs, in_specs=specs, out_specs=out_specs, scratch_shapes=list(scratch),
        compiler_params=pltpu.CompilerParams(vmem_limit_bytes=(20 if scratch else 8) * 1024 * 1024),
    )(*near)


def stages(devices):
    masks = [1 << b for b in range(devices.bit_length() - 1)]
    groups = []
    for end in range(len(masks), 1, -2):
        part = masks[max(end - 2, 1) : end]
        groups.append(part if len(part) == 1 else [part[0], part[1], part[0] | part[1]])
    return groups + [masks[:1]]


def order_table(devices):
    table = np.zeros((1,), np.int32)
    for group in stages(devices):
        table = np.concatenate([table] + [table ^ m for m in group])
    return table


def send(x, devices, mask):
    return lax.ppermute(x, "fsdp", [(i, i ^ mask) for i in range(devices)])


def send_all(parts, devices, stage):
    return [send(part, devices, m) for part, m in zip(parts, stages(devices)[stage])]


def stack(pieces, leave):
    size, rest = pieces[0].shape[0], pieces[0].shape[1:]
    if size % 8 or len(rest) != 1:
        return jnp.concatenate(pieces, axis=0)
    return call(stack_kernel, held((len(pieces) * size,) + rest, BF16), *pieces, leave=leave)


def gather(x, devices, leave=()):
    groups = stages(devices)
    core = len(groups) - 1
    pieces = [x]
    for stage in range(core):
        x = pieces[0] if len(pieces) == 1 else stack(pieces, leave)
        pieces = [x] + send_all([x] * len(groups[stage]), devices, stage)
    return pieces + [send(a, devices, 1) for a in pieces]


def fold(parts, fan, dtype):
    rows, cols = parts[0].shape
    size = rows // fan
    if size % 8:
        total = sum(part.astype(F32) for part in parts).astype(dtype)
        return [total[k * size : (k + 1) * size] for k in range(fan)]
    count = len(parts)
    return call(lambda *refs: fold_kernel(count, *refs), tuple(held((size, cols), dtype) for _ in range(fan)), *parts)


def reduce_shares(lo, hi, devices):
    groups = stages(devices)
    parts = [lo, hi]
    for stage in reversed(range(len(groups))):
        parts = [parts[0]] + send_all(parts[1:], devices, stage)
        if stage:
            parts = fold(parts, len(groups[stage - 1]) + 1, BF16)
    return parts


def total_of(x, devices):
    for stage in reversed(range(len(stages(devices)))):
        group = stages(devices)[stage]
        got = send_all([x] * len(group), devices, stage)
        if stage == 0:
            return [x] + got
        x = x + got[0] if len(got) == 1 else (x + got[0]) + (got[1] + got[2])


def layer(
    hidden, segment_ids, cot, w_in, w_out, conv_taps, gains, a_log, d_skip, dt_bias
):
    length = segment_ids.shape[1]
    width = hidden.shape[1]
    devices = lax.axis_size("fsdp")
    me = lax.axis_index("fsdp")
    nheads = a_log.shape[0]
    taps_n, tap_share = conv_taps.shape
    channels = tap_share * devices
    gain_share = gains.shape[0]
    inner = w_out.shape[0] * devices
    proj = w_in.shape[1]
    rows_in, rows_out = w_in.shape[0], w_out.shape[0]
    pairs = inner // BLK
    first = pairs // 2

    table = order_table(devices)
    inverse = np.argsort(table).astype(np.int32)
    order = jnp.asarray(table) ^ me
    place = jnp.asarray(inverse)[me ^ jnp.arange(devices)]
    mine = me.reshape(1).astype(jnp.int32)
    tab = np.zeros((8, width), np.int32)
    tab[0], tab[1], tab[2] = np.repeat(table, rows_in), np.tile(np.arange(rows_in), devices), rows_in
    tab = jnp.asarray(tab)

    spare = BLK - (proj - inner - channels)
    packed = rows_in > taps_n and max(tap_share, gain_share) <= spare
    if packed:
        gain_row = gains.reshape(1, gain_share)
        w_conv, w_gate = call(
            lambda *refs: pack_kernel(inner, *refs),
            (held((rows_in, channels + BLK), BF16), held((rows_in, inner), BF16)),
            w_in, conv_taps, gain_row, leave=(w_in, conv_taps, gain_row),
        )
    else:
        w_conv = jnp.pad(w_in[:, inner:], ((0, 0), (0, spare)))
        w_gate = w_in[:, :inner]
    cw = gather(w_conv, devices)
    gw = gather(w_gate, devices)
    ow = gather(w_out, devices, (w_out,))
    count = len(cw)

    heads = [x.reshape(1, nheads) for x in (a_log, d_skip, dt_bias)]

    if packed:
        at = np.arange(width + inner)
        where = np.stack([at % tap_share, at // tap_share, at % gain_share, at // gain_share])
        second = jnp.asarray(np.pad(where, ((0, 4), (0, 0))).astype(np.int32))
        first = jnp.asarray(table.reshape(devices, 1))
    else:
        small = jnp.zeros((8, BLK), F32)
        small = small.at[:taps_n, :tap_share].set(conv_taps.astype(F32))
        small = small.at[taps_n, :gain_share].set(gains.astype(F32))
        rows = jnp.concatenate(gather(small[None], devices), axis=0)[place]
        first = jnp.moveaxis(rows[:, :, :tap_share], 0, 1).reshape(8, channels)
        second = rows[:, taps_n, :gain_share].reshape(1, width + inner)
    xn, taps, gains_all, wc, ci, dt, sc, yd, v, slope = scan_fwd(
        cw, (proj - inner - channels, taps_n) if packed else None, taps_n, (channels, inner),
        mine, tab, hidden, first, second, segment_ids, *heads,
    )
    if rows_out % 16:
        wo_all = jnp.concatenate(ow, axis=0).reshape(devices, rows_out, width)[place].reshape(inner, width)
        ow = [wo_all[k * (inner // count) : (k + 1) * (inner // count)] for k in range(count)]
    aligned = rows_in % 8 == 0
    if aligned:
        halves = (held((width // 2, inner + 2 * width), BF16), held((width // 2, inner + 2 * width), BF16))
    else:
        halves = (sds((width, inner), BF16), sds((inner, width), BF16))
    gate, wg = call(
        lambda *refs: gate_kernel(count, *refs),
        (held((length, inner), F32), held((width, inner), BF16)), *gw, xn,
    )
    lo, hi, g, dgate, mixed, ginner, wo = call(
        lambda *refs: mid_kernel(count, table, *refs),
        halves + (
            held((length, inner), F32), held((length, inner), BF16), held((length, inner), BF16),
            held((8, inner), F32), held((inner, width), BF16),
        ),
        *ow, mine, xn, gate, sc, gains_all, cot,
        scratch=(
            pltpu.VMEM((length, inner), F32), pltpu.VMEM((inner, width), F32),
        ),
        scalar=count,
    )
    if not aligned:
        gwo = hi.reshape(devices, 2, rows_in, width)[order]
        both = jnp.concatenate([lo, gwo[:, 0].reshape(width, width), gwo[:, 1].reshape(width, width)], axis=1)
        lo, hi = both[: width // 2], both[width // 2 :]
    mid_parts = reduce_shares(lo, hi, devices)
    output, dng = call(
        branch_kernel, (sds((length, width), BF16), held((length, width), F32)),
        mixed, wo, hidden, dgate, wg,
    )
    dp, dtaps, dskip, dheads = scan_bwd(taps_n, g, yd, v, slope, ci, dt, taps, segment_ids, *heads)
    half = held((width // 2, dp.shape[1]), BF16)
    clo, chi = call(grad_in_kernel, (half, half), xn, dp)
    conv_parts_in = reduce_shares(clo, chi, devices)
    input_grad, sums = call(
        input_kernel,
        (sds((length, width), F32), held((8, width + inner), F32)),
        wc, dng, dp, mine, tab, hidden, cot, gains_all, dtaps, ginner, dskip, dheads, scalar=3, leave=(tab,),
    )
    if aligned and len(mid_parts) == 4:
        gate_share, out_share = call(
            last_out_kernel,
            (sds((rows_in, inner), F32), sds((rows_out, width), F32)), *mid_parts,
        )
        in_share = call(last_in_kernel, sds((rows_in, proj), F32), *conv_parts_in, gate_share)
    else:
        total = sum(part.astype(F32) for part in mid_parts)
        out_share = jnp.concatenate([total[:, inner : inner + width], total[:, inner + width :]], axis=0)
        conv_total = sum(part.astype(F32) for part in conv_parts_in)
        in_share = jnp.concatenate([total[:, :inner], conv_total], axis=1)[:, :proj]

    sums = total_of(sums, devices)
    one = sds((1, nheads), F32)
    taps_share, gains_share, d_alog, d_dskip, d_bias = call(
        ends_kernel, (sds((taps_n, tap_share), F32), sds((1, gain_share), F32), one, one, one),
        mine, *sums, scalar=0,
    )
    return (
        output, input_grad, in_share, out_share, taps_share, gains_share.reshape(gain_share),
        d_alog.reshape(nheads), d_dskip.reshape(nheads), d_bias.reshape(nheads),
    )


def solution(mesh):
    axis = P("fsdp")
    rows = P("fsdp", None)
    cols = P(None, "fsdp")
    return jax.shard_map(
        layer,
        mesh=mesh,
        in_specs=(rows, rows, rows, rows, rows, cols, axis, P(), P(), P()),
        out_specs=(rows, rows, rows, rows, cols, axis, P(), P(), P()),
        check_vma=False,
    )
```
